128 devices in a mesh: face: 8 (over x_lo, z), tile: 16 (over y, x_hi, core).
Axes of the slice: x: 4 (x_hi: 2, x_lo: 2; x = x_hi * 2 + x_lo), y: 4, z: 4, core: 2. Of those that a mesh axis runs over, the one named last changes fastest.
Arguments:
- state: bfloat16 [8, 16, 2, 4, 512, 128], P('face', 'tile'), may hold values from -6 to 6
- obs_values: bfloat16 [131072, 256], P(('face', 'tile')), may hold values from -6 to 6
- obs_dest: int32 [131072, 1], P(('face', 'tile')), may hold values from 0 to 127; in each aligned block of 1024 rows (0 to 1023, 1024 to 2047, ...) at most 16 rows name the same one
- obs_pixel: int32 [131072], P(('face', 'tile')), may hold values from 0 to 4095
- matching: int32 [8, 2, 3], replicated, may hold values from 0 to 7, as said below
- kernel_one: bfloat16 [9, 128, 256], replicated, may hold values from -0.1875 to 0.1875
- bias_one: float32 [256], replicated, may hold values from -3 to 3
- kernel_two: bfloat16 [9, 256, 128], replicated, may hold values from -0.125 to 0.125
- bias_two: float32 [128], replicated, may hold values from -3 to 3
- cotangent: bfloat16 [8, 16, 2, 4, 512, 128], P('face', 'tile'), may hold values from -6 to 6
Outputs:
- analysis: bfloat16 [8, 16, 2, 4, 512, 128], P('face', 'tile')
- grad_state: float32 [8, 16, 2, 4, 512, 128], P('face', 'tile')
The draws below stay inside these ranges and needn't reach their ends.
Inputs may be any that keep to these rules, and one draw needn't show every extreme that they name: `obs_dest`: of the rows of one device, at most 16 name the same pixel tile, and in every draw some device names some tile exactly 16 times. The matching pairs sides: if side s of face block f is matched with side s2 of block g and flag r, then side s2 of g is matched with side s of f and the same flag. A block may be matched with itself on its other side.
All inputs are finite; a program needn't handle non-finite values.
Results may differ from the reference program's by a relative error of at most 0.0034.
Values may be sent and summed in bfloat16 or wider, within the bound.
A program may use at most 192 MiB of HBM per device.

```python
import math
import jax
import jax.numpy as jnp
import numpy as np
from jax import lax

CHANNELS = 128
LIFTED = 256
BAND = 4
COLUMNS = 512
OBS_DEV = 1024
FACES = 8
TILES = 16
ROWS = 128
PIX = 4096
CAP = 16
OBS_TOTAL = 131072
DEVICES = 128


def draw_matching(key, part):
    perm_key, flag_key = jax.random.split(key)
    side_count = 2 * FACES
    side_order = jax.random.permutation(perm_key, side_count).astype(jnp.int32)
    pair_flags = jax.random.randint(flag_key, (FACES,), 0, 2, dtype=jnp.int32)
    first_sides = side_order[0::2]
    second_sides = side_order[1::2]
    partner_side = jnp.zeros((side_count,), jnp.int32).at[first_sides].set(second_sides).at[second_sides].set(first_sides)
    side_flag = jnp.zeros((side_count,), jnp.int32).at[first_sides].set(pair_flags).at[second_sides].set(pair_flags)
    table = jnp.stack([partner_side // 2, partner_side % 2, side_flag], axis=1)
    return table.reshape(FACES, 2, 3)


def plant(result, rng, smallest, top_value):
    place = [jax.random.randint(jax.random.fold_in(rng, axis), (), 0, length) for axis, length in enumerate(result.shape)]
    longest = result.shape.index(max(result.shape))
    next_to = place[:longest] + [(place[longest] + 1) % result.shape[longest]] + place[longest + 1:]
    return result.at[tuple(place)].set(smallest).at[tuple(next_to)].set(top_value)


def shard_levels(own_key, shape, cuts, smallest, largest):
    def one(dim, shards_of):
        draws = jax.random.uniform(jax.random.fold_in(jax.random.fold_in(own_key, 6), dim), (shards_of,), jnp.float32, smallest / len(cuts), largest / len(cuts))
        return jnp.repeat(jnp.exp(draws), shape[dim] // shards_of).reshape((-1,) + (1,) * (len(shape) - dim - 1))

    factor_of = one(*cuts[0])
    for cut in cuts[1:]:
        factor_of = factor_of * one(*cut)
    return factor_of


def shared_out(stream_key, own, number, rows, amount, top, most, lean):
    sequence = jax.random.permutation(stream_key, amount)
    packed, ordinary = portions_of(amount, rows * top, most, lean, True), portions_of(amount, rows * top, most, lean, False)
    places = jnp.arange(amount)

    def named(tallies, turn):
        used = int((tallies > 0).sum())
        fixed = max(1, used // 4)
        shifted = fixed + (places - fixed + turn * (used - fixed)) % max(1, amount - fixed)
        return jnp.zeros((amount,), jnp.int32).at[sequence[jnp.where(places < fixed, places, shifted)]].set(jnp.asarray(tallies, jnp.int32))

    tallies = jnp.where(number % 4 == 0, named(packed, number // 4), named(ordinary, number - number // 4 - 1))
    mixed = jax.random.permutation(jax.random.fold_in(own, 3), amount)
    giver, taker = mixed[0:amount // 2 * 2:2], mixed[1:amount // 2 * 2:2]
    slack = jnp.minimum(tallies[giver] - 1, most - tallies[taker]) // 2
    slack = jnp.where((giver == sequence[0]) | (taker == sequence[0]) | (tallies[taker] == 0), 0, jnp.maximum(slack, 0))
    shifted = jax.random.randint(jax.random.fold_in(own, 4), (amount // 2,), 0, 1 << 20) % (slack + 1)
    tallies = tallies.at[giver].add(-shifted).at[taker].add(shifted)
    labels = jnp.searchsorted(jnp.cumsum(tallies), jnp.arange(rows * top), side="right").astype(jnp.int32)
    listing = labels.reshape(top, rows).T
    listing = listing[jax.random.permutation(jax.random.fold_in(own, 1), rows)]
    turn = jax.random.randint(jax.random.fold_in(own, 2), (rows, 1), 0, top)
    return jnp.take_along_axis(listing, (jnp.arange(top)[None, :] + turn) % top, axis=1)


def portions_of(amount, total, reach, skew, full):
    weights = [(1 << 20) // math.isqrt(standing ** skew) + 1 for standing in range(1, amount + 1)]
    largest = reach if full else min(reach, max(-(-total // amount), total * weights[0] // sum(weights)))
    least = 1 if total - largest >= amount - 1 else 0
    given, rest = [largest] + [least] * (amount - 1), total - largest - least * (amount - 1)
    while rest > 0:
        free = [i for i in range(1, amount) if given[i] < largest] or [i for i in range(1, amount) if given[i] < reach]
        mass, remaining = sum([weights[i] for i in free]), rest
        for i in free:
            more = min(reach - given[i], max(1, remaining * weights[i] // mass), rest)
            given[i] = given[i] + more
            rest = rest - more
    return np.array(given)


def noise(key, dims, deviation, most, shards=(), kind=jnp.bfloat16):
    array = deviation * jax.random.normal(key, dims, jnp.float32)
    if shards:
        array = array * shard_levels(key, dims, shards, -0.22, 0.18)
    return jnp.clip(array, -most, most).astype(kind)


def setup_inputs(seed: int = 0) -> dict:
    arg_keys = jax.random.split(jax.random.key(seed), 11)
    state = noise(arg_keys[0], (FACES, TILES, 2, BAND, COLUMNS, CHANNELS), 1.0, 6.0, ((0, 8), (1, 16)))
    obs_values = noise(arg_keys[1], (OBS_TOTAL, LIFTED), 1.0, 6.0, ((0, 128),))
    obs_dest_keys = jax.random.split(jax.random.fold_in(arg_keys[2], 1), OBS_TOTAL // OBS_DEV)
    obs_dest_turns = jax.random.permutation(jax.random.fold_in(arg_keys[2], 3), OBS_TOTAL // OBS_DEV)
    obs_dest = jax.vmap(lambda own, number: shared_out(jax.random.fold_in(arg_keys[2], 2), own, number, OBS_DEV, DEVICES, 1, CAP, 2))(obs_dest_keys, obs_dest_turns).reshape((OBS_TOTAL, 1))
    obs_pixel = plant(jax.random.randint(arg_keys[3], (OBS_TOTAL,), 0, PIX), jax.random.fold_in(arg_keys[3], 1), 0, PIX - 1).astype(jnp.int32)
    matching = draw_matching(jax.random.fold_in(arg_keys[10], 71), 0)
    kernel_one = noise(arg_keys[5], (9, CHANNELS, LIFTED), (9 * CHANNELS) ** -0.5, 0.1875)
    bias_one = noise(arg_keys[6], (LIFTED,), 0.5, 3.0, (), jnp.float32)
    kernel_two = noise(arg_keys[7], (9, LIFTED, CHANNELS), (9 * LIFTED) ** -0.5, 0.125)
    bias_two = noise(arg_keys[8], (CHANNELS,), 0.5, 3.0, (), jnp.float32)
    cotangent = noise(arg_keys[9], (FACES, TILES, 2, BAND, COLUMNS, CHANNELS), 1.0, 6.0, ((0, 8), (1, 16)))
    return dict(state=state, obs_values=obs_values, obs_dest=obs_dest, obs_pixel=obs_pixel, matching=matching, kernel_one=kernel_one, bias_one=bias_one, kernel_two=kernel_two, bias_two=bias_two, cotangent=cotangent)


def activation(values):
    return jax.nn.gelu(values, approximate=True)

def unfold(blocks):
    lower = blocks[:, :, 0].reshape(FACES, TILES * BAND, COLUMNS, blocks.shape[-1])
    upper = blocks[:, :, 1].reshape(FACES, TILES * BAND, COLUMNS, blocks.shape[-1])[:, ::-1]
    return jnp.concatenate([lower, upper], axis=1)

def fold(grid):
    half = TILES * BAND
    lower = grid[:, :half].reshape(FACES, TILES, BAND, COLUMNS, grid.shape[-1])
    upper = grid[:, half:][:, ::-1].reshape(FACES, TILES, BAND, COLUMNS, grid.shape[-1])
    return jnp.stack([lower, upper], axis=2)

def pad_sides(grid, matching):
    row_padded = jnp.pad(grid, ((0, 0), (1, 1), (0, 0), (0, 0)))
    edges = jnp.stack([row_padded[:, :, 0], row_padded[:, :, -1]], axis=1)
    partner = matching[:, :, 0]
    their_side = matching[:, :, 1]
    flipped = matching[:, :, 2]
    picked = edges[partner, their_side]
    picked = jnp.where(flipped[:, :, None, None] == 1, picked[:, :, ::-1], picked)
    return jnp.concatenate([picked[:, 0][:, :, None], row_padded, picked[:, 1][:, :, None]], axis=2)

def convolve(padded, kernel):
    total = None
    for row_tap in range(3):
        for col_tap in range(3):
            window = padded[:, row_tap:row_tap + ROWS, col_tap:col_tap + COLUMNS]
            term = jnp.einsum('frwc,co->frwo', window, kernel[3 * row_tap + col_tap], precision=lax.Precision.HIGHEST)
            total = term if total is None else total + term
    return total

def reference(state, obs_values, obs_dest, obs_pixel, matching, kernel_one, bias_one, kernel_two, bias_two, cotangent):
    base_field = unfold(state).astype(jnp.float32)
    target = obs_dest[:, 0].astype(jnp.int32) * PIX + obs_pixel.astype(jnp.int32)
    gridded = jax.ops.segment_sum(obs_values.astype(jnp.float32), target, num_segments=DEVICES * PIX)
    gridded = unfold(gridded.reshape(FACES, TILES, 2, BAND, COLUMNS, LIFTED))
    first_kernel = kernel_one.astype(jnp.float32)
    second_kernel = kernel_two.astype(jnp.float32)

    def layer_one(values):
        return convolve(pad_sides(values, matching), first_kernel)

    def layer_two(values):
        return convolve(pad_sides(values, matching), second_kernel)
    first_out, first_pull = jax.vjp(layer_one, base_field)
    pre_act = first_out + bias_one + gridded
    inner = activation(pre_act).astype(jnp.bfloat16)
    second_out, second_pull = jax.vjp(layer_two, inner.astype(jnp.float32))
    analysis = (base_field + second_out + bias_two).astype(jnp.bfloat16)
    cot_field = unfold(cotangent).astype(jnp.float32)
    grad_inner = second_pull(cot_field)[0]
    grad_pre = jax.vjp(activation, pre_act)[1](grad_inner)[0].astype(jnp.bfloat16)
    grad_state = cot_field + first_pull(grad_pre.astype(jnp.float32))[0]
    return (fold(analysis), fold(grad_state))
```

```python
import jax
import jax.numpy as jnp
from jax import lax
from jax.sharding import PartitionSpec as P


def activation(values):
    return jax.nn.gelu(values, approximate=True)


def conv_valid(cells, weights):
    return lax.conv_general_dilated(
        cells,
        weights,
        (1, 1),
        "VALID",
        dimension_numbers=("NHWC", "HWIO", "NHWC"),
        preferred_element_type=jnp.float32,
    )


def band_kernels(kernel):
    shaped = kernel.reshape(3, 3, kernel.shape[1], kernel.shape[2])
    return shaped, shaped[::-1]


def rotated(weights):
    return jnp.transpose(weights[::-1, ::-1], (0, 1, 3, 2))


def conv_bands(padded, kernel):
    upright, flipped = band_kernels(kernel)
    return jnp.concatenate(
        [conv_valid(padded[0:1], upright), conv_valid(padded[1:2], flipped)], axis=0
    )


def conv_back_bands(grad_ext, kernel):
    upright, flipped = band_kernels(kernel)
    widened = jnp.pad(grad_ext, ((0, 0), (0, 0), (2, 2), (0, 0)))
    return jnp.concatenate(
        [
            conv_valid(widened[0:1], rotated(upright)),
            conv_valid(widened[1:2], rotated(flipped)),
        ],
        axis=0,
    )


def extend_rows(source, last_tile):
    count = lax.axis_size("tile")
    band_rows = source.shape[1]
    head = source[:, 0:1]
    tail = source[:, band_rows - 1 : band_rows]
    before = lax.ppermute(tail, "tile", [(i, i + 1) for i in range(count - 1)])
    after = lax.ppermute(head, "tile", [(i + 1, i) for i in range(count - 1)])
    after = jnp.where(last_tile, tail[::-1], after)
    return jnp.concatenate([before, source, after], axis=1)


def pick_partner(gathered, matching_row):
    picked_sides = []
    for side_number in range(2):
        partner = matching_row[side_number, 0]
        their_side = matching_row[side_number, 1]
        flipped = matching_row[side_number, 2]
        chosen = lax.dynamic_index_in_dim(gathered, partner, 0, keepdims=False)
        column = jnp.where(their_side == 0, chosen[:, :, 0], chosen[:, :, 1])
        column = jnp.where(flipped == 1, column[::-1], column)
        picked_sides.append(column)
    return picked_sides


def gather_faces(parts):
    flat = jnp.concatenate([part.astype(jnp.float32).reshape(-1) for part in parts])
    gathered = lax.all_gather(flat, "face", axis=0, tiled=False)
    face_count = gathered.shape[0]
    pieces = []
    offset = 0
    for part in parts:
        size = part.size
        piece = gathered[:, offset : offset + size].reshape((face_count,) + part.shape)
        pieces.append(piece)
        offset += size
    return pieces


def add_sides(extended, gathered_edges, matching_row):
    left_side, right_side = pick_partner(gathered_edges, matching_row)
    left_side = left_side.astype(extended.dtype)
    right_side = right_side.astype(extended.dtype)
    return jnp.concatenate([left_side[:, :, None], extended, right_side[:, :, None]], axis=2)


def edge_cols(extended):
    return jnp.stack([extended[:, :, 0], extended[:, :, -1]], axis=2)


def add_ends(field, first_add, last_add, axis):
    length = field.shape[axis]
    head = lax.slice_in_dim(field, 0, 1, axis=axis) + jnp.expand_dims(first_add, axis)
    middle = lax.slice_in_dim(field, 1, length - 1, axis=axis)
    tail = lax.slice_in_dim(field, length - 1, length, axis=axis) + jnp.expand_dims(last_add, axis)
    return jnp.concatenate([head, middle, tail], axis=axis)


def return_sides(grad_padded, gathered_margins, matching_row):
    inside = grad_padded[:, :, 1:-1]
    left_back, right_back = pick_partner(gathered_margins, matching_row)
    return add_ends(inside, left_back, right_back, 2)


def route_observations(obs_values, obs_dest, obs_pixel, device_count):
    obs_rows = obs_values.shape[0]
    obs_width = obs_values.shape[1]
    capacity = 2 * obs_rows // device_count
    target = obs_dest[:, 0]
    positions = lax.iota(jnp.int32, obs_rows)
    same_target = (target[:, None] == target[None, :]) & (positions[None, :] < positions[:, None])
    rank_within = jnp.sum(same_target.astype(jnp.int32), axis=1)
    slot_index = target * capacity + rank_within
    slot_ids = lax.iota(jnp.int32, device_count * capacity)
    hits = slot_ids[:, None] == slot_index[None, :]
    value_slots = jnp.dot(
        hits.astype(jnp.bfloat16), obs_values, preferred_element_type=jnp.float32
    ).astype(jnp.bfloat16)
    pixel_slots = jnp.sum(jnp.where(hits, obs_pixel[None, :], 0), axis=1)
    high = (pixel_slots // 16).astype(jnp.bfloat16).reshape(device_count, capacity)
    low = (pixel_slots % 16).astype(jnp.bfloat16).reshape(device_count, capacity)
    pixel_row = jnp.concatenate(
        [high, low, jnp.zeros((device_count, obs_width - 2 * capacity), jnp.bfloat16)], axis=1
    )
    payload = jnp.concatenate(
        [value_slots.reshape(device_count, capacity, obs_width), pixel_row[:, None]], axis=1
    )
    arrived = lax.all_to_all(payload, ("face", "tile"), split_axis=0, concat_axis=0, tiled=True)
    got_values = arrived[:, :capacity].reshape(-1, obs_width)
    got_high = arrived[:, capacity, 0:capacity].astype(jnp.int32)
    got_low = arrived[:, capacity, capacity : 2 * capacity].astype(jnp.int32)
    got_pixels = (got_high * 16 + got_low).reshape(-1)
    return got_values, got_pixels


def per_device(
    state,
    obs_values,
    obs_dest,
    obs_pixel,
    matching,
    kernel_one,
    bias_one,
    kernel_two,
    bias_two,
    cotangent,
):
    base_field = state[0, 0]
    cot_field = cotangent[0, 0]
    band_rows = base_field.shape[1]
    column_count = base_field.shape[2]
    channels = base_field.shape[3]
    tile_count = lax.axis_size("tile")
    face_count = lax.axis_size("face")
    tile_at = lax.axis_index("tile")
    face_at = lax.axis_index("face")
    device_count = tile_count * face_count
    obs_width = obs_values.shape[1]

    got_values, got_pixels = route_observations(obs_values, obs_dest, obs_pixel, device_count)
    pixel_count = 2 * band_rows * column_count
    pixel_ids = lax.iota(jnp.int32, pixel_count)
    onehot = (pixel_ids[:, None] == got_pixels[None, :]).astype(jnp.bfloat16)
    gridded = jnp.dot(onehot, got_values, preferred_element_type=jnp.float32)
    gridded = gridded.reshape(2, band_rows, column_count, obs_width)

    last_tile = tile_at == tile_count - 1
    matching_row = lax.dynamic_index_in_dim(matching, face_at, 0, keepdims=False)

    both_ext = extend_rows(jnp.concatenate([base_field, cot_field], axis=3), last_tile)
    base_ext = both_ext[..., :channels]
    cot_ext = both_ext[..., channels:]
    cot_back = conv_back_bands(cot_ext, kernel_two)
    base_edges, cot_margins = gather_faces([edge_cols(base_ext), edge_cols(cot_back)])

    padded_base = add_sides(base_ext, base_edges, matching_row)
    pre_act = conv_bands(padded_base, kernel_one) + bias_one + gridded
    inner = activation(pre_act).astype(jnp.bfloat16)
    grad_inner = return_sides(cot_back, cot_margins, matching_row)
    grad_pre = jax.vjp(activation, pre_act)[1](grad_inner)[0].astype(jnp.bfloat16)

    lifted = inner.shape[3]
    pair_ext = extend_rows(jnp.concatenate([inner, grad_pre], axis=3), last_tile)
    inner_ext = pair_ext[..., :lifted]
    grad_pre_ext = pair_ext[..., lifted:]
    pre_back = conv_back_bands(grad_pre_ext, kernel_one)
    inner_edges, pre_margins = gather_faces([edge_cols(inner_ext), edge_cols(pre_back)])

    padded_inner = add_sides(inner_ext, inner_edges, matching_row)
    analysis = (
        base_field.astype(jnp.float32) + conv_bands(padded_inner, kernel_two) + bias_two
    ).astype(jnp.bfloat16)
    grad_base = cot_field.astype(jnp.float32) + return_sides(pre_back, pre_margins, matching_row)
    return (analysis[None, None], grad_base[None, None])


def solution(mesh):
    return jax.shard_map(
        per_device,
        mesh=mesh,
        in_specs=(
            P("face", "tile", None, None, None, None),
            P(("face", "tile"), None),
            P(("face", "tile"), None),
            P(("face", "tile")),
            P(),
            P(),
            P(),
            P(),
            P(),
            P("face", "tile", None, None, None, None),
        ),
        out_specs=(
            P("face", "tile", None, None, None, None),
            P("face", "tile", None, None, None, None),
        ),
        check_vma=False,
    )
```

```python
import functools

import jax
import jax.numpy as jnp
from jax import lax
from jax.experimental import pallas as pl
from jax.experimental.pallas import tpu as pltpu
from jax.sharding import PartitionSpec as P

MESH_IDS = pl.DeviceIdType.MESH


def activation(values):
    return jax.nn.gelu(values, approximate=True)


def conv_valid(cells, weights):
    return lax.conv_general_dilated(
        cells,
        weights,
        (1, 1),
        "VALID",
        dimension_numbers=("NHWC", "HWIO", "NHWC"),
        preferred_element_type=jnp.float32,
    )


def band_kernels(kernel):
    shaped = kernel.reshape(3, 3, kernel.shape[1], kernel.shape[2])
    return shaped, shaped[::-1]


def rotated(weights):
    return jnp.transpose(weights[::-1, ::-1], (0, 1, 3, 2))


def conv_bands(padded, kernel):
    upright, flipped = band_kernels(kernel)
    return jnp.concatenate(
        [conv_valid(padded[0:1], upright), conv_valid(padded[1:2], flipped)], axis=0
    )


def conv_back_bands(grad_ext, kernel):
    upright, flipped = band_kernels(kernel)
    widened = jnp.pad(grad_ext, ((0, 0), (0, 0), (2, 2), (0, 0)))
    return jnp.concatenate(
        [
            conv_valid(widened[0:1], rotated(upright)),
            conv_valid(widened[1:2], rotated(flipped)),
        ],
        axis=0,
    )


def extend_rows(source, last_tile):
    count = lax.axis_size("tile")
    band_rows = source.shape[1]
    head = source[:, 0:1]
    tail = source[:, band_rows - 1 : band_rows]
    before = lax.ppermute(tail, "tile", [(i, i + 1) for i in range(count - 1)])
    after = lax.ppermute(head, "tile", [(i + 1, i) for i in range(count - 1)])
    after = jnp.where(last_tile, tail[::-1], after)
    return jnp.concatenate([before, source, after], axis=1)


def pick_partner(gathered, matching_row):
    picked_sides = []
    for side_number in range(2):
        partner = matching_row[side_number, 0]
        their_side = matching_row[side_number, 1]
        flipped = matching_row[side_number, 2]
        chosen = lax.dynamic_index_in_dim(gathered, partner, 0, keepdims=False)
        column = jnp.where(their_side == 0, chosen[:, :, 0], chosen[:, :, 1])
        column = jnp.where(flipped == 1, column[::-1], column)
        picked_sides.append(column)
    return picked_sides


def face_gather_kernel(count, block_ref, out_ref, landed, send_sems, recv_sems):
    face = lax.axis_index("face")
    tile = lax.axis_index("tile")
    barrier = pltpu.get_barrier_semaphore()
    for step in range(1, count):
        peer = lax.rem(face + step, count)
        pl.semaphore_signal(barrier, inc=1, device_id=(peer, tile), device_id_type=MESH_IDS)
    pl.semaphore_wait(barrier, count - 1)
    copies = []
    for step in range(1, count):
        peer = lax.rem(face + step, count)
        copy = pltpu.make_async_remote_copy(
            src_ref=block_ref,
            dst_ref=landed.at[step],
            send_sem=send_sems.at[step],
            recv_sem=recv_sems.at[step],
            device_id=(peer, tile),
            device_id_type=MESH_IDS,
        )
        copy.start()
        copies.append(copy)
    out_ref[0] = block_ref[...]
    for copy in copies:
        copy.wait()
    for step in range(1, count):
        out_ref[step] = landed[step]


def face_gather(block, count, gather_id):
    rows, lanes = block.shape
    return pl.pallas_call(
        functools.partial(face_gather_kernel, count),
        out_shape=jax.ShapeDtypeStruct((count, rows, lanes), block.dtype),
        in_specs=[pl.BlockSpec(memory_space=pltpu.VMEM)],
        out_specs=pl.BlockSpec(memory_space=pltpu.VMEM),
        scratch_shapes=[
            pltpu.VMEM((count, rows, lanes), block.dtype),
            pltpu.SemaphoreType.DMA((count,)),
            pltpu.SemaphoreType.DMA((count,)),
        ],
        compiler_params=pltpu.CompilerParams(collective_id=gather_id, has_side_effects=True),
    )(block)


def gather_faces(parts, gather_id):
    flat = jnp.concatenate([part.astype(jnp.float32).reshape(-1) for part in parts])
    face_count = lax.axis_size("face")
    face_at = lax.axis_index("face")
    landed = face_gather(flat.reshape(-1, 128), face_count, gather_id).reshape(face_count, -1)
    slot_of_face = lax.rem(face_at - lax.iota(jnp.int32, face_count) + face_count, face_count)
    gathered = jnp.take(landed, slot_of_face, axis=0)
    pieces = []
    offset = 0
    for part in parts:
        size = part.size
        piece = gathered[:, offset : offset + size].reshape((face_count,) + part.shape)
        pieces.append(piece)
        offset += size
    return pieces


def add_sides(extended, gathered_edges, matching_row):
    left_side, right_side = pick_partner(gathered_edges, matching_row)
    left_side = left_side.astype(extended.dtype)
    right_side = right_side.astype(extended.dtype)
    return jnp.concatenate([left_side[:, :, None], extended, right_side[:, :, None]], axis=2)


def edge_cols(extended):
    return jnp.stack([extended[:, :, 0], extended[:, :, -1]], axis=2)


def add_ends(field, first_add, last_add, axis):
    length = field.shape[axis]
    head = lax.slice_in_dim(field, 0, 1, axis=axis) + jnp.expand_dims(first_add, axis)
    middle = lax.slice_in_dim(field, 1, length - 1, axis=axis)
    tail = lax.slice_in_dim(field, length - 1, length, axis=axis) + jnp.expand_dims(last_add, axis)
    return jnp.concatenate([head, middle, tail], axis=axis)


def return_sides(grad_padded, gathered_margins, matching_row):
    inside = grad_padded[:, :, 1:-1]
    left_back, right_back = pick_partner(gathered_margins, matching_row)
    return add_ends(inside, left_back, right_back, 2)


def route_observations(obs_values, obs_dest, obs_pixel, device_count):
    obs_rows = obs_values.shape[0]
    obs_width = obs_values.shape[1]
    capacity = 2 * obs_rows // device_count
    target = obs_dest[:, 0]
    positions = lax.iota(jnp.int32, obs_rows)
    same_target = (target[:, None] == target[None, :]) & (positions[None, :] < positions[:, None])
    rank_within = jnp.sum(same_target.astype(jnp.int32), axis=1)
    slot_index = target * capacity + rank_within
    slot_ids = lax.iota(jnp.int32, device_count * capacity)
    hits = slot_ids[:, None] == slot_index[None, :]
    value_slots = jnp.dot(
        hits.astype(jnp.bfloat16), obs_values, preferred_element_type=jnp.float32
    ).astype(jnp.bfloat16)
    pixel_slots = jnp.sum(jnp.where(hits, obs_pixel[None, :], 0), axis=1)
    high = (pixel_slots // 16).astype(jnp.bfloat16).reshape(device_count, capacity)
    low = (pixel_slots % 16).astype(jnp.bfloat16).reshape(device_count, capacity)
    pixel_row = jnp.concatenate(
        [high, low, jnp.zeros((device_count, obs_width - 2 * capacity), jnp.bfloat16)], axis=1
    )
    payload = jnp.concatenate(
        [value_slots.reshape(device_count, capacity, obs_width), pixel_row[:, None]], axis=1
    )
    arrived = lax.all_to_all(payload, ("face", "tile"), split_axis=0, concat_axis=0, tiled=True)
    got_values = arrived[:, :capacity].reshape(-1, obs_width)
    got_high = arrived[:, capacity, 0:capacity].astype(jnp.int32)
    got_low = arrived[:, capacity, capacity : 2 * capacity].astype(jnp.int32)
    got_pixels = (got_high * 16 + got_low).reshape(-1)
    return got_values, got_pixels


def per_device(
    state,
    obs_values,
    obs_dest,
    obs_pixel,
    matching,
    kernel_one,
    bias_one,
    kernel_two,
    bias_two,
    cotangent,
):
    base_field = state[0, 0]
    cot_field = cotangent[0, 0]
    band_rows = base_field.shape[1]
    column_count = base_field.shape[2]
    channels = base_field.shape[3]
    tile_count = lax.axis_size("tile")
    face_count = lax.axis_size("face")
    tile_at = lax.axis_index("tile")
    face_at = lax.axis_index("face")
    device_count = tile_count * face_count
    obs_width = obs_values.shape[1]

    got_values, got_pixels = route_observations(obs_values, obs_dest, obs_pixel, device_count)
    pixel_count = 2 * band_rows * column_count
    pixel_ids = lax.iota(jnp.int32, pixel_count)
    onehot = (pixel_ids[:, None] == got_pixels[None, :]).astype(jnp.bfloat16)
    gridded = jnp.dot(onehot, got_values, preferred_element_type=jnp.float32)
    gridded = gridded.reshape(2, band_rows, column_count, obs_width)

    last_tile = tile_at == tile_count - 1
    matching_row = lax.dynamic_index_in_dim(matching, face_at, 0, keepdims=False)

    both_ext = extend_rows(jnp.concatenate([base_field, cot_field], axis=3), last_tile)
    base_ext = both_ext[..., :channels]
    cot_ext = both_ext[..., channels:]
    cot_back = conv_back_bands(cot_ext, kernel_two)
    base_edges, cot_margins = gather_faces([edge_cols(base_ext), edge_cols(cot_back)], 0)

    padded_base = add_sides(base_ext, base_edges, matching_row)
    pre_act = conv_bands(padded_base, kernel_one) + bias_one + gridded
    inner = activation(pre_act).astype(jnp.bfloat16)
    grad_inner = return_sides(cot_back, cot_margins, matching_row)
    grad_pre = jax.vjp(activation, pre_act)[1](grad_inner)[0].astype(jnp.bfloat16)

    lifted = inner.shape[3]
    pair_ext = extend_rows(jnp.concatenate([inner, grad_pre], axis=3), last_tile)
    inner_ext = pair_ext[..., :lifted]
    grad_pre_ext = pair_ext[..., lifted:]
    pre_back = conv_back_bands(grad_pre_ext, kernel_one)
    inner_edges, pre_margins = gather_faces([edge_cols(inner_ext), edge_cols(pre_back)], 1)

    padded_inner = add_sides(inner_ext, inner_edges, matching_row)
    analysis = (
        base_field.astype(jnp.float32) + conv_bands(padded_inner, kernel_two) + bias_two
    ).astype(jnp.bfloat16)
    grad_base = cot_field.astype(jnp.float32) + return_sides(pre_back, pre_margins, matching_row)
    return (analysis[None, None], grad_base[None, None])


def solution(mesh):
    return jax.shard_map(
        per_device,
        mesh=mesh,
        in_specs=(
            P("face", "tile", None, None, None, None),
            P(("face", "tile"), None),
            P(("face", "tile"), None),
            P(("face", "tile")),
            P(),
            P(),
            P(),
            P(),
            P(),
            P("face", "tile", None, None, None, None),
        ),
        out_specs=(
            P("face", "tile", None, None, None, None),
            P("face", "tile", None, None, None, None),
        ),
        check_vma=False,
    )
```

```python
import functools

import jax
import jax.numpy as jnp
from jax import lax
from jax.experimental import pallas as pl
from jax.experimental.pallas import tpu as pltpu
from jax.sharding import PartitionSpec as P

MESH_IDS = pl.DeviceIdType.MESH


def activation(values):
    return jax.nn.gelu(values, approximate=True)


def conv_kernel(x_ref, side_ref, w_ref, out_ref, margin_ref):
    rows = out_ref.shape[1]
    cols = out_ref.shape[2]
    cout = out_ref.shape[3]
    cin = x_ref.shape[3]
    pixels = rows * cols
    lhs = jnp.concatenate(
        [x_ref[0, dy : dy + rows].reshape(pixels, cin) for dy in range(3)], axis=1
    )
    sides = side_ref[0]
    left = jnp.concatenate([sides[0, dy : dy + rows] for dy in range(3)], axis=1)
    right = jnp.concatenate([sides[1, dy : dy + rows] for dy in range(3)], axis=1)
    left_term = jnp.dot(left, w_ref[0, 0], preferred_element_type=jnp.float32)
    right_term = jnp.dot(right, w_ref[0, 2], preferred_element_type=jnp.float32)
    z_left = jnp.dot(lhs, w_ref[0, 0], preferred_element_type=jnp.float32)
    z_mid = jnp.dot(lhs, w_ref[0, 1], preferred_element_type=jnp.float32)
    z_right = jnp.dot(lhs, w_ref[0, 2], preferred_element_type=jnp.float32)
    col = lax.broadcasted_iota(jnp.int32, (rows, cols, cout), 1).reshape(pixels, cout)
    left_full = jnp.broadcast_to(left_term[:, None, :], (rows, cols, cout)).reshape(pixels, cout)
    right_full = jnp.broadcast_to(right_term[:, None, :], (rows, cols, cout)).reshape(pixels, cout)
    from_left = jnp.where(col == 0, left_full, pltpu.roll(z_left, 1, 0))
    from_right = jnp.where(col == cols - 1, right_full, pltpu.roll(z_right, pixels - 1, 0))
    out_ref[0] = (z_mid + from_left + from_right).reshape(rows, cols, cout)
    z_left3 = z_left.reshape(rows, cols, cout)
    z_right3 = z_right.reshape(rows, cols, cout)
    margin_ref[0, 0] = z_right3[:, 0, :]
    margin_ref[0, 1] = z_left3[:, cols - 1, :]


def conv_pallas(x_ext, sides, weights):
    bands, ext_rows, cols, cin = x_ext.shape
    rows = ext_rows - 2
    cout = weights.shape[-1]
    return pl.pallas_call(
        conv_kernel,
        grid=(bands,),
        in_specs=[
            pl.BlockSpec((1, ext_rows, cols, cin), lambda b: (b, 0, 0, 0)),
            pl.BlockSpec((1, 2, ext_rows, cin), lambda b: (b, 0, 0, 0)),
            pl.BlockSpec((1, 3, 3 * cin, cout), lambda b: (b, 0, 0, 0)),
        ],
        out_specs=[
            pl.BlockSpec((1, rows, cols, cout), lambda b: (b, 0, 0, 0)),
            pl.BlockSpec((1, 2, rows, cout), lambda b: (b, 0, 0, 0)),
        ],
        out_shape=[
            jax.ShapeDtypeStruct((bands, rows, cols, cout), jnp.float32),
            jax.ShapeDtypeStruct((bands, 2, rows, cout), jnp.float32),
        ],
        compiler_params=pltpu.CompilerParams(vmem_limit_bytes=60 * 1024 * 1024),
    )(x_ext, sides, weights)


def forward_weights(kernel):
    shaped = kernel.reshape(3, 3, kernel.shape[1], kernel.shape[2])
    per_band = []
    for oriented in (shaped, shaped[::-1]):
        per_band.append(jnp.stack([oriented[:, dx].reshape(-1, kernel.shape[2]) for dx in range(3)]))
    return jnp.stack(per_band)


def backward_weights(kernel):
    shaped = kernel.reshape(3, 3, kernel.shape[1], kernel.shape[2])
    per_band = []
    for oriented in (shaped, shaped[::-1]):
        turned = jnp.transpose(oriented[::-1, ::-1], (0, 1, 3, 2))
        per_band.append(jnp.stack([turned[:, dx].reshape(-1, kernel.shape[1]) for dx in range(3)]))
    return jnp.stack(per_band)


def extend_rows(source, last_tile):
    count = lax.axis_size("tile")
    band_rows = source.shape[1]
    head = source[:, 0:1]
    tail = source[:, band_rows - 1 : band_rows]
    before = lax.ppermute(tail, "tile", [(i, i + 1) for i in range(count - 1)])
    after = lax.ppermute(head, "tile", [(i + 1, i) for i in range(count - 1)])
    after = jnp.where(last_tile, tail[::-1], after)
    return jnp.concatenate([before, source, after], axis=1)


def pick_partner(gathered, matching_row):
    picked_sides = []
    for side_number in range(2):
        partner = matching_row[side_number, 0]
        their_side = matching_row[side_number, 1]
        flipped = matching_row[side_number, 2]
        chosen = lax.dynamic_index_in_dim(gathered, partner, 0, keepdims=False)
        column = jnp.where(their_side == 0, chosen[:, :, 0], chosen[:, :, 1])
        column = jnp.where(flipped == 1, column[::-1], column)
        picked_sides.append(column)
    return picked_sides


def face_gather_kernel(count, block_ref, out_ref, landed, send_sems, recv_sems):
    face = lax.axis_index("face")
    tile = lax.axis_index("tile")
    barrier = pltpu.get_barrier_semaphore()
    for step in range(1, count):
        peer = lax.rem(face + step, count)
        pl.semaphore_signal(barrier, inc=1, device_id=(peer, tile), device_id_type=MESH_IDS)
    pl.semaphore_wait(barrier, count - 1)
    copies = []
    for step in range(1, count):
        peer = lax.rem(face + step, count)
        copy = pltpu.make_async_remote_copy(
            src_ref=block_ref,
            dst_ref=landed.at[step],
            send_sem=send_sems.at[step],
            recv_sem=recv_sems.at[step],
            device_id=(peer, tile),
            device_id_type=MESH_IDS,
        )
        copy.start()
        copies.append(copy)
    out_ref[0] = block_ref[...]
    for copy in copies:
        copy.wait()
    for step in range(1, count):
        out_ref[step] = landed[step]


def face_gather(block, count, gather_id):
    rows, lanes = block.shape
    return pl.pallas_call(
        functools.partial(face_gather_kernel, count),
        out_shape=jax.ShapeDtypeStruct((count, rows, lanes), block.dtype),
        in_specs=[pl.BlockSpec(memory_space=pltpu.VMEM)],
        out_specs=pl.BlockSpec(memory_space=pltpu.VMEM),
        scratch_shapes=[
            pltpu.VMEM((count, rows, lanes), block.dtype),
            pltpu.SemaphoreType.DMA((count,)),
            pltpu.SemaphoreType.DMA((count,)),
        ],
        compiler_params=pltpu.CompilerParams(collective_id=gather_id, has_side_effects=True),
    )(block)


def gather_faces(parts, gather_id):
    flat = jnp.concatenate([part.astype(jnp.float32).reshape(-1) for part in parts])
    face_count = lax.axis_size("face")
    face_at = lax.axis_index("face")
    landed = face_gather(flat.reshape(-1, 128), face_count, gather_id).reshape(face_count, -1)
    slot_of_face = lax.rem(face_at - lax.iota(jnp.int32, face_count) + face_count, face_count)
    gathered = jnp.take(landed, slot_of_face, axis=0)
    pieces = []
    offset = 0
    for part in parts:
        size = part.size
        piece = gathered[:, offset : offset + size].reshape((face_count,) + part.shape)
        pieces.append(piece)
        offset += size
    return pieces


def side_columns(gathered_edges, matching_row):
    left_side, right_side = pick_partner(gathered_edges, matching_row)
    return jnp.stack([left_side, right_side], axis=1).astype(jnp.bfloat16)


def edge_cols(extended):
    return jnp.stack([extended[:, :, 0], extended[:, :, -1]], axis=2)


def add_ends(field, first_add, last_add, axis):
    length = field.shape[axis]
    head = lax.slice_in_dim(field, 0, 1, axis=axis) + jnp.expand_dims(first_add, axis)
    middle = lax.slice_in_dim(field, 1, length - 1, axis=axis)
    tail = lax.slice_in_dim(field, length - 1, length, axis=axis) + jnp.expand_dims(last_add, axis)
    return jnp.concatenate([head, middle, tail], axis=axis)


def return_sides(inside, margins, gathered_margins, matching_row):
    left_back, right_back = pick_partner(gathered_margins, matching_row)
    return add_ends(inside, left_back, right_back, 2)


def route_observations(obs_values, obs_dest, obs_pixel, device_count):
    obs_rows = obs_values.shape[0]
    obs_width = obs_values.shape[1]
    capacity = 2 * obs_rows // device_count
    target = obs_dest[:, 0]
    positions = lax.iota(jnp.int32, obs_rows)
    same_target = (target[:, None] == target[None, :]) & (positions[None, :] < positions[:, None])
    rank_within = jnp.sum(same_target.astype(jnp.int32), axis=1)
    slot_index = target * capacity + rank_within
    slot_ids = lax.iota(jnp.int32, device_count * capacity)
    hits = slot_ids[:, None] == slot_index[None, :]
    value_slots = jnp.dot(
        hits.astype(jnp.bfloat16), obs_values, preferred_element_type=jnp.float32
    ).astype(jnp.bfloat16)
    pixel_slots = jnp.sum(jnp.where(hits, obs_pixel[None, :], 0), axis=1)
    high = (pixel_slots // 16).astype(jnp.bfloat16).reshape(device_count, capacity)
    low = (pixel_slots % 16).astype(jnp.bfloat16).reshape(device_count, capacity)
    pixel_row = jnp.concatenate(
        [high, low, jnp.zeros((device_count, obs_width - 2 * capacity), jnp.bfloat16)], axis=1
    )
    payload = jnp.concatenate(
        [value_slots.reshape(device_count, capacity, obs_width), pixel_row[:, None]], axis=1
    )
    arrived = lax.all_to_all(payload, ("face", "tile"), split_axis=0, concat_axis=0, tiled=True)
    got_values = arrived[:, :capacity].reshape(-1, obs_width)
    got_high = arrived[:, capacity, 0:capacity].astype(jnp.int32)
    got_low = arrived[:, capacity, capacity : 2 * capacity].astype(jnp.int32)
    got_pixels = (got_high * 16 + got_low).reshape(-1)
    return got_values, got_pixels


def per_device(
    state,
    obs_values,
    obs_dest,
    obs_pixel,
    matching,
    kernel_one,
    bias_one,
    kernel_two,
    bias_two,
    cotangent,
):
    base_field = state[0, 0]
    cot_field = cotangent[0, 0]
    band_rows = base_field.shape[1]
    column_count = base_field.shape[2]
    channels = base_field.shape[3]
    tile_count = lax.axis_size("tile")
    face_count = lax.axis_size("face")
    tile_at = lax.axis_index("tile")
    face_at = lax.axis_index("face")
    device_count = tile_count * face_count
    obs_width = obs_values.shape[1]

    got_values, got_pixels = route_observations(obs_values, obs_dest, obs_pixel, device_count)
    pixel_count = 2 * band_rows * column_count
    pixel_ids = lax.iota(jnp.int32, pixel_count)
    onehot = (pixel_ids[:, None] == got_pixels[None, :]).astype(jnp.bfloat16)
    gridded = jnp.dot(onehot, got_values, preferred_element_type=jnp.float32)
    gridded = gridded.reshape(2, band_rows, column_count, obs_width)

    last_tile = tile_at == tile_count - 1
    matching_row = lax.dynamic_index_in_dim(matching, face_at, 0, keepdims=False)

    both_ext = extend_rows(jnp.concatenate([base_field, cot_field], axis=3), last_tile)
    base_ext = both_ext[..., :channels]
    cot_ext = both_ext[..., channels:]
    lifted = kernel_one.shape[2]
    no_sides = jnp.zeros((2, 2, band_rows + 2, channels), jnp.bfloat16)
    cot_back, cot_margins = conv_pallas(cot_ext, no_sides, backward_weights(kernel_two))
    base_edges, cot_gathered = gather_faces(
        [edge_cols(base_ext), jnp.swapaxes(cot_margins, 1, 2)], 0
    )

    pre_act = conv_pallas(base_ext, side_columns(base_edges, matching_row), forward_weights(kernel_one))[0]
    pre_act = pre_act + bias_one + gridded
    inner = activation(pre_act).astype(jnp.bfloat16)
    grad_inner = return_sides(cot_back, cot_margins, cot_gathered, matching_row)
    grad_pre = jax.vjp(activation, pre_act)[1](grad_inner)[0].astype(jnp.bfloat16)

    pair_ext = extend_rows(jnp.concatenate([inner, grad_pre], axis=3), last_tile)
    inner_ext = pair_ext[..., :lifted]
    grad_pre_ext = pair_ext[..., lifted:]
    no_lifted_sides = jnp.zeros((2, 2, band_rows + 2, lifted), jnp.bfloat16)
    pre_back, pre_margins = conv_pallas(grad_pre_ext, no_lifted_sides, backward_weights(kernel_one))
    inner_edges, pre_gathered = gather_faces(
        [edge_cols(inner_ext), jnp.swapaxes(pre_margins, 1, 2)], 1
    )

    second_out = conv_pallas(inner_ext, side_columns(inner_edges, matching_row), forward_weights(kernel_two))[0]
    analysis = (base_field.astype(jnp.float32) + second_out + bias_two).astype(jnp.bfloat16)
    grad_base = cot_field.astype(jnp.float32) + return_sides(pre_back, pre_margins, pre_gathered, matching_row)
    return (analysis[None, None], grad_base[None, None])


def solution(mesh):
    return jax.shard_map(
        per_device,
        mesh=mesh,
        in_specs=(
            P("face", "tile", None, None, None, None),
            P(("face", "tile"), None),
            P(("face", "tile"), None),
            P(("face", "tile")),
            P(),
            P(),
            P(),
            P(),
            P(),
            P("face", "tile", None, None, None, None),
        ),
        out_specs=(
            P("face", "tile", None, None, None, None),
            P("face", "tile", None, None, None, None),
        ),
        check_vma=False,
    )
```

```python
import functools

import jax
import jax.numpy as jnp
from jax import lax
from jax.experimental import pallas as pl
from jax.experimental.pallas import tpu as pltpu
from jax.sharding import PartitionSpec as P

MESH_IDS = pl.DeviceIdType.MESH


def activation(values):
    return jax.nn.gelu(values, approximate=True)


def tap_index(band, row_tap, col_tap, backward):
    if backward:
        row = 2 - row_tap if band == 0 else row_tap
        return 3 * row + 2 - col_tap
    row = row_tap if band == 0 else 2 - row_tap
    return 3 * row + col_tap


def conv_kernel(backward, first, width, src_ref, before_ref, after_ref, side_ref, k_ref, out_ref, margin_ref):
    bands, rows, cols, cout = out_ref.shape
    pixels = rows * cols
    lanes = slice(first, first + width)
    col = lax.broadcasted_iota(jnp.int32, (rows, cols, cout), 1).reshape(pixels, cout)
    for band in range(bands):
        ext = jnp.concatenate(
            [before_ref[band, :, :, lanes], src_ref[band, :, :, lanes], after_ref[band, :, :, lanes]],
            axis=0,
        )
        lhs = jnp.concatenate(
            [ext[dy : dy + rows].reshape(pixels, width) for dy in range(3)], axis=1
        )
        stacks = []
        for col_tap in range(3):
            taps = [k_ref[tap_index(band, dy, col_tap, backward)] for dy in range(3)]
            if backward:
                stacks.append(jnp.concatenate(taps, axis=1))
            else:
                stacks.append(jnp.concatenate(taps, axis=0))

        def product(values, stack):
            if backward:
                return lax.dot_general(
                    values, stack, (((1,), (1,)), ((), ())), preferred_element_type=jnp.float32
                )
            return jnp.dot(values, stack, preferred_element_type=jnp.float32)

        z_left = product(lhs, stacks[0])
        z_mid = product(lhs, stacks[1])
        z_right = product(lhs, stacks[2])
        if backward:
            left_full = jnp.zeros((pixels, cout), jnp.float32)
            right_full = left_full
        else:
            sides = side_ref[band]
            left = jnp.concatenate([sides[0, dy : dy + rows] for dy in range(3)], axis=1)
            right = jnp.concatenate([sides[1, dy : dy + rows] for dy in range(3)], axis=1)
            left_term = product(left, stacks[0])
            right_term = product(right, stacks[2])
            left_full = jnp.broadcast_to(left_term[:, None, :], (rows, cols, cout)).reshape(pixels, cout)
            right_full = jnp.broadcast_to(right_term[:, None, :], (rows, cols, cout)).reshape(pixels, cout)
        from_left = jnp.where(col == 0, left_full, pltpu.roll(z_left, 1, 0))
        from_right = jnp.where(col == cols - 1, right_full, pltpu.roll(z_right, pixels - 1, 0))
        out_ref[band] = (z_mid + from_left + from_right).reshape(rows, cols, cout)
        if backward:
            margin_ref[band, 0] = z_right.reshape(rows, cols, cout)[:, 0, :]
            margin_ref[band, 1] = z_left.reshape(rows, cols, cout)[:, cols - 1, :]


def conv_pallas(pieces, first, width, sides, kernel, backward):
    source, before, after = pieces
    bands, rows, cols, _ = source.shape
    cout = kernel.shape[1] if backward else kernel.shape[2]
    if sides is None:
        sides = jnp.zeros((bands, 2, rows + 2, width), jnp.bfloat16)
    vmem = pl.BlockSpec(memory_space=pltpu.VMEM)
    out, margins = pl.pallas_call(
        functools.partial(conv_kernel, backward, first, width),
        in_specs=[vmem] * 5,
        out_specs=[vmem, vmem],
        out_shape=[
            jax.ShapeDtypeStruct((bands, rows, cols, cout), jnp.float32),
            jax.ShapeDtypeStruct((bands, 2, rows, cout), jnp.float32),
        ],
        compiler_params=pltpu.CompilerParams(vmem_limit_bytes=60 * 1024 * 1024),
    )(source, before, after, sides, kernel)
    return out, margins


def extend_rows(source, last_tile):
    count = lax.axis_size("tile")
    band_rows = source.shape[1]
    head = source[:, 0:1]
    tail = source[:, band_rows - 1 : band_rows]
    before = lax.ppermute(tail, "tile", [(i, i + 1) for i in range(count - 1)])
    after = lax.ppermute(head, "tile", [(i + 1, i) for i in range(count - 1)])
    after = jnp.where(last_tile, tail[::-1], after)
    return source, before, after


def edge_cols(pieces, first, width):
    extended = jnp.concatenate([piece[..., first : first + width] for piece in (pieces[1], pieces[0], pieces[2])], axis=1)
    return jnp.stack([extended[:, :, 0], extended[:, :, -1]], axis=2)


def pick_partner(gathered, matching_row):
    picked_sides = []
    for side_number in range(2):
        partner = matching_row[side_number, 0]
        their_side = matching_row[side_number, 1]
        flipped = matching_row[side_number, 2]
        chosen = lax.dynamic_index_in_dim(gathered, partner, 0, keepdims=False)
        column = jnp.where(their_side == 0, chosen[:, :, 0], chosen[:, :, 1])
        column = jnp.where(flipped == 1, column[::-1], column)
        picked_sides.append(column)
    return picked_sides


def face_gather_kernel(count, block_ref, out_ref, landed, send_sems, recv_sems):
    face = lax.axis_index("face")
    tile = lax.axis_index("tile")
    barrier = pltpu.get_barrier_semaphore()
    for step in range(1, count):
        peer = lax.rem(face + step, count)
        pl.semaphore_signal(barrier, inc=1, device_id=(peer, tile), device_id_type=MESH_IDS)
    pl.semaphore_wait(barrier, count - 1)
    copies = []
    for step in range(1, count):
        peer = lax.rem(face + step, count)
        copy = pltpu.make_async_remote_copy(
            src_ref=block_ref,
            dst_ref=landed.at[step],
            send_sem=send_sems.at[step],
            recv_sem=recv_sems.at[step],
            device_id=(peer, tile),
            device_id_type=MESH_IDS,
        )
        copy.start()
        copies.append(copy)
    out_ref[0] = block_ref[...]
    for copy in copies:
        copy.wait()
    for step in range(1, count):
        out_ref[step] = landed[step]


def face_gather(block, count, gather_id):
    rows, lanes = block.shape
    return pl.pallas_call(
        functools.partial(face_gather_kernel, count),
        out_shape=jax.ShapeDtypeStruct((count, rows, lanes), block.dtype),
        in_specs=[pl.BlockSpec(memory_space=pltpu.VMEM)],
        out_specs=pl.BlockSpec(memory_space=pltpu.VMEM),
        scratch_shapes=[
            pltpu.VMEM((count, rows, lanes), block.dtype),
            pltpu.SemaphoreType.DMA((count,)),
            pltpu.SemaphoreType.DMA((count,)),
        ],
        compiler_params=pltpu.CompilerParams(collective_id=gather_id, has_side_effects=True),
    )(block)


def gather_faces(parts, gather_id):
    flat = jnp.concatenate([part.astype(jnp.float32).reshape(-1) for part in parts])
    face_count = lax.axis_size("face")
    face_at = lax.axis_index("face")
    landed = face_gather(flat.reshape(-1, 128), face_count, gather_id).reshape(face_count, -1)
    slot_of_face = lax.rem(face_at - lax.iota(jnp.int32, face_count) + face_count, face_count)
    gathered = jnp.take(landed, slot_of_face, axis=0)
    pieces = []
    offset = 0
    for part in parts:
        size = part.size
        piece = gathered[:, offset : offset + size].reshape((face_count,) + part.shape)
        pieces.append(piece)
        offset += size
    return pieces


def side_columns(gathered_edges, matching_row):
    left_side, right_side = pick_partner(gathered_edges, matching_row)
    return jnp.stack([left_side, right_side], axis=1).astype(jnp.bfloat16)


def add_ends(field, first_add, last_add, axis):
    length = field.shape[axis]
    head = lax.slice_in_dim(field, 0, 1, axis=axis) + jnp.expand_dims(first_add, axis)
    middle = lax.slice_in_dim(field, 1, length - 1, axis=axis)
    tail = lax.slice_in_dim(field, length - 1, length, axis=axis) + jnp.expand_dims(last_add, axis)
    return jnp.concatenate([head, middle, tail], axis=axis)


def return_sides(inside, gathered_margins, matching_row):
    left_back, right_back = pick_partner(gathered_margins, matching_row)
    inside = inside.at[:, :, 0].add(left_back)
    return inside.at[:, :, inside.shape[2] - 1].add(right_back)


def route_observations(obs_values, obs_dest, obs_pixel, device_count):
    obs_rows = obs_values.shape[0]
    obs_width = obs_values.shape[1]
    capacity = 2 * obs_rows // device_count
    target = obs_dest[:, 0]
    positions = lax.iota(jnp.int32, obs_rows)
    same_target = (target[:, None] == target[None, :]) & (positions[None, :] < positions[:, None])
    rank_within = jnp.sum(same_target.astype(jnp.int32), axis=1)
    slot_index = target * capacity + rank_within
    slot_ids = lax.iota(jnp.int32, device_count * capacity)
    hits = slot_ids[:, None] == slot_index[None, :]
    value_slots = jnp.dot(
        hits.astype(jnp.bfloat16), obs_values, preferred_element_type=jnp.float32
    ).astype(jnp.bfloat16)
    pixel_slots = jnp.sum(jnp.where(hits, obs_pixel[None, :], 0), axis=1)
    high = (pixel_slots // 16).astype(jnp.bfloat16).reshape(device_count, capacity)
    low = (pixel_slots % 16).astype(jnp.bfloat16).reshape(device_count, capacity)
    pixel_row = jnp.concatenate(
        [high, low, jnp.zeros((device_count, obs_width - 2 * capacity), jnp.bfloat16)], axis=1
    )
    payload = jnp.concatenate(
        [value_slots.reshape(device_count, capacity, obs_width), pixel_row[:, None]], axis=1
    )
    arrived = lax.all_to_all(payload, ("face", "tile"), split_axis=0, concat_axis=0, tiled=True)
    got_values = arrived[:, :capacity].reshape(-1, obs_width)
    got_high = arrived[:, capacity, 0:capacity].astype(jnp.int32)
    got_low = arrived[:, capacity, capacity : 2 * capacity].astype(jnp.int32)
    got_pixels = (got_high * 16 + got_low).reshape(-1)
    return got_values, got_pixels


def per_device(
    state,
    obs_values,
    obs_dest,
    obs_pixel,
    matching,
    kernel_one,
    bias_one,
    kernel_two,
    bias_two,
    cotangent,
):
    base_field = state[0, 0]
    cot_field = cotangent[0, 0]
    band_rows = base_field.shape[1]
    column_count = base_field.shape[2]
    channels = base_field.shape[3]
    tile_count = lax.axis_size("tile")
    face_count = lax.axis_size("face")
    tile_at = lax.axis_index("tile")
    face_at = lax.axis_index("face")
    device_count = tile_count * face_count
    obs_width = obs_values.shape[1]

    got_values, got_pixels = route_observations(obs_values, obs_dest, obs_pixel, device_count)
    pixel_count = 2 * band_rows * column_count
    pixel_ids = lax.iota(jnp.int32, pixel_count)
    onehot = (pixel_ids[:, None] == got_pixels[None, :]).astype(jnp.bfloat16)
    gridded = jnp.dot(onehot, got_values, preferred_element_type=jnp.float32)
    gridded = gridded.reshape(2, band_rows, column_count, obs_width)

    last_tile = tile_at == tile_count - 1
    matching_row = lax.dynamic_index_in_dim(matching, face_at, 0, keepdims=False)

    lifted = kernel_one.shape[2]
    both = extend_rows(jnp.concatenate([base_field, cot_field], axis=3), last_tile)
    cot_back, cot_margins = conv_pallas(both, channels, channels, None, kernel_two, True)
    base_edges, cot_gathered = gather_faces(
        [edge_cols(both, 0, channels), jnp.swapaxes(cot_margins, 1, 2)], 0
    )

    first_out = conv_pallas(both, 0, channels, side_columns(base_edges, matching_row), kernel_one, False)[0]
    pre_act = first_out + bias_one + gridded
    inner = activation(pre_act).astype(jnp.bfloat16)
    grad_inner = return_sides(cot_back, cot_gathered, matching_row)
    grad_pre = jax.vjp(activation, pre_act)[1](grad_inner)[0].astype(jnp.bfloat16)

    pair = extend_rows(jnp.concatenate([inner, grad_pre], axis=3), last_tile)
    pre_back, pre_margins = conv_pallas(pair, lifted, lifted, None, kernel_one, True)
    inner_edges, pre_gathered = gather_faces(
        [edge_cols(pair, 0, lifted), jnp.swapaxes(pre_margins, 1, 2)], 1
    )

    second_out = conv_pallas(pair, 0, lifted, side_columns(inner_edges, matching_row), kernel_two, False)[0]
    analysis = (base_field.astype(jnp.float32) + second_out + bias_two).astype(jnp.bfloat16)
    grad_base = cot_field.astype(jnp.float32) + return_sides(pre_back, pre_gathered, matching_row)
    return (analysis[None, None], grad_base[None, None])


def solution(mesh):
    return jax.shard_map(
        per_device,
        mesh=mesh,
        in_specs=(
            P("face", "tile", None, None, None, None),
            P(("face", "tile"), None),
            P(("face", "tile"), None),
            P(("face", "tile")),
            P(),
            P(),
            P(),
            P(),
            P(),
            P("face", "tile", None, None, None, None),
        ),
        out_specs=(
            P("face", "tile", None, None, None, None),
            P("face", "tile", None, None, None, None),
        ),
        check_vma=False,
    )
```

```python
import functools

import jax
import jax.numpy as jnp
from jax import lax
from jax.experimental import pallas as pl
from jax.experimental.pallas import tpu as pltpu
from jax.sharding import PartitionSpec as P

MESH_IDS = pl.DeviceIdType.MESH


def activation(values):
    return jax.nn.gelu(values, approximate=True)


def tap_index(band, row_tap, col_tap, backward):
    if backward:
        row = 2 - row_tap if band == 0 else row_tap
        return 3 * row + 2 - col_tap
    row = row_tap if band == 0 else 2 - row_tap
    return 3 * row + col_tap


def conv_kernel(backward, first, width, src_ref, before_ref, after_ref, side_ref, k_ref, out_ref, margin_ref):
    bands, rows, cols, cout = out_ref.shape
    pixels = rows * cols
    lanes = slice(first, first + width)
    col = lax.broadcasted_iota(jnp.int32, (rows, cols, cout), 1).reshape(pixels, cout)
    for band in range(bands):
        ext = jnp.concatenate(
            [before_ref[band, :, :, lanes], src_ref[band, :, :, lanes], after_ref[band, :, :, lanes]],
            axis=0,
        )
        lhs = jnp.concatenate(
            [ext[dy : dy + rows].reshape(pixels, width) for dy in range(3)], axis=1
        )
        stacks = []
        for col_tap in range(3):
            taps = [k_ref[tap_index(band, dy, col_tap, backward)] for dy in range(3)]
            if backward:
                stacks.append(jnp.concatenate(taps, axis=1))
            else:
                stacks.append(jnp.concatenate(taps, axis=0))

        def product(values, stack):
            if backward:
                return lax.dot_general(
                    values, stack, (((1,), (1,)), ((), ())), preferred_element_type=jnp.float32
                )
            return jnp.dot(values, stack, preferred_element_type=jnp.float32)

        z_left = product(lhs, stacks[0])
        z_mid = product(lhs, stacks[1])
        z_right = product(lhs, stacks[2])
        if backward or side_ref is None:
            left_full = jnp.zeros((pixels, cout), jnp.float32)
            right_full = left_full
        else:
            sides = side_ref[band]
            left = jnp.concatenate([sides[0, dy : dy + rows] for dy in range(3)], axis=1)
            right = jnp.concatenate([sides[1, dy : dy + rows] for dy in range(3)], axis=1)
            left_term = product(left, stacks[0])
            right_term = product(right, stacks[2])
            left_full = jnp.broadcast_to(left_term[:, None, :], (rows, cols, cout)).reshape(pixels, cout)
            right_full = jnp.broadcast_to(right_term[:, None, :], (rows, cols, cout)).reshape(pixels, cout)
        from_left = jnp.where(col == 0, left_full, pltpu.roll(z_left, 1, 0))
        from_right = jnp.where(col == cols - 1, right_full, pltpu.roll(z_right, pixels - 1, 0))
        out_ref[band] = (z_mid + from_left + from_right).reshape(rows, cols, cout)
        if backward:
            margin_ref[band, 0] = z_right.reshape(rows, cols, cout)[:, 0, :]
            margin_ref[band, 1] = z_left.reshape(rows, cols, cout)[:, cols - 1, :]


def conv_pallas(pieces, first, width, sides, kernel, backward):
    source, before, after = pieces
    bands, rows, cols, _ = source.shape
    cout = kernel.shape[1] if backward else kernel.shape[2]
    if sides is None:
        sides = jnp.zeros((bands, 2, rows + 2, width), jnp.bfloat16)
    vmem = pl.BlockSpec(memory_space=pltpu.VMEM)
    out, margins = pl.pallas_call(
        functools.partial(conv_kernel, backward, first, width),
        in_specs=[vmem] * 5,
        out_specs=[vmem, vmem],
        out_shape=[
            jax.ShapeDtypeStruct((bands, rows, cols, cout), jnp.float32),
            jax.ShapeDtypeStruct((bands, 2, rows, cout), jnp.float32),
        ],
        compiler_params=pltpu.CompilerParams(vmem_limit_bytes=60 * 1024 * 1024),
    )(source, before, after, sides, kernel)
    return out, margins


def conv_gather_kernel(count, first, width, block_ref, src_ref, before_ref, after_ref, k_ref,
                       out_ref, gathered_ref, landed, send_sems, recv_sems):
    face = lax.axis_index("face")
    tile = lax.axis_index("tile")
    barrier = pltpu.get_barrier_semaphore()
    for step in range(1, count):
        peer = lax.rem(face + step, count)
        pl.semaphore_signal(barrier, inc=1, device_id=(peer, tile), device_id_type=MESH_IDS)
    pl.semaphore_wait(barrier, count - 1)
    copies = []
    for step in range(1, count):
        peer = lax.rem(face + step, count)
        copy = pltpu.make_async_remote_copy(
            src_ref=block_ref,
            dst_ref=landed.at[step],
            send_sem=send_sems.at[step],
            recv_sem=recv_sems.at[step],
            device_id=(peer, tile),
            device_id_type=MESH_IDS,
        )
        copy.start()
        copies.append(copy)
    gathered_ref[0] = block_ref[...]
    conv_kernel(False, first, width, src_ref, before_ref, after_ref, None, k_ref, out_ref, None)
    for copy in copies:
        copy.wait()
    for step in range(1, count):
        gathered_ref[step] = landed[step]


def conv_gather(pieces, first, width, block, kernel, gather_id):
    source, before, after = pieces
    bands, rows, cols, _ = source.shape
    cout = kernel.shape[2]
    count = lax.axis_size("face")
    block_rows, lanes = block.shape
    vmem = pl.BlockSpec(memory_space=pltpu.VMEM)
    return pl.pallas_call(
        functools.partial(conv_gather_kernel, count, first, width),
        in_specs=[vmem] * 5,
        out_specs=[vmem, vmem],
        out_shape=[
            jax.ShapeDtypeStruct((bands, rows, cols, cout), jnp.float32),
            jax.ShapeDtypeStruct((count, block_rows, lanes), block.dtype),
        ],
        scratch_shapes=[
            pltpu.VMEM((count, block_rows, lanes), block.dtype),
            pltpu.SemaphoreType.DMA((count,)),
            pltpu.SemaphoreType.DMA((count,)),
        ],
        compiler_params=pltpu.CompilerParams(
            collective_id=gather_id, has_side_effects=True, vmem_limit_bytes=60 * 1024 * 1024
        ),
    )(block, source, before, after, kernel)


def side_terms(sides, kernel):
    bands, _, ext_rows, width = sides.shape
    rows = ext_rows - 2
    terms = []
    for band in range(bands):
        per_side = []
        for side, col_tap in ((0, 0), (1, 2)):
            stacked = jnp.concatenate([sides[band, side, dy : dy + rows] for dy in range(3)], axis=1)
            weights = jnp.concatenate(
                [kernel[tap_index(band, dy, col_tap, False)] for dy in range(3)], axis=0
            )
            per_side.append(jnp.dot(stacked, weights, preferred_element_type=jnp.float32))
        terms.append(jnp.stack(per_side))
    return jnp.stack(terms)


def at_edges(field, left_add, right_add):
    cols = field.shape[2]
    col = lax.broadcasted_iota(jnp.int32, field.shape, 2)
    return field + jnp.where(col == 0, left_add[:, :, None], 0.0) + jnp.where(
        col == cols - 1, right_add[:, :, None], 0.0
    )


def extend_rows(source, last_tile):
    count = lax.axis_size("tile")
    band_rows = source.shape[1]
    head = source[:, 0:1]
    tail = source[:, band_rows - 1 : band_rows]
    before = lax.ppermute(tail, "tile", [(i, i + 1) for i in range(count - 1)])
    after = lax.ppermute(head, "tile", [(i + 1, i) for i in range(count - 1)])
    after = jnp.where(last_tile, tail[::-1], after)
    return source, before, after


def edge_cols(pieces, first, width):
    extended = jnp.concatenate([piece[..., first : first + width] for piece in (pieces[1], pieces[0], pieces[2])], axis=1)
    return jnp.stack([extended[:, :, 0], extended[:, :, -1]], axis=2)


def pick_partner(gathered, matching_row):
    picked_sides = []
    for side_number in range(2):
        partner = matching_row[side_number, 0]
        their_side = matching_row[side_number, 1]
        flipped = matching_row[side_number, 2]
        chosen = lax.dynamic_index_in_dim(gathered, partner, 0, keepdims=False)
        column = jnp.where(their_side == 0, chosen[:, :, 0], chosen[:, :, 1])
        column = jnp.where(flipped == 1, column[::-1], column)
        picked_sides.append(column)
    return picked_sides


def pack_parts(parts):
    flat = jnp.concatenate([part.astype(jnp.float32).reshape(-1) for part in parts])
    return flat.reshape(-1, 128)


def unpack_parts(landed, parts):
    face_count = lax.axis_size("face")
    face_at = lax.axis_index("face")
    landed = landed.reshape(face_count, -1)
    slot_of_face = lax.rem(face_at - lax.iota(jnp.int32, face_count) + face_count, face_count)
    gathered = jnp.take(landed, slot_of_face, axis=0)
    pieces = []
    offset = 0
    for part in parts:
        size = part.size
        piece = gathered[:, offset : offset + size].reshape((face_count,) + part.shape)
        pieces.append(piece)
        offset += size
    return pieces


def side_columns(gathered_edges, matching_row):
    left_side, right_side = pick_partner(gathered_edges, matching_row)
    return jnp.stack([left_side, right_side], axis=1).astype(jnp.bfloat16)


def add_ends(field, first_add, last_add, axis):
    length = field.shape[axis]
    head = lax.slice_in_dim(field, 0, 1, axis=axis) + jnp.expand_dims(first_add, axis)
    middle = lax.slice_in_dim(field, 1, length - 1, axis=axis)
    tail = lax.slice_in_dim(field, length - 1, length, axis=axis) + jnp.expand_dims(last_add, axis)
    return jnp.concatenate([head, middle, tail], axis=axis)


def return_sides(inside, gathered_margins, matching_row):
    left_back, right_back = pick_partner(gathered_margins, matching_row)
    return at_edges(inside, left_back, right_back)


def route_observations(obs_values, obs_dest, obs_pixel, device_count):
    obs_rows = obs_values.shape[0]
    obs_width = obs_values.shape[1]
    capacity = 2 * obs_rows // device_count
    target = obs_dest[:, 0]
    positions = lax.iota(jnp.int32, obs_rows)
    same_target = (target[:, None] == target[None, :]) & (positions[None, :] < positions[:, None])
    rank_within = jnp.sum(same_target.astype(jnp.int32), axis=1)
    slot_index = target * capacity + rank_within
    slot_ids = lax.iota(jnp.int32, device_count * capacity)
    hits = slot_ids[:, None] == slot_index[None, :]
    value_slots = jnp.dot(
        hits.astype(jnp.bfloat16), obs_values, preferred_element_type=jnp.float32
    ).astype(jnp.bfloat16)
    pixel_slots = jnp.sum(jnp.where(hits, obs_pixel[None, :], 0), axis=1)
    high = (pixel_slots // 16).astype(jnp.bfloat16).reshape(device_count, capacity)
    low = (pixel_slots % 16).astype(jnp.bfloat16).reshape(device_count, capacity)
    pixel_row = jnp.concatenate(
        [high, low, jnp.zeros((device_count, obs_width - 2 * capacity), jnp.bfloat16)], axis=1
    )
    payload = jnp.concatenate(
        [value_slots.reshape(device_count, capacity, obs_width), pixel_row[:, None]], axis=1
    )
    arrived = lax.all_to_all(payload, ("face", "tile"), split_axis=0, concat_axis=0, tiled=True)
    got_values = arrived[:, :capacity].reshape(-1, obs_width)
    got_high = arrived[:, capacity, 0:capacity].astype(jnp.int32)
    got_low = arrived[:, capacity, capacity : 2 * capacity].astype(jnp.int32)
    got_pixels = (got_high * 16 + got_low).reshape(-1)
    return got_values, got_pixels


def per_device(
    state,
    obs_values,
    obs_dest,
    obs_pixel,
    matching,
    kernel_one,
    bias_one,
    kernel_two,
    bias_two,
    cotangent,
):
    base_field = state[0, 0]
    cot_field = cotangent[0, 0]
    band_rows = base_field.shape[1]
    column_count = base_field.shape[2]
    channels = base_field.shape[3]
    tile_count = lax.axis_size("tile")
    face_count = lax.axis_size("face")
    tile_at = lax.axis_index("tile")
    face_at = lax.axis_index("face")
    device_count = tile_count * face_count
    obs_width = obs_values.shape[1]

    got_values, got_pixels = route_observations(obs_values, obs_dest, obs_pixel, device_count)
    pixel_count = 2 * band_rows * column_count
    pixel_ids = lax.iota(jnp.int32, pixel_count)
    onehot = (pixel_ids[:, None] == got_pixels[None, :]).astype(jnp.bfloat16)
    gridded = jnp.dot(onehot, got_values, preferred_element_type=jnp.float32)
    gridded = gridded.reshape(2, band_rows, column_count, obs_width)

    last_tile = tile_at == tile_count - 1
    matching_row = lax.dynamic_index_in_dim(matching, face_at, 0, keepdims=False)

    lifted = kernel_one.shape[2]
    both = extend_rows(jnp.concatenate([base_field, cot_field], axis=3), last_tile)
    cot_back, cot_margins = conv_pallas(both, channels, channels, None, kernel_two, True)
    parts = [edge_cols(both, 0, channels), jnp.swapaxes(cot_margins, 1, 2)]
    first_out, landed = conv_gather(both, 0, channels, pack_parts(parts), kernel_one, 0)
    base_edges, cot_gathered = unpack_parts(landed, parts)
    first_sides = side_terms(side_columns(base_edges, matching_row), kernel_one)

    pre_act = at_edges(first_out, first_sides[:, 0], first_sides[:, 1]) + bias_one + gridded
    inner = activation(pre_act).astype(jnp.bfloat16)
    grad_inner = return_sides(cot_back, cot_gathered, matching_row)
    grad_pre = jax.vjp(activation, pre_act)[1](grad_inner)[0].astype(jnp.bfloat16)

    pair = extend_rows(jnp.concatenate([inner, grad_pre], axis=3), last_tile)
    pre_back, pre_margins = conv_pallas(pair, lifted, lifted, None, kernel_one, True)
    parts = [edge_cols(pair, 0, lifted), jnp.swapaxes(pre_margins, 1, 2)]
    second_out, landed = conv_gather(pair, 0, lifted, pack_parts(parts), kernel_two, 1)
    inner_edges, pre_gathered = unpack_parts(landed, parts)
    second_sides = side_terms(side_columns(inner_edges, matching_row), kernel_two)

    second_out = at_edges(second_out, second_sides[:, 0], second_sides[:, 1])
    analysis = (base_field.astype(jnp.float32) + second_out + bias_two).astype(jnp.bfloat16)
    grad_base = cot_field.astype(jnp.float32) + return_sides(pre_back, pre_gathered, matching_row)
    return (analysis[None, None], grad_base[None, None])


def solution(mesh):
    return jax.shard_map(
        per_device,
        mesh=mesh,
        in_specs=(
            P("face", "tile", None, None, None, None),
            P(("face", "tile"), None),
            P(("face", "tile"), None),
            P(("face", "tile")),
            P(),
            P(),
            P(),
            P(),
            P(),
            P("face", "tile", None, None, None, None),
        ),
        out_specs=(
            P("face", "tile", None, None, None, None),
            P("face", "tile", None, None, None, None),
        ),
        check_vma=False,
    )
```

```python
import functools

import jax
import jax.numpy as jnp
from jax import lax
from jax.experimental import pallas as pl
from jax.experimental.pallas import tpu as pltpu
from jax.sharding import PartitionSpec as P

MESH_IDS = pl.DeviceIdType.MESH


def activation(values):
    return jax.nn.gelu(values, approximate=True)


def tap_index(band, row_tap, col_tap, backward):
    if backward:
        row = 2 - row_tap if band == 0 else row_tap
        return 3 * row + 2 - col_tap
    row = row_tap if band == 0 else 2 - row_tap
    return 3 * row + col_tap


def conv_kernel(backward, first, width, src_ref, before_ref, after_ref, side_ref, k_ref, out_ref, margin_ref):
    bands, rows, cols, cout = out_ref.shape
    pixels = rows * cols
    lanes = slice(first, first + width)
    col = lax.broadcasted_iota(jnp.int32, (rows, cols, cout), 1).reshape(pixels, cout)
    for band in range(bands):
        ext = jnp.concatenate(
            [before_ref[band, :, :, lanes], src_ref[band, :, :, lanes], after_ref[band, :, :, lanes]],
            axis=0,
        )
        lhs = jnp.concatenate(
            [ext[dy : dy + rows].reshape(pixels, width) for dy in range(3)], axis=1
        )
        stacks = []
        for col_tap in range(3):
            taps = [k_ref[tap_index(band, dy, col_tap, backward)] for dy in range(3)]
            if backward:
                stacks.append(jnp.concatenate(taps, axis=1))
            else:
                stacks.append(jnp.concatenate(taps, axis=0))

        def product(values, stack):
            if backward:
                return lax.dot_general(
                    values, stack, (((1,), (1,)), ((), ())), preferred_element_type=jnp.float32
                )
            return jnp.dot(values, stack, preferred_element_type=jnp.float32)

        z_left = product(lhs, stacks[0])
        z_mid = product(lhs, stacks[1])
        z_right = product(lhs, stacks[2])
        if backward or side_ref is None:
            left_full = jnp.zeros((pixels, cout), jnp.float32)
            right_full = left_full
        else:
            sides = side_ref[band]
            left = jnp.concatenate([sides[0, dy : dy + rows] for dy in range(3)], axis=1)
            right = jnp.concatenate([sides[1, dy : dy + rows] for dy in range(3)], axis=1)
            left_term = product(left, stacks[0])
            right_term = product(right, stacks[2])
            left_full = jnp.broadcast_to(left_term[:, None, :], (rows, cols, cout)).reshape(pixels, cout)
            right_full = jnp.broadcast_to(right_term[:, None, :], (rows, cols, cout)).reshape(pixels, cout)
        from_left = jnp.where(col == 0, left_full, pltpu.roll(z_left, 1, 0))
        from_right = jnp.where(col == cols - 1, right_full, pltpu.roll(z_right, pixels - 1, 0))
        out_ref[band] = (z_mid + from_left + from_right).reshape(rows, cols, cout)
        if backward:
            margin_ref[band, 0] = z_right.reshape(rows, cols, cout)[:, 0, :]
            margin_ref[band, 1] = z_left.reshape(rows, cols, cout)[:, cols - 1, :]


def conv_pallas(pieces, first, width, sides, kernel, backward):
    source, before, after = pieces
    bands, rows, cols, _ = source.shape
    cout = kernel.shape[1] if backward else kernel.shape[2]
    if sides is None:
        sides = jnp.zeros((bands, 2, rows + 2, width), jnp.bfloat16)
    vmem = pl.BlockSpec(memory_space=pltpu.VMEM)
    out, margins = pl.pallas_call(
        functools.partial(conv_kernel, backward, first, width),
        in_specs=[vmem] * 5,
        out_specs=[vmem, vmem],
        out_shape=[
            jax.ShapeDtypeStruct((bands, rows, cols, cout), jnp.float32),
            jax.ShapeDtypeStruct((bands, 2, rows, cout), jnp.float32),
        ],
        compiler_params=pltpu.CompilerParams(vmem_limit_bytes=60 * 1024 * 1024),
    )(source, before, after, sides, kernel)
    return out, margins


def conv_gather_kernel(count, first, width, block_ref, src_ref, before_ref, after_ref, k_ref,
                       out_ref, gathered_ref, landed, send_sems, recv_sems):
    face = lax.axis_index("face")
    tile = lax.axis_index("tile")
    barrier = pltpu.get_barrier_semaphore()
    for step in range(1, count):
        peer = lax.rem(face + step, count)
        pl.semaphore_signal(barrier, inc=1, device_id=(peer, tile), device_id_type=MESH_IDS)
    pl.semaphore_wait(barrier, count - 1)
    copies = []
    for step in range(1, count):
        peer = lax.rem(face + step, count)
        copy = pltpu.make_async_remote_copy(
            src_ref=block_ref,
            dst_ref=landed.at[step],
            send_sem=send_sems.at[step],
            recv_sem=recv_sems.at[step],
            device_id=(peer, tile),
            device_id_type=MESH_IDS,
        )
        copy.start()
        copies.append(copy)
    gathered_ref[0] = block_ref[...]
    conv_kernel(False, first, width, src_ref, before_ref, after_ref, None, k_ref, out_ref, None)
    for copy in copies:
        copy.wait()
    for step in range(1, count):
        gathered_ref[step] = landed[step]


def conv_gather(pieces, first, width, block, kernel, gather_id):
    source, before, after = pieces
    bands, rows, cols, _ = source.shape
    cout = kernel.shape[2]
    count = lax.axis_size("face")
    block_rows, lanes = block.shape
    vmem = pl.BlockSpec(memory_space=pltpu.VMEM)
    return pl.pallas_call(
        functools.partial(conv_gather_kernel, count, first, width),
        in_specs=[vmem] * 5,
        out_specs=[vmem, vmem],
        out_shape=[
            jax.ShapeDtypeStruct((bands, rows, cols, cout), jnp.float32),
            jax.ShapeDtypeStruct((count, block_rows, lanes), block.dtype),
        ],
        scratch_shapes=[
            pltpu.VMEM((count, block_rows, lanes), block.dtype),
            pltpu.SemaphoreType.DMA((count,)),
            pltpu.SemaphoreType.DMA((count,)),
        ],
        compiler_params=pltpu.CompilerParams(
            collective_id=gather_id, has_side_effects=True, vmem_limit_bytes=60 * 1024 * 1024
        ),
    )(block, source, before, after, kernel)


def side_terms(sides, kernel):
    bands, _, ext_rows, width = sides.shape
    rows = ext_rows - 2
    terms = []
    for band in range(bands):
        per_side = []
        for side, col_tap in ((0, 0), (1, 2)):
            stacked = jnp.concatenate([sides[band, side, dy : dy + rows] for dy in range(3)], axis=1)
            weights = jnp.concatenate(
                [kernel[tap_index(band, dy, col_tap, False)] for dy in range(3)], axis=0
            )
            per_side.append(jnp.dot(stacked, weights, preferred_element_type=jnp.float32))
        terms.append(jnp.stack(per_side))
    return jnp.stack(terms)


def at_edges(field, left_add, right_add):
    cols = field.shape[2]
    col = lax.broadcasted_iota(jnp.int32, field.shape, 2)
    return field + jnp.where(col == 0, left_add[:, :, None], 0.0) + jnp.where(
        col == cols - 1, right_add[:, :, None], 0.0
    )


def extend_rows(source, last_tile):
    count = lax.axis_size("tile")
    band_rows = source.shape[1]
    head = source[:, 0:1]
    tail = source[:, band_rows - 1 : band_rows]
    before = lax.ppermute(tail, "tile", [(i, i + 1) for i in range(count - 1)])
    after = lax.ppermute(head, "tile", [(i + 1, i) for i in range(count - 1)])
    after = jnp.where(last_tile, tail[::-1], after)
    return source, before, after


def edge_cols(pieces, first, width):
    extended = jnp.concatenate([piece[..., first : first + width] for piece in (pieces[1], pieces[0], pieces[2])], axis=1)
    return jnp.stack([extended[:, :, 0], extended[:, :, -1]], axis=2)


def pick_partner(gathered, matching_row):
    picked_sides = []
    for side_number in range(2):
        partner = matching_row[side_number, 0]
        their_side = matching_row[side_number, 1]
        flipped = matching_row[side_number, 2]
        chosen = lax.dynamic_index_in_dim(gathered, partner, 0, keepdims=False)
        column = jnp.where(their_side == 0, chosen[:, :, 0], chosen[:, :, 1])
        column = jnp.where(flipped == 1, column[::-1], column)
        picked_sides.append(column)
    return picked_sides


def pack_parts(parts):
    flat = jnp.concatenate([part.astype(jnp.float32).reshape(-1) for part in parts])
    return flat.reshape(-1, 128)


def unpack_parts(landed, parts):
    face_count = lax.axis_size("face")
    face_at = lax.axis_index("face")
    landed = landed.reshape(face_count, -1)
    slot_of_face = lax.rem(face_at - lax.iota(jnp.int32, face_count) + face_count, face_count)
    gathered = jnp.take(landed, slot_of_face, axis=0)
    pieces = []
    offset = 0
    for part in parts:
        size = part.size
        piece = gathered[:, offset : offset + size].reshape((face_count,) + part.shape)
        pieces.append(piece)
        offset += size
    return pieces


def side_columns(gathered_edges, matching_row):
    left_side, right_side = pick_partner(gathered_edges, matching_row)
    return jnp.stack([left_side, right_side], axis=1).astype(jnp.bfloat16)


def add_ends(field, first_add, last_add, axis):
    length = field.shape[axis]
    head = lax.slice_in_dim(field, 0, 1, axis=axis) + jnp.expand_dims(first_add, axis)
    middle = lax.slice_in_dim(field, 1, length - 1, axis=axis)
    tail = lax.slice_in_dim(field, length - 1, length, axis=axis) + jnp.expand_dims(last_add, axis)
    return jnp.concatenate([head, middle, tail], axis=axis)


def return_sides(inside, gathered_margins, matching_row):
    left_back, right_back = pick_partner(gathered_margins, matching_row)
    return at_edges(inside, left_back, right_back)


def route_observations(obs_values, obs_dest, obs_pixel, device_count):
    obs_rows = obs_values.shape[0]
    obs_width = obs_values.shape[1]
    capacity = 2 * obs_rows // device_count
    target = obs_dest[:, 0]
    positions = lax.iota(jnp.int32, obs_rows)
    same_target = (target[:, None] == target[None, :]) & (positions[None, :] < positions[:, None])
    rank_within = jnp.sum(same_target.astype(jnp.int32), axis=1)
    slot_index = target * capacity + rank_within
    slot_ids = lax.iota(jnp.int32, device_count * capacity)
    hits = slot_ids[:, None] == slot_index[None, :]
    value_slots = jnp.dot(
        hits.astype(jnp.bfloat16), obs_values, preferred_element_type=jnp.float32
    ).astype(jnp.bfloat16)
    pixel_slots = jnp.sum(jnp.where(hits, obs_pixel[None, :], 0), axis=1)
    high = (pixel_slots // 16).astype(jnp.bfloat16).reshape(device_count, capacity)
    low = (pixel_slots % 16).astype(jnp.bfloat16).reshape(device_count, capacity)
    pixel_row = jnp.concatenate(
        [high, low, jnp.zeros((device_count, obs_width - 2 * capacity), jnp.bfloat16)], axis=1
    )
    payload = jnp.concatenate(
        [value_slots.reshape(device_count, capacity, obs_width), pixel_row[:, None]], axis=1
    )
    arrived = lax.all_to_all(payload, ("face", "tile"), split_axis=0, concat_axis=0, tiled=True)
    got_values = arrived[:, :capacity].reshape(-1, obs_width)
    got_high = arrived[:, capacity, 0:capacity].astype(jnp.int32)
    got_low = arrived[:, capacity, capacity : 2 * capacity].astype(jnp.int32)
    got_pixels = (got_high * 16 + got_low).reshape(-1)
    return got_values, got_pixels


def per_device(
    state,
    obs_values,
    obs_dest,
    obs_pixel,
    matching,
    kernel_one,
    bias_one,
    kernel_two,
    bias_two,
    cotangent,
):
    base_field = state[0, 0]
    cot_field = cotangent[0, 0]
    band_rows = base_field.shape[1]
    column_count = base_field.shape[2]
    channels = base_field.shape[3]
    tile_count = lax.axis_size("tile")
    face_count = lax.axis_size("face")
    tile_at = lax.axis_index("tile")
    face_at = lax.axis_index("face")
    device_count = tile_count * face_count
    obs_width = obs_values.shape[1]

    got_values, got_pixels = route_observations(obs_values, obs_dest, obs_pixel, device_count)
    pixel_count = 2 * band_rows * column_count
    pixel_ids = lax.iota(jnp.int32, pixel_count)
    onehot = (pixel_ids[:, None] == got_pixels[None, :]).astype(jnp.bfloat16)
    gridded = jnp.dot(onehot, got_values, preferred_element_type=jnp.float32)
    gridded = gridded.reshape(2, band_rows, column_count, obs_width)

    last_tile = tile_at == tile_count - 1
    matching_row = lax.dynamic_index_in_dim(matching, face_at, 0, keepdims=False)

    lifted = kernel_one.shape[2]
    cot_rows = extend_rows(cot_field, last_tile)
    base_src = lax.optimization_barrier((base_field, cot_rows[1], cot_rows[2]))[0]
    base_rows = extend_rows(base_src, last_tile)
    cot_back, cot_margins = conv_pallas(cot_rows, 0, channels, None, kernel_two, True)
    parts = [edge_cols(base_rows, 0, channels), jnp.swapaxes(cot_margins, 1, 2)]
    first_out, landed = conv_gather(base_rows, 0, channels, pack_parts(parts), kernel_one, 0)
    base_edges, cot_gathered = unpack_parts(landed, parts)
    first_sides = side_terms(side_columns(base_edges, matching_row), kernel_one)

    pre_act = at_edges(first_out, first_sides[:, 0], first_sides[:, 1]) + bias_one + gridded
    inner = activation(pre_act).astype(jnp.bfloat16)
    grad_inner = return_sides(cot_back, cot_gathered, matching_row)
    grad_pre = jax.vjp(activation, pre_act)[1](grad_inner)[0].astype(jnp.bfloat16)

    grad_pre_rows = extend_rows(grad_pre, last_tile)
    inner_src = lax.optimization_barrier((inner, grad_pre_rows[1], grad_pre_rows[2]))[0]
    inner_rows = extend_rows(inner_src, last_tile)
    pre_back, pre_margins = conv_pallas(grad_pre_rows, 0, lifted, None, kernel_one, True)
    parts = [edge_cols(inner_rows, 0, lifted), jnp.swapaxes(pre_margins, 1, 2)]
    second_out, landed = conv_gather(inner_rows, 0, lifted, pack_parts(parts), kernel_two, 1)
    inner_edges, pre_gathered = unpack_parts(landed, parts)
    second_sides = side_terms(side_columns(inner_edges, matching_row), kernel_two)

    second_out = at_edges(second_out, second_sides[:, 0], second_sides[:, 1])
    analysis = (base_field.astype(jnp.float32) + second_out + bias_two).astype(jnp.bfloat16)
    grad_base = cot_field.astype(jnp.float32) + return_sides(pre_back, pre_gathered, matching_row)
    return (analysis[None, None], grad_base[None, None])


def solution(mesh):
    return jax.shard_map(
        per_device,
        mesh=mesh,
        in_specs=(
            P("face", "tile", None, None, None, None),
            P(("face", "tile"), None),
            P(("face", "tile"), None),
            P(("face", "tile")),
            P(),
            P(),
            P(),
            P(),
            P(),
            P("face", "tile", None, None, None, None),
        ),
        out_specs=(
            P("face", "tile", None, None, None, None),
            P("face", "tile", None, None, None, None),
        ),
        check_vma=False,
    )
```

```python
import functools

import jax
import jax.numpy as jnp
from jax import lax
from jax.experimental import pallas as pl
from jax.experimental.pallas import tpu as pltpu
from jax.sharding import PartitionSpec as P

MESH_IDS = pl.DeviceIdType.MESH


def activation(values):
    return jax.nn.gelu(values, approximate=True)


def tap_index(band, row_tap, col_tap, backward):
    if backward:
        row = 2 - row_tap if band == 0 else row_tap
        return 3 * row + 2 - col_tap
    row = row_tap if band == 0 else 2 - row_tap
    return 3 * row + col_tap


def conv_kernel(backward, first, width, src_ref, before_ref, after_ref, side_ref, k_ref, out_ref, margin_ref):
    bands, rows, cols, cout = out_ref.shape
    pixels = rows * cols
    lanes = slice(first, first + width)
    col = lax.broadcasted_iota(jnp.int32, (rows, cols, cout), 1).reshape(pixels, cout)
    for band in range(bands):
        ext = jnp.concatenate(
            [before_ref[band, :, :, lanes], src_ref[band, :, :, lanes], after_ref[band, :, :, lanes]],
            axis=0,
        )
        lhs = jnp.concatenate(
            [ext[dy : dy + rows].reshape(pixels, width) for dy in range(3)], axis=1
        )
        stacks = []
        for col_tap in range(3):
            taps = [k_ref[tap_index(band, dy, col_tap, backward)] for dy in range(3)]
            if backward:
                stacks.append(jnp.concatenate(taps, axis=1))
            else:
                stacks.append(jnp.concatenate(taps, axis=0))

        def product(values, stack):
            if backward:
                return lax.dot_general(
                    values, stack, (((1,), (1,)), ((), ())), preferred_element_type=jnp.float32
                )
            return jnp.dot(values, stack, preferred_element_type=jnp.float32)

        z_left = product(lhs, stacks[0])
        z_mid = product(lhs, stacks[1])
        z_right = product(lhs, stacks[2])
        if backward or side_ref is None:
            left_full = jnp.zeros((pixels, cout), jnp.float32)
            right_full = left_full
        else:
            sides = side_ref[band]
            left = jnp.concatenate([sides[0, dy : dy + rows] for dy in range(3)], axis=1)
            right = jnp.concatenate([sides[1, dy : dy + rows] for dy in range(3)], axis=1)
            left_term = product(left, stacks[0])
            right_term = product(right, stacks[2])
            left_full = jnp.broadcast_to(left_term[:, None, :], (rows, cols, cout)).reshape(pixels, cout)
            right_full = jnp.broadcast_to(right_term[:, None, :], (rows, cols, cout)).reshape(pixels, cout)
        from_left = jnp.where(col == 0, left_full, pltpu.roll(z_left, 1, 0))
        from_right = jnp.where(col == cols - 1, right_full, pltpu.roll(z_right, pixels - 1, 0))
        out_ref[band] = (z_mid + from_left + from_right).reshape(rows, cols, cout)
        if backward:
            margin_ref[band, 0] = z_right.reshape(rows, cols, cout)[:, 0, :]
            margin_ref[band, 1] = z_left.reshape(rows, cols, cout)[:, cols - 1, :]


def conv_pallas(pieces, first, width, sides, kernel, backward):
    source, before, after = pieces
    bands, rows, cols, _ = source.shape
    cout = kernel.shape[1] if backward else kernel.shape[2]
    if sides is None:
        sides = jnp.zeros((bands, 2, rows + 2, width), jnp.bfloat16)
    vmem = pl.BlockSpec(memory_space=pltpu.VMEM)
    out, margins = pl.pallas_call(
        functools.partial(conv_kernel, backward, first, width),
        in_specs=[vmem] * 5,
        out_specs=[vmem, vmem],
        out_shape=[
            jax.ShapeDtypeStruct((bands, rows, cols, cout), jnp.float32),
            jax.ShapeDtypeStruct((bands, 2, rows, cout), jnp.float32),
        ],
        compiler_params=pltpu.CompilerParams(vmem_limit_bytes=60 * 1024 * 1024),
    )(source, before, after, sides, kernel)
    return out, margins


def conv_gather_kernel(count, first, width, block_ref, src_ref, before_ref, after_ref, k_ref,
                       out_ref, gathered_ref, landed, send_sems, recv_sems):
    face = lax.axis_index("face")
    tile = lax.axis_index("tile")
    barrier = pltpu.get_barrier_semaphore()
    for step in range(1, count):
        peer = lax.rem(face + step, count)
        pl.semaphore_signal(barrier, inc=1, device_id=(peer, tile), device_id_type=MESH_IDS)
    pl.semaphore_wait(barrier, count - 1)
    copies = []
    for step in range(1, count):
        peer = lax.rem(face + step, count)
        copy = pltpu.make_async_remote_copy(
            src_ref=block_ref,
            dst_ref=landed.at[step],
            send_sem=send_sems.at[step],
            recv_sem=recv_sems.at[step],
            device_id=(peer, tile),
            device_id_type=MESH_IDS,
        )
        copy.start()
        copies.append(copy)
    gathered_ref[0] = block_ref[...]
    conv_kernel(False, first, width, src_ref, before_ref, after_ref, None, k_ref, out_ref, None)
    for copy in copies:
        copy.wait()
    for step in range(1, count):
        gathered_ref[step] = landed[step]


def conv_gather(pieces, first, width, block, kernel, gather_id):
    source, before, after = pieces
    bands, rows, cols, _ = source.shape
    cout = kernel.shape[2]
    count = lax.axis_size("face")
    block_rows, lanes = block.shape
    vmem = pl.BlockSpec(memory_space=pltpu.VMEM)
    return pl.pallas_call(
        functools.partial(conv_gather_kernel, count, first, width),
        in_specs=[vmem] * 5,
        out_specs=[vmem, vmem],
        out_shape=[
            jax.ShapeDtypeStruct((bands, rows, cols, cout), jnp.float32),
            jax.ShapeDtypeStruct((count, block_rows, lanes), block.dtype),
        ],
        scratch_shapes=[
            pltpu.VMEM((count, block_rows, lanes), block.dtype),
            pltpu.SemaphoreType.DMA((count,)),
            pltpu.SemaphoreType.DMA((count,)),
        ],
        compiler_params=pltpu.CompilerParams(
            collective_id=gather_id, has_side_effects=True, vmem_limit_bytes=60 * 1024 * 1024
        ),
    )(block, source, before, after, kernel)


def side_terms(sides, kernel):
    bands, _, ext_rows, width = sides.shape
    rows = ext_rows - 2
    terms = []
    for band in range(bands):
        per_side = []
        for side, col_tap in ((0, 0), (1, 2)):
            stacked = jnp.concatenate([sides[band, side, dy : dy + rows] for dy in range(3)], axis=1)
            weights = jnp.concatenate(
                [kernel[tap_index(band, dy, col_tap, False)] for dy in range(3)], axis=0
            )
            per_side.append(jnp.dot(stacked, weights, preferred_element_type=jnp.float32))
        terms.append(jnp.stack(per_side))
    return jnp.stack(terms)


def at_edges(field, left_add, right_add):
    cols = field.shape[2]
    col = lax.broadcasted_iota(jnp.int32, field.shape, 2)
    return field + jnp.where(col == 0, left_add[:, :, None], 0.0) + jnp.where(
        col == cols - 1, right_add[:, :, None], 0.0
    )


def extend_rows(source, last_tile):
    band_rows = source.shape[1]
    return exchange_rows(source, source[:, 0:1], source[:, band_rows - 1 : band_rows], last_tile)


def exchange_rows(source, head, tail, last_tile):
    count = lax.axis_size("tile")
    before = lax.ppermute(tail, "tile", [(i, i + 1) for i in range(count - 1)])
    after = lax.ppermute(head, "tile", [(i + 1, i) for i in range(count - 1)])
    after = jnp.where(last_tile, tail[::-1], after)
    return source, before, after


def edge_cols(pieces, first, width):
    extended = jnp.concatenate([piece[..., first : first + width] for piece in (pieces[1], pieces[0], pieces[2])], axis=1)
    return jnp.stack([extended[:, :, 0], extended[:, :, -1]], axis=2)


def pick_partner(gathered, matching_row):
    picked_sides = []
    for side_number in range(2):
        partner = matching_row[side_number, 0]
        their_side = matching_row[side_number, 1]
        flipped = matching_row[side_number, 2]
        chosen = lax.dynamic_index_in_dim(gathered, partner, 0, keepdims=False)
        column = jnp.where(their_side == 0, chosen[:, :, 0], chosen[:, :, 1])
        column = jnp.where(flipped == 1, column[::-1], column)
        picked_sides.append(column)
    return picked_sides


def pack_parts(parts):
    flat = jnp.concatenate([part.astype(jnp.float32).reshape(-1) for part in parts])
    return flat.reshape(-1, 128)


def unpack_parts(landed, parts):
    face_count = lax.axis_size("face")
    face_at = lax.axis_index("face")
    landed = landed.reshape(face_count, -1)
    slot_of_face = lax.rem(face_at - lax.iota(jnp.int32, face_count) + face_count, face_count)
    gathered = jnp.take(landed, slot_of_face, axis=0)
    pieces = []
    offset = 0
    for part in parts:
        size = part.size
        piece = gathered[:, offset : offset + size].reshape((face_count,) + part.shape)
        pieces.append(piece)
        offset += size
    return pieces


def side_columns(gathered_edges, matching_row):
    left_side, right_side = pick_partner(gathered_edges, matching_row)
    return jnp.stack([left_side, right_side], axis=1).astype(jnp.bfloat16)


def add_ends(field, first_add, last_add, axis):
    length = field.shape[axis]
    head = lax.slice_in_dim(field, 0, 1, axis=axis) + jnp.expand_dims(first_add, axis)
    middle = lax.slice_in_dim(field, 1, length - 1, axis=axis)
    tail = lax.slice_in_dim(field, length - 1, length, axis=axis) + jnp.expand_dims(last_add, axis)
    return jnp.concatenate([head, middle, tail], axis=axis)


def return_sides(inside, gathered_margins, matching_row):
    left_back, right_back = pick_partner(gathered_margins, matching_row)
    return at_edges(inside, left_back, right_back)


def route_observations(obs_values, obs_dest, obs_pixel, device_count):
    obs_rows = obs_values.shape[0]
    obs_width = obs_values.shape[1]
    capacity = 2 * obs_rows // device_count
    target = obs_dest[:, 0]
    positions = lax.iota(jnp.int32, obs_rows)
    same_target = (target[:, None] == target[None, :]) & (positions[None, :] < positions[:, None])
    rank_within = jnp.sum(same_target.astype(jnp.int32), axis=1)
    slot_index = target * capacity + rank_within
    slot_ids = lax.iota(jnp.int32, device_count * capacity)
    hits = slot_ids[:, None] == slot_index[None, :]
    value_slots = jnp.dot(
        hits.astype(jnp.bfloat16), obs_values, preferred_element_type=jnp.float32
    ).astype(jnp.bfloat16)
    pixel_slots = jnp.sum(jnp.where(hits, obs_pixel[None, :], 0), axis=1)
    high = (pixel_slots // 16).astype(jnp.bfloat16).reshape(device_count, capacity)
    low = (pixel_slots % 16).astype(jnp.bfloat16).reshape(device_count, capacity)
    pixel_row = jnp.concatenate(
        [high, low, jnp.zeros((device_count, obs_width - 2 * capacity), jnp.bfloat16)], axis=1
    )
    payload = jnp.concatenate(
        [value_slots.reshape(device_count, capacity, obs_width), pixel_row[:, None]], axis=1
    )
    arrived = lax.all_to_all(payload, ("face", "tile"), split_axis=0, concat_axis=0, tiled=True)
    got_values = arrived[:, :capacity].reshape(-1, obs_width)
    got_high = arrived[:, capacity, 0:capacity].astype(jnp.int32)
    got_low = arrived[:, capacity, capacity : 2 * capacity].astype(jnp.int32)
    got_pixels = (got_high * 16 + got_low).reshape(-1)
    return got_values, got_pixels


def per_device(
    state,
    obs_values,
    obs_dest,
    obs_pixel,
    matching,
    kernel_one,
    bias_one,
    kernel_two,
    bias_two,
    cotangent,
):
    base_field = state[0, 0]
    cot_field = cotangent[0, 0]
    band_rows = base_field.shape[1]
    column_count = base_field.shape[2]
    channels = base_field.shape[3]
    tile_count = lax.axis_size("tile")
    face_count = lax.axis_size("face")
    tile_at = lax.axis_index("tile")
    face_at = lax.axis_index("face")
    device_count = tile_count * face_count
    obs_width = obs_values.shape[1]

    got_values, got_pixels = route_observations(obs_values, obs_dest, obs_pixel, device_count)
    pixel_count = 2 * band_rows * column_count
    pixel_ids = lax.iota(jnp.int32, pixel_count)
    onehot = (pixel_ids[:, None] == got_pixels[None, :]).astype(jnp.bfloat16)
    gridded = jnp.dot(onehot, got_values, preferred_element_type=jnp.float32)
    gridded = gridded.reshape(2, band_rows, column_count, obs_width)

    last_tile = tile_at == tile_count - 1
    matching_row = lax.dynamic_index_in_dim(matching, face_at, 0, keepdims=False)

    lifted = kernel_one.shape[2]
    both = extend_rows(jnp.concatenate([base_field, cot_field], axis=3), last_tile)
    gridded, cot_before = lax.optimization_barrier((gridded, both[1]))
    both = (both[0], cot_before, both[2])
    cot_back, cot_margins = conv_pallas(both, channels, channels, None, kernel_two, True)
    parts = [edge_cols(both, 0, channels), jnp.swapaxes(cot_margins, 1, 2)]
    first_out, landed = conv_gather(both, 0, channels, pack_parts(parts), kernel_one, 0)
    base_edges, cot_gathered = unpack_parts(landed, parts)
    first_sides = side_terms(side_columns(base_edges, matching_row), kernel_one)
    cot_left, cot_right = pick_partner(cot_gathered, matching_row)

    def epilogue(rows):
        pre_act = at_edges(first_out[:, rows], first_sides[:, 0, rows], first_sides[:, 1, rows])
        pre_act = pre_act + bias_one + gridded[:, rows]
        inner = activation(pre_act).astype(jnp.bfloat16)
        grad_inner = at_edges(cot_back[:, rows], cot_left[:, rows], cot_right[:, rows])
        grad_pre = jax.vjp(activation, pre_act)[1](grad_inner)[0].astype(jnp.bfloat16)
        return jnp.concatenate([inner, grad_pre], axis=3)

    edge_pair = epilogue(slice(0, band_rows, band_rows - 1))
    middle_pair = epilogue(slice(1, band_rows - 1))
    whole_pair = jnp.concatenate([edge_pair[:, 0:1], middle_pair, edge_pair[:, 1:2]], axis=1)
    pair = exchange_rows(whole_pair, edge_pair[:, 0:1], edge_pair[:, 1:2], last_tile)
    pre_back, pre_margins = conv_pallas(pair, lifted, lifted, None, kernel_one, True)
    parts = [edge_cols(pair, 0, lifted), jnp.swapaxes(pre_margins, 1, 2)]
    second_out, landed = conv_gather(pair, 0, lifted, pack_parts(parts), kernel_two, 1)
    inner_edges, pre_gathered = unpack_parts(landed, parts)
    second_sides = side_terms(side_columns(inner_edges, matching_row), kernel_two)

    second_out = at_edges(second_out, second_sides[:, 0], second_sides[:, 1])
    analysis = (base_field.astype(jnp.float32) + second_out + bias_two).astype(jnp.bfloat16)
    grad_base = cot_field.astype(jnp.float32) + return_sides(pre_back, pre_gathered, matching_row)
    return (analysis[None, None], grad_base[None, None])


def solution(mesh):
    return jax.shard_map(
        per_device,
        mesh=mesh,
        in_specs=(
            P("face", "tile", None, None, None, None),
            P(("face", "tile"), None),
            P(("face", "tile"), None),
            P(("face", "tile")),
            P(),
            P(),
            P(),
            P(),
            P(),
            P("face", "tile", None, None, None, None),
        ),
        out_specs=(
            P("face", "tile", None, None, None, None),
            P("face", "tile", None, None, None, None),
        ),
        check_vma=False,
    )
```

```python
import functools

import jax
import jax.numpy as jnp
from jax import lax
from jax.experimental import pallas as pl
from jax.experimental.pallas import tpu as pltpu
from jax.sharding import PartitionSpec as P

MESH_IDS = pl.DeviceIdType.MESH


def activation(values):
    return jax.nn.gelu(values, approximate=True)


def tap_index(band, row_tap, col_tap, backward):
    if backward:
        row = 2 - row_tap if band == 0 else row_tap
        return 3 * row + 2 - col_tap
    row = row_tap if band == 0 else 2 - row_tap
    return 3 * row + col_tap


def conv_kernel(backward, first, width, src_ref, before_ref, after_ref, side_ref, k_ref, out_ref, margin_ref):
    bands, rows, cols, cout = out_ref.shape
    pixels = rows * cols
    lanes = slice(first, first + width)
    col = lax.broadcasted_iota(jnp.int32, (rows, cols, cout), 1).reshape(pixels, cout)
    for band in range(bands):
        ext = jnp.concatenate(
            [before_ref[band, :, :, lanes], src_ref[band, :, :, lanes], after_ref[band, :, :, lanes]],
            axis=0,
        )
        lhs = jnp.concatenate(
            [ext[dy : dy + rows].reshape(pixels, width) for dy in range(3)], axis=1
        )
        stacks = []
        for col_tap in range(3):
            taps = [k_ref[tap_index(band, dy, col_tap, backward)] for dy in range(3)]
            if backward:
                stacks.append(jnp.concatenate(taps, axis=1))
            else:
                stacks.append(jnp.concatenate(taps, axis=0))

        def product(values, stack):
            if backward:
                return lax.dot_general(
                    values, stack, (((1,), (1,)), ((), ())), preferred_element_type=jnp.float32
                )
            return jnp.dot(values, stack, preferred_element_type=jnp.float32)

        z_left = product(lhs, stacks[0])
        z_mid = product(lhs, stacks[1])
        z_right = product(lhs, stacks[2])
        if backward or side_ref is None:
            left_full = jnp.zeros((pixels, cout), jnp.float32)
            right_full = left_full
        else:
            sides = side_ref[band]
            left = jnp.concatenate([sides[0, dy : dy + rows] for dy in range(3)], axis=1)
            right = jnp.concatenate([sides[1, dy : dy + rows] for dy in range(3)], axis=1)
            left_term = product(left, stacks[0])
            right_term = product(right, stacks[2])
            left_full = jnp.broadcast_to(left_term[:, None, :], (rows, cols, cout)).reshape(pixels, cout)
            right_full = jnp.broadcast_to(right_term[:, None, :], (rows, cols, cout)).reshape(pixels, cout)
        from_left = jnp.where(col == 0, left_full, pltpu.roll(z_left, 1, 0))
        from_right = jnp.where(col == cols - 1, right_full, pltpu.roll(z_right, pixels - 1, 0))
        out_ref[band] = (z_mid + from_left + from_right).reshape(rows, cols, cout)
        if backward:
            margin_ref[band, 0] = z_right.reshape(rows, cols, cout)[:, 0, :]
            margin_ref[band, 1] = z_left.reshape(rows, cols, cout)[:, cols - 1, :]


def conv_pallas(pieces, first, width, sides, kernel, backward):
    source, before, after = pieces
    bands, rows, cols, _ = source.shape
    cout = kernel.shape[1] if backward else kernel.shape[2]
    if sides is None:
        sides = jnp.zeros((bands, 2, rows + 2, width), jnp.bfloat16)
    vmem = pl.BlockSpec(memory_space=pltpu.VMEM)
    out, margins = pl.pallas_call(
        functools.partial(conv_kernel, backward, first, width),
        in_specs=[vmem] * 5,
        out_specs=[vmem, vmem],
        out_shape=[
            jax.ShapeDtypeStruct((bands, rows, cols, cout), jnp.float32),
            jax.ShapeDtypeStruct((bands, 2, rows, cout), jnp.float32),
        ],
        compiler_params=pltpu.CompilerParams(vmem_limit_bytes=60 * 1024 * 1024),
    )(source, before, after, sides, kernel)
    return out, margins


def back_kernel(src_ref, before_ref, after_ref, k_ref, out_ref, margin_ref):
    band = pl.program_id(0)
    _, rows, cols, cout = out_ref.shape
    width = src_ref.shape[3]
    pixels = rows * cols
    col = lax.broadcasted_iota(jnp.int32, (rows, cols, cout), 1).reshape(pixels, cout)
    ext = jnp.concatenate([before_ref[0], src_ref[0], after_ref[0]], axis=0)
    lhs = jnp.concatenate([ext[dy : dy + rows].reshape(pixels, width) for dy in range(3)], axis=1)
    products = []
    for col_tap in range(3):
        taps = [k_ref[3 * (2 - dy + band * (2 * dy - 2)) + 2 - col_tap] for dy in range(3)]
        stack = jnp.concatenate(taps, axis=1)
        products.append(
            lax.dot_general(lhs, stack, (((1,), (1,)), ((), ())), preferred_element_type=jnp.float32)
        )
    z_left, z_mid, z_right = products
    from_left = jnp.where(col == 0, 0.0, pltpu.roll(z_left, 1, 0))
    from_right = jnp.where(col == cols - 1, 0.0, pltpu.roll(z_right, pixels - 1, 0))
    out_ref[0] = (z_mid + from_left + from_right).reshape(rows, cols, cout)
    margin_ref[0, 0] = z_right.reshape(rows, cols, cout)[:, 0, :]
    margin_ref[0, 1] = z_left.reshape(rows, cols, cout)[:, cols - 1, :]


def conv_back(pieces, first, width, kernel):
    source, before, after = pieces
    bands, rows, cols, _ = source.shape
    cout = kernel.shape[1]
    block = first // width
    return pl.pallas_call(
        back_kernel,
        grid=(bands,),
        in_specs=[
            pl.BlockSpec((1, rows, cols, width), lambda b: (b, 0, 0, block)),
            pl.BlockSpec((1, 1, cols, width), lambda b: (b, 0, 0, block)),
            pl.BlockSpec((1, 1, cols, width), lambda b: (b, 0, 0, block)),
            pl.BlockSpec(kernel.shape, lambda b: (0, 0, 0)),
        ],
        out_specs=[
            pl.BlockSpec((1, rows, cols, cout), lambda b: (b, 0, 0, 0)),
            pl.BlockSpec((1, 2, rows, cout), lambda b: (b, 0, 0, 0)),
        ],
        out_shape=[
            jax.ShapeDtypeStruct((bands, rows, cols, cout), jnp.float32),
            jax.ShapeDtypeStruct((bands, 2, rows, cout), jnp.float32),
        ],
        compiler_params=pltpu.CompilerParams(vmem_limit_bytes=60 * 1024 * 1024),
    )(source, before, after, kernel)


def conv_gather_kernel(count, first, width, block_ref, src_ref, before_ref, after_ref, k_ref,
                       out_ref, gathered_ref, landed, send_sems, recv_sems):
    face = lax.axis_index("face")
    tile = lax.axis_index("tile")
    barrier = pltpu.get_barrier_semaphore()
    for step in range(1, count):
        peer = lax.rem(face + step, count)
        pl.semaphore_signal(barrier, inc=1, device_id=(peer, tile), device_id_type=MESH_IDS)
    pl.semaphore_wait(barrier, count - 1)
    copies = []
    for step in range(1, count):
        peer = lax.rem(face + step, count)
        copy = pltpu.make_async_remote_copy(
            src_ref=block_ref,
            dst_ref=landed.at[step],
            send_sem=send_sems.at[step],
            recv_sem=recv_sems.at[step],
            device_id=(peer, tile),
            device_id_type=MESH_IDS,
        )
        copy.start()
        copies.append(copy)
    gathered_ref[0] = block_ref[...]
    conv_kernel(False, first, width, src_ref, before_ref, after_ref, None, k_ref, out_ref, None)
    for copy in copies:
        copy.wait()
    for step in range(1, count):
        gathered_ref[step] = landed[step]


def conv_gather(pieces, first, width, block, kernel, gather_id):
    source, before, after = pieces
    bands, rows, cols, _ = source.shape
    cout = kernel.shape[2]
    count = lax.axis_size("face")
    block_rows, lanes = block.shape
    vmem = pl.BlockSpec(memory_space=pltpu.VMEM)
    return pl.pallas_call(
        functools.partial(conv_gather_kernel, count, first, width),
        in_specs=[vmem] * 5,
        out_specs=[vmem, vmem],
        out_shape=[
            jax.ShapeDtypeStruct((bands, rows, cols, cout), jnp.float32),
            jax.ShapeDtypeStruct((count, block_rows, lanes), block.dtype),
        ],
        scratch_shapes=[
            pltpu.VMEM((count, block_rows, lanes), block.dtype),
            pltpu.SemaphoreType.DMA((count,)),
            pltpu.SemaphoreType.DMA((count,)),
        ],
        compiler_params=pltpu.CompilerParams(
            collective_id=gather_id, has_side_effects=True, vmem_limit_bytes=60 * 1024 * 1024
        ),
    )(block, source, before, after, kernel)


def side_terms(sides, kernel):
    bands, _, ext_rows, width = sides.shape
    rows = ext_rows - 2
    terms = []
    for band in range(bands):
        per_side = []
        for side, col_tap in ((0, 0), (1, 2)):
            stacked = jnp.concatenate([sides[band, side, dy : dy + rows] for dy in range(3)], axis=1)
            weights = jnp.concatenate(
                [kernel[tap_index(band, dy, col_tap, False)] for dy in range(3)], axis=0
            )
            per_side.append(jnp.dot(stacked, weights, preferred_element_type=jnp.float32))
        terms.append(jnp.stack(per_side))
    return jnp.stack(terms)


def at_edges(field, left_add, right_add):
    cols = field.shape[2]
    col = lax.broadcasted_iota(jnp.int32, field.shape, 2)
    return field + jnp.where(col == 0, left_add[:, :, None], 0.0) + jnp.where(
        col == cols - 1, right_add[:, :, None], 0.0
    )


def extend_rows(source, last_tile):
    count = lax.axis_size("tile")
    band_rows = source.shape[1]
    head = source[:, 0:1]
    tail = source[:, band_rows - 1 : band_rows]
    before = lax.ppermute(tail, "tile", [(i, i + 1) for i in range(count - 1)])
    after = lax.ppermute(head, "tile", [(i + 1, i) for i in range(count - 1)])
    after = jnp.where(last_tile, tail[::-1], after)
    return source, before, after


def edge_cols(pieces, first, width):
    extended = jnp.concatenate([piece[..., first : first + width] for piece in (pieces[1], pieces[0], pieces[2])], axis=1)
    return jnp.stack([extended[:, :, 0], extended[:, :, -1]], axis=2)


def pick_partner(gathered, matching_row):
    picked_sides = []
    for side_number in range(2):
        partner = matching_row[side_number, 0]
        their_side = matching_row[side_number, 1]
        flipped = matching_row[side_number, 2]
        chosen = lax.dynamic_index_in_dim(gathered, partner, 0, keepdims=False)
        column = jnp.where(their_side == 0, chosen[:, :, 0], chosen[:, :, 1])
        column = jnp.where(flipped == 1, column[::-1], column)
        picked_sides.append(column)
    return picked_sides


def pack_parts(parts):
    flat = jnp.concatenate([part.astype(jnp.float32).reshape(-1) for part in parts])
    return flat.reshape(-1, 128)


def unpack_parts(landed, parts):
    face_count = lax.axis_size("face")
    face_at = lax.axis_index("face")
    landed = landed.reshape(face_count, -1)
    slot_of_face = lax.rem(face_at - lax.iota(jnp.int32, face_count) + face_count, face_count)
    gathered = jnp.take(landed, slot_of_face, axis=0)
    pieces = []
    offset = 0
    for part in parts:
        size = part.size
        piece = gathered[:, offset : offset + size].reshape((face_count,) + part.shape)
        pieces.append(piece)
        offset += size
    return pieces


def side_columns(gathered_edges, matching_row):
    left_side, right_side = pick_partner(gathered_edges, matching_row)
    return jnp.stack([left_side, right_side], axis=1).astype(jnp.bfloat16)


def add_ends(field, first_add, last_add, axis):
    length = field.shape[axis]
    head = lax.slice_in_dim(field, 0, 1, axis=axis) + jnp.expand_dims(first_add, axis)
    middle = lax.slice_in_dim(field, 1, length - 1, axis=axis)
    tail = lax.slice_in_dim(field, length - 1, length, axis=axis) + jnp.expand_dims(last_add, axis)
    return jnp.concatenate([head, middle, tail], axis=axis)


def return_sides(inside, gathered_margins, matching_row):
    left_back, right_back = pick_partner(gathered_margins, matching_row)
    return at_edges(inside, left_back, right_back)


def route_observations(obs_values, obs_dest, obs_pixel, device_count):
    obs_rows = obs_values.shape[0]
    obs_width = obs_values.shape[1]
    capacity = 2 * obs_rows // device_count
    target = obs_dest[:, 0]
    positions = lax.iota(jnp.int32, obs_rows)
    same_target = (target[:, None] == target[None, :]) & (positions[None, :] < positions[:, None])
    rank_within = jnp.sum(same_target.astype(jnp.int32), axis=1)
    slot_index = target * capacity + rank_within
    slot_ids = lax.iota(jnp.int32, device_count * capacity)
    hits = slot_ids[:, None] == slot_index[None, :]
    value_slots = jnp.dot(
        hits.astype(jnp.bfloat16), obs_values, preferred_element_type=jnp.float32
    ).astype(jnp.bfloat16)
    pixel_slots = jnp.sum(jnp.where(hits, obs_pixel[None, :], 0), axis=1)
    high = (pixel_slots // 16).astype(jnp.bfloat16).reshape(device_count, capacity)
    low = (pixel_slots % 16).astype(jnp.bfloat16).reshape(device_count, capacity)
    pixel_row = jnp.concatenate(
        [high, low, jnp.zeros((device_count, obs_width - 2 * capacity), jnp.bfloat16)], axis=1
    )
    payload = jnp.concatenate(
        [value_slots.reshape(device_count, capacity, obs_width), pixel_row[:, None]], axis=1
    )
    arrived = lax.all_to_all(payload, ("face", "tile"), split_axis=0, concat_axis=0, tiled=True)
    got_values = arrived[:, :capacity].reshape(-1, obs_width)
    got_high = arrived[:, capacity, 0:capacity].astype(jnp.int32)
    got_low = arrived[:, capacity, capacity : 2 * capacity].astype(jnp.int32)
    got_pixels = (got_high * 16 + got_low).reshape(-1)
    return got_values, got_pixels


def per_device(
    state,
    obs_values,
    obs_dest,
    obs_pixel,
    matching,
    kernel_one,
    bias_one,
    kernel_two,
    bias_two,
    cotangent,
):
    base_field = state[0, 0]
    cot_field = cotangent[0, 0]
    band_rows = base_field.shape[1]
    column_count = base_field.shape[2]
    channels = base_field.shape[3]
    tile_count = lax.axis_size("tile")
    face_count = lax.axis_size("face")
    tile_at = lax.axis_index("tile")
    face_at = lax.axis_index("face")
    device_count = tile_count * face_count
    obs_width = obs_values.shape[1]

    got_values, got_pixels = route_observations(obs_values, obs_dest, obs_pixel, device_count)
    pixel_count = 2 * band_rows * column_count
    pixel_ids = lax.iota(jnp.int32, pixel_count)
    onehot = (pixel_ids[:, None] == got_pixels[None, :]).astype(jnp.bfloat16)
    gridded = jnp.dot(onehot, got_values, preferred_element_type=jnp.float32)
    gridded = gridded.reshape(2, band_rows, column_count, obs_width)

    last_tile = tile_at == tile_count - 1
    matching_row = lax.dynamic_index_in_dim(matching, face_at, 0, keepdims=False)

    lifted = kernel_one.shape[2]
    both = extend_rows(jnp.concatenate([base_field, cot_field], axis=3), last_tile)
    cot_back, cot_margins = conv_back(both, channels, channels, kernel_two)
    parts = [edge_cols(both, 0, channels), jnp.swapaxes(cot_margins, 1, 2)]
    first_out, landed = conv_gather(both, 0, channels, pack_parts(parts), kernel_one, 0)
    base_edges, cot_gathered = unpack_parts(landed, parts)
    first_sides = side_terms(side_columns(base_edges, matching_row), kernel_one)

    pre_act = at_edges(first_out, first_sides[:, 0], first_sides[:, 1]) + bias_one + gridded
    inner = activation(pre_act).astype(jnp.bfloat16)
    grad_inner = return_sides(cot_back, cot_gathered, matching_row)
    grad_pre = jax.vjp(activation, pre_act)[1](grad_inner)[0].astype(jnp.bfloat16)

    pair = extend_rows(jnp.concatenate([inner, grad_pre], axis=3), last_tile)
    pre_back, pre_margins = conv_back(pair, lifted, lifted, kernel_one)
    parts = [edge_cols(pair, 0, lifted), jnp.swapaxes(pre_margins, 1, 2)]
    second_out, landed = conv_gather(pair, 0, lifted, pack_parts(parts), kernel_two, 1)
    inner_edges, pre_gathered = unpack_parts(landed, parts)
    second_sides = side_terms(side_columns(inner_edges, matching_row), kernel_two)

    second_out = at_edges(second_out, second_sides[:, 0], second_sides[:, 1])
    analysis = (base_field.astype(jnp.float32) + second_out + bias_two).astype(jnp.bfloat16)
    grad_base = cot_field.astype(jnp.float32) + return_sides(pre_back, pre_gathered, matching_row)
    return (analysis[None, None], grad_base[None, None])


def solution(mesh):
    return jax.shard_map(
        per_device,
        mesh=mesh,
        in_specs=(
            P("face", "tile", None, None, None, None),
            P(("face", "tile"), None),
            P(("face", "tile"), None),
            P(("face", "tile")),
            P(),
            P(),
            P(),
            P(),
            P(),
            P("face", "tile", None, None, None, None),
        ),
        out_specs=(
            P("face", "tile", None, None, None, None),
            P("face", "tile", None, None, None, None),
        ),
        check_vma=False,
    )
```

```python
import functools

import jax
import jax.numpy as jnp
from jax import lax
from jax.experimental import pallas as pl
from jax.experimental.pallas import tpu as pltpu
from jax.sharding import PartitionSpec as P

MESH_IDS = pl.DeviceIdType.MESH


def activation(values):
    return jax.nn.gelu(values, approximate=True)


def tap_index(band, row_tap, col_tap, backward):
    if backward:
        row = 2 - row_tap if band == 0 else row_tap
        return 3 * row + 2 - col_tap
    row = row_tap if band == 0 else 2 - row_tap
    return 3 * row + col_tap


def conv_kernel(backward, first, width, src_ref, before_ref, after_ref, side_ref, k_ref, out_ref, margin_ref):
    bands, rows, cols, cout = out_ref.shape
    pixels = rows * cols
    lanes = slice(first, first + width)
    col = lax.broadcasted_iota(jnp.int32, (rows, cols, cout), 1).reshape(pixels, cout)
    for band in range(bands):
        ext = jnp.concatenate(
            [before_ref[band, :, :, lanes], src_ref[band, :, :, lanes], after_ref[band, :, :, lanes]],
            axis=0,
        )
        lhs = jnp.concatenate(
            [ext[dy : dy + rows].reshape(pixels, width) for dy in range(3)], axis=1
        )
        stacks = []
        for col_tap in range(3):
            taps = [k_ref[tap_index(band, dy, col_tap, backward)] for dy in range(3)]
            if backward:
                stacks.append(jnp.concatenate(taps, axis=1))
            else:
                stacks.append(jnp.concatenate(taps, axis=0))

        def product(values, stack):
            if backward:
                return lax.dot_general(
                    values, stack, (((1,), (1,)), ((), ())), preferred_element_type=jnp.float32
                )
            return jnp.dot(values, stack, preferred_element_type=jnp.float32)

        z_left = product(lhs, stacks[0])
        z_mid = product(lhs, stacks[1])
        z_right = product(lhs, stacks[2])
        if backward or side_ref is None:
            left_full = jnp.zeros((pixels, cout), jnp.float32)
            right_full = left_full
        else:
            sides = side_ref[band]
            left = jnp.concatenate([sides[0, dy : dy + rows] for dy in range(3)], axis=1)
            right = jnp.concatenate([sides[1, dy : dy + rows] for dy in range(3)], axis=1)
            left_term = product(left, stacks[0])
            right_term = product(right, stacks[2])
            left_full = jnp.broadcast_to(left_term[:, None, :], (rows, cols, cout)).reshape(pixels, cout)
            right_full = jnp.broadcast_to(right_term[:, None, :], (rows, cols, cout)).reshape(pixels, cout)
        from_left = jnp.where(col == 0, left_full, pltpu.roll(z_left, 1, 0))
        from_right = jnp.where(col == cols - 1, right_full, pltpu.roll(z_right, pixels - 1, 0))
        out_ref[band] = (z_mid + from_left + from_right).reshape(rows, cols, cout)
        if backward:
            margin_ref[band, 0] = z_right.reshape(rows, cols, cout)[:, 0, :]
            margin_ref[band, 1] = z_left.reshape(rows, cols, cout)[:, cols - 1, :]


def conv_pallas(pieces, first, width, sides, kernel, backward):
    source, before, after = pieces
    bands, rows, cols, _ = source.shape
    cout = kernel.shape[1] if backward else kernel.shape[2]
    if sides is None:
        sides = jnp.zeros((bands, 2, rows + 2, width), jnp.bfloat16)
    vmem = pl.BlockSpec(memory_space=pltpu.VMEM)
    out, margins = pl.pallas_call(
        functools.partial(conv_kernel, backward, first, width),
        in_specs=[vmem] * 5,
        out_specs=[vmem, vmem],
        out_shape=[
            jax.ShapeDtypeStruct((bands, rows, cols, cout), jnp.float32),
            jax.ShapeDtypeStruct((bands, 2, rows, cout), jnp.float32),
        ],
        compiler_params=pltpu.CompilerParams(vmem_limit_bytes=60 * 1024 * 1024),
    )(source, before, after, sides, kernel)
    return out, margins


def back_kernel(src_ref, before_ref, after_ref, k_ref, *rest):
    if len(rest) == 3:
        residual_ref, out_ref, margin_ref = rest
    else:
        residual_ref = None
        out_ref, margin_ref = rest
    band = pl.program_id(0)
    _, rows, cols, cout = out_ref.shape
    width = src_ref.shape[3]
    pixels = rows * cols
    col = lax.broadcasted_iota(jnp.int32, (rows, cols, cout), 1).reshape(pixels, cout)
    ext = jnp.concatenate([before_ref[0], src_ref[0], after_ref[0]], axis=0)
    lhs = jnp.concatenate([ext[dy : dy + rows].reshape(pixels, width) for dy in range(3)], axis=1)
    products = []
    for col_tap in range(3):
        taps = [k_ref[3 * (2 - dy + band * (2 * dy - 2)) + 2 - col_tap] for dy in range(3)]
        stack = jnp.concatenate(taps, axis=1)
        products.append(
            lax.dot_general(lhs, stack, (((1,), (1,)), ((), ())), preferred_element_type=jnp.float32)
        )
    z_left, z_mid, z_right = products
    from_left = jnp.where(col == 0, 0.0, pltpu.roll(z_left, 1, 0))
    from_right = jnp.where(col == cols - 1, 0.0, pltpu.roll(z_right, pixels - 1, 0))
    total = (z_mid + from_left + from_right).reshape(rows, cols, cout)
    if residual_ref is not None:
        total = total + residual_ref[0].astype(jnp.float32)
    out_ref[0] = total
    margin_ref[0, 0] = z_right.reshape(rows, cols, cout)[:, 0, :]
    margin_ref[0, 1] = z_left.reshape(rows, cols, cout)[:, cols - 1, :]


def conv_back(pieces, first, width, kernel, residual=None):
    source, before, after = pieces
    bands, rows, cols, _ = source.shape
    cout = kernel.shape[1]
    block = first // width
    extra_specs = []
    extra_args = ()
    if residual is not None:
        extra_specs = [pl.BlockSpec((1, rows, cols, cout), lambda b: (b, 0, 0, 0))]
        extra_args = (residual,)
    return pl.pallas_call(
        back_kernel,
        grid=(bands,),
        in_specs=[
            pl.BlockSpec((1, rows, cols, width), lambda b: (b, 0, 0, block)),
            pl.BlockSpec((1, 1, cols, width), lambda b: (b, 0, 0, block)),
            pl.BlockSpec((1, 1, cols, width), lambda b: (b, 0, 0, block)),
            pl.BlockSpec(kernel.shape, lambda b: (0, 0, 0)),
        ]
        + extra_specs,
        out_specs=[
            pl.BlockSpec((1, rows, cols, cout), lambda b: (b, 0, 0, 0)),
            pl.BlockSpec((1, 2, rows, cout), lambda b: (b, 0, 0, 0)),
        ],
        out_shape=[
            jax.ShapeDtypeStruct((bands, rows, cols, cout), jnp.float32),
            jax.ShapeDtypeStruct((bands, 2, rows, cout), jnp.float32),
        ],
        compiler_params=pltpu.CompilerParams(vmem_limit_bytes=60 * 1024 * 1024),
    )(source, before, after, kernel, *extra_args)


def conv_gather_kernel(count, first, width, block_ref, src_ref, before_ref, after_ref, k_ref,
                       out_ref, gathered_ref, landed, send_sems, recv_sems):
    face = lax.axis_index("face")
    tile = lax.axis_index("tile")
    barrier = pltpu.get_barrier_semaphore()
    for step in range(1, count):
        peer = lax.rem(face + step, count)
        pl.semaphore_signal(barrier, inc=1, device_id=(peer, tile), device_id_type=MESH_IDS)
    pl.semaphore_wait(barrier, count - 1)
    copies = []
    for step in range(1, count):
        peer = lax.rem(face + step, count)
        copy = pltpu.make_async_remote_copy(
            src_ref=block_ref,
            dst_ref=landed.at[step],
            send_sem=send_sems.at[step],
            recv_sem=recv_sems.at[step],
            device_id=(peer, tile),
            device_id_type=MESH_IDS,
        )
        copy.start()
        copies.append(copy)
    gathered_ref[0] = block_ref[...]
    conv_kernel(False, first, width, src_ref, before_ref, after_ref, None, k_ref, out_ref, None)
    for copy in copies:
        copy.wait()
    for step in range(1, count):
        gathered_ref[step] = landed[step]


def conv_gather(pieces, first, width, block, kernel, gather_id):
    source, before, after = pieces
    bands, rows, cols, _ = source.shape
    cout = kernel.shape[2]
    count = lax.axis_size("face")
    block_rows, lanes = block.shape
    vmem = pl.BlockSpec(memory_space=pltpu.VMEM)
    return pl.pallas_call(
        functools.partial(conv_gather_kernel, count, first, width),
        in_specs=[vmem] * 5,
        out_specs=[vmem, vmem],
        out_shape=[
            jax.ShapeDtypeStruct((bands, rows, cols, cout), jnp.float32),
            jax.ShapeDtypeStruct((count, block_rows, lanes), block.dtype),
        ],
        scratch_shapes=[
            pltpu.VMEM((count, block_rows, lanes), block.dtype),
            pltpu.SemaphoreType.DMA((count,)),
            pltpu.SemaphoreType.DMA((count,)),
        ],
        compiler_params=pltpu.CompilerParams(
            collective_id=gather_id, has_side_effects=True, vmem_limit_bytes=60 * 1024 * 1024
        ),
    )(block, source, before, after, kernel)


def side_terms(sides, kernel):
    bands, _, ext_rows, width = sides.shape
    rows = ext_rows - 2
    terms = []
    for band in range(bands):
        per_side = []
        for side, col_tap in ((0, 0), (1, 2)):
            stacked = jnp.concatenate([sides[band, side, dy : dy + rows] for dy in range(3)], axis=1)
            weights = jnp.concatenate(
                [kernel[tap_index(band, dy, col_tap, False)] for dy in range(3)], axis=0
            )
            per_side.append(jnp.dot(stacked, weights, preferred_element_type=jnp.float32))
        terms.append(jnp.stack(per_side))
    return jnp.stack(terms)


def at_edges(field, left_add, right_add):
    cols = field.shape[2]
    col = lax.broadcasted_iota(jnp.int32, field.shape, 2)
    return field + jnp.where(col == 0, left_add[:, :, None], 0.0) + jnp.where(
        col == cols - 1, right_add[:, :, None], 0.0
    )


def extend_rows(source, last_tile):
    count = lax.axis_size("tile")
    band_rows = source.shape[1]
    head = source[:, 0:1]
    tail = source[:, band_rows - 1 : band_rows]
    before = lax.ppermute(tail, "tile", [(i, i + 1) for i in range(count - 1)])
    after = lax.ppermute(head, "tile", [(i + 1, i) for i in range(count - 1)])
    after = jnp.where(last_tile, tail[::-1], after)
    return source, before, after


def edge_cols(pieces, first, width):
    extended = jnp.concatenate([piece[..., first : first + width] for piece in (pieces[1], pieces[0], pieces[2])], axis=1)
    return jnp.stack([extended[:, :, 0], extended[:, :, -1]], axis=2)


def pick_partner(gathered, matching_row):
    picked_sides = []
    for side_number in range(2):
        partner = matching_row[side_number, 0]
        their_side = matching_row[side_number, 1]
        flipped = matching_row[side_number, 2]
        chosen = lax.dynamic_index_in_dim(gathered, partner, 0, keepdims=False)
        column = jnp.where(their_side == 0, chosen[:, :, 0], chosen[:, :, 1])
        column = jnp.where(flipped == 1, column[::-1], column)
        picked_sides.append(column)
    return picked_sides


def pack_parts(parts):
    flat = jnp.concatenate([part.astype(jnp.float32).reshape(-1) for part in parts])
    return flat.reshape(-1, 128)


def unpack_parts(landed, parts):
    face_count = lax.axis_size("face")
    face_at = lax.axis_index("face")
    landed = landed.reshape(face_count, -1)
    slot_of_face = lax.rem(face_at - lax.iota(jnp.int32, face_count) + face_count, face_count)
    gathered = jnp.take(landed, slot_of_face, axis=0)
    pieces = []
    offset = 0
    for part in parts:
        size = part.size
        piece = gathered[:, offset : offset + size].reshape((face_count,) + part.shape)
        pieces.append(piece)
        offset += size
    return pieces


def side_columns(gathered_edges, matching_row):
    left_side, right_side = pick_partner(gathered_edges, matching_row)
    return jnp.stack([left_side, right_side], axis=1).astype(jnp.bfloat16)


def add_ends(field, first_add, last_add, axis):
    length = field.shape[axis]
    head = lax.slice_in_dim(field, 0, 1, axis=axis) + jnp.expand_dims(first_add, axis)
    middle = lax.slice_in_dim(field, 1, length - 1, axis=axis)
    tail = lax.slice_in_dim(field, length - 1, length, axis=axis) + jnp.expand_dims(last_add, axis)
    return jnp.concatenate([head, middle, tail], axis=axis)


def return_sides(inside, gathered_margins, matching_row):
    left_back, right_back = pick_partner(gathered_margins, matching_row)
    return at_edges(inside, left_back, right_back)


def route_observations(obs_values, obs_dest, obs_pixel, device_count):
    obs_rows = obs_values.shape[0]
    obs_width = obs_values.shape[1]
    capacity = 2 * obs_rows // device_count
    target = obs_dest[:, 0]
    positions = lax.iota(jnp.int32, obs_rows)
    same_target = (target[:, None] == target[None, :]) & (positions[None, :] < positions[:, None])
    rank_within = jnp.sum(same_target.astype(jnp.int32), axis=1)
    slot_index = target * capacity + rank_within
    slot_ids = lax.iota(jnp.int32, device_count * capacity)
    hits = slot_ids[:, None] == slot_index[None, :]
    value_slots = jnp.dot(
        hits.astype(jnp.bfloat16), obs_values, preferred_element_type=jnp.float32
    ).astype(jnp.bfloat16)
    pixel_slots = jnp.sum(jnp.where(hits, obs_pixel[None, :], 0), axis=1)
    high = (pixel_slots // 16).astype(jnp.bfloat16).reshape(device_count, capacity)
    low = (pixel_slots % 16).astype(jnp.bfloat16).reshape(device_count, capacity)
    pixel_row = jnp.concatenate(
        [high, low, jnp.zeros((device_count, obs_width - 2 * capacity), jnp.bfloat16)], axis=1
    )
    payload = jnp.concatenate(
        [value_slots.reshape(device_count, capacity, obs_width), pixel_row[:, None]], axis=1
    )
    arrived = lax.all_to_all(payload, ("face", "tile"), split_axis=0, concat_axis=0, tiled=True)
    got_values = arrived[:, :capacity].reshape(-1, obs_width)
    got_high = arrived[:, capacity, 0:capacity].astype(jnp.int32)
    got_low = arrived[:, capacity, capacity : 2 * capacity].astype(jnp.int32)
    got_pixels = (got_high * 16 + got_low).reshape(-1)
    return got_values, got_pixels


def per_device(
    state,
    obs_values,
    obs_dest,
    obs_pixel,
    matching,
    kernel_one,
    bias_one,
    kernel_two,
    bias_two,
    cotangent,
):
    base_field = state[0, 0]
    cot_field = cotangent[0, 0]
    band_rows = base_field.shape[1]
    column_count = base_field.shape[2]
    channels = base_field.shape[3]
    tile_count = lax.axis_size("tile")
    face_count = lax.axis_size("face")
    tile_at = lax.axis_index("tile")
    face_at = lax.axis_index("face")
    device_count = tile_count * face_count
    obs_width = obs_values.shape[1]

    got_values, got_pixels = route_observations(obs_values, obs_dest, obs_pixel, device_count)
    pixel_count = 2 * band_rows * column_count
    pixel_ids = lax.iota(jnp.int32, pixel_count)
    onehot = (pixel_ids[:, None] == got_pixels[None, :]).astype(jnp.bfloat16)
    gridded = jnp.dot(onehot, got_values, preferred_element_type=jnp.float32)
    gridded = gridded.reshape(2, band_rows, column_count, obs_width)

    last_tile = tile_at == tile_count - 1
    matching_row = lax.dynamic_index_in_dim(matching, face_at, 0, keepdims=False)

    lifted = kernel_one.shape[2]
    both = extend_rows(jnp.concatenate([base_field, cot_field], axis=3), last_tile)
    cot_back, cot_margins = conv_back(both, channels, channels, kernel_two)
    parts = [edge_cols(both, 0, channels), jnp.swapaxes(cot_margins, 1, 2)]
    first_out, landed = conv_gather(both, 0, channels, pack_parts(parts), kernel_one, 0)
    base_edges, cot_gathered = unpack_parts(landed, parts)
    first_sides = side_terms(side_columns(base_edges, matching_row), kernel_one)

    pre_act = at_edges(first_out, first_sides[:, 0], first_sides[:, 1]) + bias_one + gridded
    inner = activation(pre_act).astype(jnp.bfloat16)
    grad_inner = return_sides(cot_back, cot_gathered, matching_row)
    grad_pre = jax.vjp(activation, pre_act)[1](grad_inner)[0].astype(jnp.bfloat16)

    pair = extend_rows(jnp.concatenate([inner, grad_pre], axis=3), last_tile)
    pre_back, pre_margins = conv_back(pair, lifted, lifted, kernel_one, cot_field)
    parts = [edge_cols(pair, 0, lifted), jnp.swapaxes(pre_margins, 1, 2)]
    second_out, landed = conv_gather(pair, 0, lifted, pack_parts(parts), kernel_two, 1)
    inner_edges, pre_gathered = unpack_parts(landed, parts)
    second_sides = side_terms(side_columns(inner_edges, matching_row), kernel_two)

    second_out = at_edges(second_out, second_sides[:, 0], second_sides[:, 1])
    analysis = (base_field.astype(jnp.float32) + second_out + bias_two).astype(jnp.bfloat16)
    left_back, right_back = pick_partner(pre_gathered, matching_row)
    last_col = column_count - 1
    grad_base = lax.dynamic_update_slice(
        pre_back, pre_back[:, :, 0:1] + left_back[:, :, None], (0, 0, 0, 0)
    )
    grad_base = lax.dynamic_update_slice(
        grad_base, pre_back[:, :, last_col:] + right_back[:, :, None], (0, 0, last_col, 0)
    )
    return (analysis[None, None], grad_base[None, None])


def solution(mesh):
    return jax.shard_map(
        per_device,
        mesh=mesh,
        in_specs=(
            P("face", "tile", None, None, None, None),
            P(("face", "tile"), None),
            P(("face", "tile"), None),
            P(("face", "tile")),
            P(),
            P(),
            P(),
            P(),
            P(),
            P("face", "tile", None, None, None, None),
        ),
        out_specs=(
            P("face", "tile", None, None, None, None),
            P("face", "tile", None, None, None, None),
        ),
        check_vma=False,
    )
```

```python
import functools

import jax
import jax.numpy as jnp
from jax import lax
from jax.experimental import pallas as pl
from jax.experimental.pallas import tpu as pltpu
from jax.sharding import PartitionSpec as P

MESH_IDS = pl.DeviceIdType.MESH


def activation(values):
    return jax.nn.gelu(values, approximate=True)


def tap_index(band, row_tap, col_tap, backward):
    if backward:
        row = 2 - row_tap if band == 0 else row_tap
        return 3 * row + 2 - col_tap
    row = row_tap if band == 0 else 2 - row_tap
    return 3 * row + col_tap


def conv_kernel(backward, first, width, src_ref, before_ref, after_ref, side_ref, k_ref, out_ref, margin_ref):
    bands, rows, cols, cout = out_ref.shape
    pixels = rows * cols
    lanes = slice(first, first + width)
    col = lax.broadcasted_iota(jnp.int32, (rows, cols, cout), 1).reshape(pixels, cout)
    for band in range(bands):
        ext = jnp.concatenate(
            [before_ref[band, :, :, lanes], src_ref[band, :, :, lanes], after_ref[band, :, :, lanes]],
            axis=0,
        )
        lhs = jnp.concatenate(
            [ext[dy : dy + rows].reshape(pixels, width) for dy in range(3)], axis=1
        )
        stacks = []
        for col_tap in range(3):
            taps = [k_ref[tap_index(band, dy, col_tap, backward)] for dy in range(3)]
            if backward:
                stacks.append(jnp.concatenate(taps, axis=1))
            else:
                stacks.append(jnp.concatenate(taps, axis=0))

        def product(values, stack):
            if backward:
                return lax.dot_general(
                    values, stack, (((1,), (1,)), ((), ())), preferred_element_type=jnp.float32
                )
            return jnp.dot(values, stack, preferred_element_type=jnp.float32)

        z_left = product(lhs, stacks[0])
        z_mid = product(lhs, stacks[1])
        z_right = product(lhs, stacks[2])
        if backward or side_ref is None:
            left_full = jnp.zeros((pixels, cout), jnp.float32)
            right_full = left_full
        else:
            sides = side_ref[band]
            left = jnp.concatenate([sides[0, dy : dy + rows] for dy in range(3)], axis=1)
            right = jnp.concatenate([sides[1, dy : dy + rows] for dy in range(3)], axis=1)
            left_term = product(left, stacks[0])
            right_term = product(right, stacks[2])
            left_full = jnp.broadcast_to(left_term[:, None, :], (rows, cols, cout)).reshape(pixels, cout)
            right_full = jnp.broadcast_to(right_term[:, None, :], (rows, cols, cout)).reshape(pixels, cout)
        from_left = jnp.where(col == 0, left_full, pltpu.roll(z_left, 1, 0))
        from_right = jnp.where(col == cols - 1, right_full, pltpu.roll(z_right, pixels - 1, 0))
        out_ref[band] = (z_mid + from_left + from_right).reshape(rows, cols, cout)
        if backward:
            margin_ref[band, 0] = z_right.reshape(rows, cols, cout)[:, 0, :]
            margin_ref[band, 1] = z_left.reshape(rows, cols, cout)[:, cols - 1, :]


def conv_pallas(pieces, first, width, sides, kernel, backward):
    source, before, after = pieces
    bands, rows, cols, _ = source.shape
    cout = kernel.shape[1] if backward else kernel.shape[2]
    if sides is None:
        sides = jnp.zeros((bands, 2, rows + 2, width), jnp.bfloat16)
    vmem = pl.BlockSpec(memory_space=pltpu.VMEM)
    out, margins = pl.pallas_call(
        functools.partial(conv_kernel, backward, first, width),
        in_specs=[vmem] * 5,
        out_specs=[vmem, vmem],
        out_shape=[
            jax.ShapeDtypeStruct((bands, rows, cols, cout), jnp.float32),
            jax.ShapeDtypeStruct((bands, 2, rows, cout), jnp.float32),
        ],
        compiler_params=pltpu.CompilerParams(vmem_limit_bytes=60 * 1024 * 1024),
    )(source, before, after, sides, kernel)
    return out, margins


def back_kernel(src_ref, before_ref, after_ref, k_ref, out_ref, margin_ref):
    band = pl.program_id(0)
    _, rows, cols, cout = out_ref.shape
    width = src_ref.shape[3]
    pixels = rows * cols
    col = lax.broadcasted_iota(jnp.int32, (rows, cols, cout), 1).reshape(pixels, cout)
    ext = jnp.concatenate([before_ref[0], src_ref[0], after_ref[0]], axis=0)
    lhs = jnp.concatenate([ext[dy : dy + rows].reshape(pixels, width) for dy in range(3)], axis=1)
    products = []
    for col_tap in range(3):
        taps = [k_ref[3 * (2 - dy + band * (2 * dy - 2)) + 2 - col_tap] for dy in range(3)]
        stack = jnp.concatenate(taps, axis=1)
        products.append(
            lax.dot_general(lhs, stack, (((1,), (1,)), ((), ())), preferred_element_type=jnp.float32)
        )
    z_left, z_mid, z_right = products
    from_left = jnp.where(col == 0, 0.0, pltpu.roll(z_left, 1, 0))
    from_right = jnp.where(col == cols - 1, 0.0, pltpu.roll(z_right, pixels - 1, 0))
    out_ref[0] = (z_mid + from_left + from_right).reshape(rows, cols, cout)
    margin_ref[0, 0] = z_right.reshape(rows, cols, cout)[:, 0, :]
    margin_ref[0, 1] = z_left.reshape(rows, cols, cout)[:, cols - 1, :]


def conv_back(pieces, first, width, kernel):
    source, before, after = pieces
    bands, rows, cols, _ = source.shape
    cout = kernel.shape[1]
    block = first // width
    return pl.pallas_call(
        back_kernel,
        grid=(bands,),
        in_specs=[
            pl.BlockSpec((1, rows, cols, width), lambda b: (b, 0, 0, block)),
            pl.BlockSpec((1, 1, cols, width), lambda b: (b, 0, 0, block)),
            pl.BlockSpec((1, 1, cols, width), lambda b: (b, 0, 0, block)),
            pl.BlockSpec(kernel.shape, lambda b: (0, 0, 0)),
        ],
        out_specs=[
            pl.BlockSpec((1, rows, cols, cout), lambda b: (b, 0, 0, 0)),
            pl.BlockSpec((1, 2, rows, cout), lambda b: (b, 0, 0, 0)),
        ],
        out_shape=[
            jax.ShapeDtypeStruct((bands, rows, cols, cout), jnp.float32),
            jax.ShapeDtypeStruct((bands, 2, rows, cout), jnp.float32),
        ],
        compiler_params=pltpu.CompilerParams(vmem_limit_bytes=60 * 1024 * 1024),
    )(source, before, after, kernel)


def conv_gather_kernel(count, block_ref, src_ref, before_ref, after_ref, k_ref,
                       out_ref, gathered_ref, landed, send_sems, recv_sems):
    step_at = pl.program_id(0)
    face = lax.axis_index("face")
    tile = lax.axis_index("tile")
    copies = []
    for step in range(1, count):
        peer = lax.rem(face + step, count)
        copies.append(
            pltpu.make_async_remote_copy(
                src_ref=block_ref,
                dst_ref=landed.at[step],
                send_sem=send_sems.at[step],
                recv_sem=recv_sems.at[step],
                device_id=(peer, tile),
                device_id_type=MESH_IDS,
            )
        )

    @pl.when(step_at == 0)
    def _():
        barrier = pltpu.get_barrier_semaphore()
        for step in range(1, count):
            peer = lax.rem(face + step, count)
            pl.semaphore_signal(barrier, inc=1, device_id=(peer, tile), device_id_type=MESH_IDS)
        pl.semaphore_wait(barrier, count - 1)
        for copy in copies:
            copy.start()
        gathered_ref[0] = block_ref[...]

    _, rows, cols, cout = out_ref.shape
    width = src_ref.shape[3]
    pixels = rows * cols
    col = lax.broadcasted_iota(jnp.int32, (rows, cols, cout), 1).reshape(pixels, cout)
    ext = jnp.concatenate([before_ref[0], src_ref[0], after_ref[0]], axis=0)
    lhs = jnp.concatenate([ext[dy : dy + rows].reshape(pixels, width) for dy in range(3)], axis=1)
    products = []
    for col_tap in range(3):
        taps = [k_ref[3 * (dy + step_at * (2 - 2 * dy)) + col_tap] for dy in range(3)]
        stack = jnp.concatenate(taps, axis=0)
        products.append(jnp.dot(lhs, stack, preferred_element_type=jnp.float32))
    z_left, z_mid, z_right = products
    from_left = jnp.where(col == 0, 0.0, pltpu.roll(z_left, 1, 0))
    from_right = jnp.where(col == cols - 1, 0.0, pltpu.roll(z_right, pixels - 1, 0))
    out_ref[0] = (z_mid + from_left + from_right).reshape(rows, cols, cout)

    @pl.when(step_at == pl.num_programs(0) - 1)
    def _():
        for copy in copies:
            copy.wait()
        for step in range(1, count):
            gathered_ref[step] = landed[step]


def conv_gather(pieces, first, width, block, kernel, gather_id):
    source, before, after = pieces
    bands, rows, cols, _ = source.shape
    cout = kernel.shape[2]
    count = lax.axis_size("face")
    block_rows, lanes = block.shape
    lane_block = first // width
    return pl.pallas_call(
        functools.partial(conv_gather_kernel, count),
        grid=(bands,),
        in_specs=[
            pl.BlockSpec((block_rows, lanes), lambda b: (0, 0)),
            pl.BlockSpec((1, rows, cols, width), lambda b: (b, 0, 0, lane_block)),
            pl.BlockSpec((1, 1, cols, width), lambda b: (b, 0, 0, lane_block)),
            pl.BlockSpec((1, 1, cols, width), lambda b: (b, 0, 0, lane_block)),
            pl.BlockSpec(kernel.shape, lambda b: (0, 0, 0)),
        ],
        out_specs=[
            pl.BlockSpec((1, rows, cols, cout), lambda b: (b, 0, 0, 0)),
            pl.BlockSpec((count, block_rows, lanes), lambda b: (0, 0, 0)),
        ],
        out_shape=[
            jax.ShapeDtypeStruct((bands, rows, cols, cout), jnp.float32),
            jax.ShapeDtypeStruct((count, block_rows, lanes), block.dtype),
        ],
        scratch_shapes=[
            pltpu.VMEM((count, block_rows, lanes), block.dtype),
            pltpu.SemaphoreType.DMA((count,)),
            pltpu.SemaphoreType.DMA((count,)),
        ],
        compiler_params=pltpu.CompilerParams(
            collective_id=gather_id, has_side_effects=True, vmem_limit_bytes=60 * 1024 * 1024
        ),
    )(block, source, before, after, kernel)


def side_terms(sides, kernel):
    bands, _, ext_rows, width = sides.shape
    rows = ext_rows - 2
    terms = []
    for band in range(bands):
        per_side = []
        for side, col_tap in ((0, 0), (1, 2)):
            stacked = jnp.concatenate([sides[band, side, dy : dy + rows] for dy in range(3)], axis=1)
            weights = jnp.concatenate(
                [kernel[tap_index(band, dy, col_tap, False)] for dy in range(3)], axis=0
            )
            per_side.append(jnp.dot(stacked, weights, preferred_element_type=jnp.float32))
        terms.append(jnp.stack(per_side))
    return jnp.stack(terms)


def at_edges(field, left_add, right_add):
    cols = field.shape[2]
    col = lax.broadcasted_iota(jnp.int32, field.shape, 2)
    return field + jnp.where(col == 0, left_add[:, :, None], 0.0) + jnp.where(
        col == cols - 1, right_add[:, :, None], 0.0
    )


def extend_rows(source, last_tile):
    count = lax.axis_size("tile")
    band_rows = source.shape[1]
    head = source[:, 0:1]
    tail = source[:, band_rows - 1 : band_rows]
    before = lax.ppermute(tail, "tile", [(i, i + 1) for i in range(count - 1)])
    after = lax.ppermute(head, "tile", [(i + 1, i) for i in range(count - 1)])
    after = jnp.where(last_tile, tail[::-1], after)
    return source, before, after


def edge_cols(pieces, first, width):
    extended = jnp.concatenate([piece[..., first : first + width] for piece in (pieces[1], pieces[0], pieces[2])], axis=1)
    return jnp.stack([extended[:, :, 0], extended[:, :, -1]], axis=2)


def pick_partner(gathered, matching_row):
    picked_sides = []
    for side_number in range(2):
        partner = matching_row[side_number, 0]
        their_side = matching_row[side_number, 1]
        flipped = matching_row[side_number, 2]
        chosen = lax.dynamic_index_in_dim(gathered, partner, 0, keepdims=False)
        column = jnp.where(their_side == 0, chosen[:, :, 0], chosen[:, :, 1])
        column = jnp.where(flipped == 1, column[::-1], column)
        picked_sides.append(column)
    return picked_sides


def pack_parts(parts):
    flat = jnp.concatenate([part.astype(jnp.float32).reshape(-1) for part in parts])
    return flat.reshape(-1, 128)


def unpack_parts(landed, parts):
    face_count = lax.axis_size("face")
    face_at = lax.axis_index("face")
    landed = landed.reshape(face_count, -1)
    slot_of_face = lax.rem(face_at - lax.iota(jnp.int32, face_count) + face_count, face_count)
    gathered = jnp.take(landed, slot_of_face, axis=0)
    pieces = []
    offset = 0
    for part in parts:
        size = part.size
        piece = gathered[:, offset : offset + size].reshape((face_count,) + part.shape)
        pieces.append(piece)
        offset += size
    return pieces


def side_columns(gathered_edges, matching_row):
    left_side, right_side = pick_partner(gathered_edges, matching_row)
    return jnp.stack([left_side, right_side], axis=1).astype(jnp.bfloat16)


def add_ends(field, first_add, last_add, axis):
    length = field.shape[axis]
    head = lax.slice_in_dim(field, 0, 1, axis=axis) + jnp.expand_dims(first_add, axis)
    middle = lax.slice_in_dim(field, 1, length - 1, axis=axis)
    tail = lax.slice_in_dim(field, length - 1, length, axis=axis) + jnp.expand_dims(last_add, axis)
    return jnp.concatenate([head, middle, tail], axis=axis)


def return_sides(inside, gathered_margins, matching_row):
    left_back, right_back = pick_partner(gathered_margins, matching_row)
    return at_edges(inside, left_back, right_back)


def route_observations(obs_values, obs_dest, obs_pixel, device_count):
    obs_rows = obs_values.shape[0]
    obs_width = obs_values.shape[1]
    capacity = 2 * obs_rows // device_count
    target = obs_dest[:, 0]
    positions = lax.iota(jnp.int32, obs_rows)
    same_target = (target[:, None] == target[None, :]) & (positions[None, :] < positions[:, None])
    rank_within = jnp.sum(same_target.astype(jnp.int32), axis=1)
    slot_index = target * capacity + rank_within
    slot_ids = lax.iota(jnp.int32, device_count * capacity)
    hits = slot_ids[:, None] == slot_index[None, :]
    value_slots = jnp.dot(
        hits.astype(jnp.bfloat16), obs_values, preferred_element_type=jnp.float32
    ).astype(jnp.bfloat16)
    pixel_slots = jnp.sum(jnp.where(hits, obs_pixel[None, :], 0), axis=1)
    high = (pixel_slots // 16).astype(jnp.bfloat16).reshape(device_count, capacity)
    low = (pixel_slots % 16).astype(jnp.bfloat16).reshape(device_count, capacity)
    pixel_row = jnp.concatenate(
        [high, low, jnp.zeros((device_count, obs_width - 2 * capacity), jnp.bfloat16)], axis=1
    )
    payload = jnp.concatenate(
        [value_slots.reshape(device_count, capacity, obs_width), pixel_row[:, None]], axis=1
    )
    arrived = lax.all_to_all(payload, ("face", "tile"), split_axis=0, concat_axis=0, tiled=True)
    got_values = arrived[:, :capacity].reshape(-1, obs_width)
    got_high = arrived[:, capacity, 0:capacity].astype(jnp.int32)
    got_low = arrived[:, capacity, capacity : 2 * capacity].astype(jnp.int32)
    got_pixels = (got_high * 16 + got_low).reshape(-1)
    return got_values, got_pixels


def per_device(
    state,
    obs_values,
    obs_dest,
    obs_pixel,
    matching,
    kernel_one,
    bias_one,
    kernel_two,
    bias_two,
    cotangent,
):
    base_field = state[0, 0]
    cot_field = cotangent[0, 0]
    band_rows = base_field.shape[1]
    column_count = base_field.shape[2]
    channels = base_field.shape[3]
    tile_count = lax.axis_size("tile")
    face_count = lax.axis_size("face")
    tile_at = lax.axis_index("tile")
    face_at = lax.axis_index("face")
    device_count = tile_count * face_count
    obs_width = obs_values.shape[1]

    got_values, got_pixels = route_observations(obs_values, obs_dest, obs_pixel, device_count)
    pixel_count = 2 * band_rows * column_count
    pixel_ids = lax.iota(jnp.int32, pixel_count)
    onehot = (pixel_ids[:, None] == got_pixels[None, :]).astype(jnp.bfloat16)
    gridded = jnp.dot(onehot, got_values, preferred_element_type=jnp.float32)
    gridded = gridded.reshape(2, band_rows, column_count, obs_width)

    last_tile = tile_at == tile_count - 1
    matching_row = lax.dynamic_index_in_dim(matching, face_at, 0, keepdims=False)

    lifted = kernel_one.shape[2]
    both = extend_rows(jnp.concatenate([base_field, cot_field], axis=3), last_tile)
    cot_back, cot_margins = conv_back(both, channels, channels, kernel_two)
    parts = [edge_cols(both, 0, channels), jnp.swapaxes(cot_margins, 1, 2)]
    first_out, landed = conv_gather(both, 0, channels, pack_parts(parts), kernel_one, 0)
    base_edges, cot_gathered = unpack_parts(landed, parts)
    first_sides = side_terms(side_columns(base_edges, matching_row), kernel_one)

    pre_act = at_edges(first_out, first_sides[:, 0], first_sides[:, 1]) + bias_one + gridded
    inner = activation(pre_act).astype(jnp.bfloat16)
    grad_inner = return_sides(cot_back, cot_gathered, matching_row)
    grad_pre = jax.vjp(activation, pre_act)[1](grad_inner)[0].astype(jnp.bfloat16)

    pair = extend_rows(jnp.concatenate([inner, grad_pre], axis=3), last_tile)
    pre_back, pre_margins = conv_back(pair, lifted, lifted, kernel_one)
    parts = [edge_cols(pair, 0, lifted), jnp.swapaxes(pre_margins, 1, 2)]
    second_out, landed = conv_gather(pair, 0, lifted, pack_parts(parts), kernel_two, 1)
    inner_edges, pre_gathered = unpack_parts(landed, parts)
    second_sides = side_terms(side_columns(inner_edges, matching_row), kernel_two)

    second_out = at_edges(second_out, second_sides[:, 0], second_sides[:, 1])
    analysis = (base_field.astype(jnp.float32) + second_out + bias_two).astype(jnp.bfloat16)
    grad_base = cot_field.astype(jnp.float32) + return_sides(pre_back, pre_gathered, matching_row)
    return (analysis[None, None], grad_base[None, None])


def solution(mesh):
    return jax.shard_map(
        per_device,
        mesh=mesh,
        in_specs=(
            P("face", "tile", None, None, None, None),
            P(("face", "tile"), None),
            P(("face", "tile"), None),
            P(("face", "tile")),
            P(),
            P(),
            P(),
            P(),
            P(),
            P("face", "tile", None, None, None, None),
        ),
        out_specs=(
            P("face", "tile", None, None, None, None),
            P("face", "tile", None, None, None, None),
        ),
        check_vma=False,
    )
```

```python
import functools

import jax
import jax.numpy as jnp
from jax import lax
from jax.experimental import pallas as pl
from jax.experimental.pallas import tpu as pltpu
from jax.sharding import PartitionSpec as P

MESH_IDS = pl.DeviceIdType.MESH


def activation(values):
    return jax.nn.gelu(values, approximate=True)


def tap_index(band, row_tap, col_tap, backward):
    if backward:
        row = 2 - row_tap if band == 0 else row_tap
        return 3 * row + 2 - col_tap
    row = row_tap if band == 0 else 2 - row_tap
    return 3 * row + col_tap


def conv_kernel(backward, first, width, src_ref, before_ref, after_ref, side_ref, k_ref, out_ref, margin_ref):
    bands, rows, cols, cout = out_ref.shape
    pixels = rows * cols
    lanes = slice(first, first + width)
    col = lax.broadcasted_iota(jnp.int32, (rows, cols, cout), 1).reshape(pixels, cout)
    for band in range(bands):
        ext = jnp.concatenate(
            [before_ref[band, :, :, lanes], src_ref[band, :, :, lanes], after_ref[band, :, :, lanes]],
            axis=0,
        )
        lhs = jnp.concatenate(
            [ext[dy : dy + rows].reshape(pixels, width) for dy in range(3)], axis=1
        )
        stacks = []
        for col_tap in range(3):
            taps = [k_ref[tap_index(band, dy, col_tap, backward)] for dy in range(3)]
            if backward:
                stacks.append(jnp.concatenate(taps, axis=1))
            else:
                stacks.append(jnp.concatenate(taps, axis=0))

        def product(values, stack):
            if backward:
                return lax.dot_general(
                    values, stack, (((1,), (1,)), ((), ())), preferred_element_type=jnp.float32
                )
            return jnp.dot(values, stack, preferred_element_type=jnp.float32)

        z_left = product(lhs, stacks[0])
        z_mid = product(lhs, stacks[1])
        z_right = product(lhs, stacks[2])
        if backward or side_ref is None:
            left_full = jnp.zeros((pixels, cout), jnp.float32)
            right_full = left_full
        else:
            sides = side_ref[band]
            left = jnp.concatenate([sides[0, dy : dy + rows] for dy in range(3)], axis=1)
            right = jnp.concatenate([sides[1, dy : dy + rows] for dy in range(3)], axis=1)
            left_term = product(left, stacks[0])
            right_term = product(right, stacks[2])
            left_full = jnp.broadcast_to(left_term[:, None, :], (rows, cols, cout)).reshape(pixels, cout)
            right_full = jnp.broadcast_to(right_term[:, None, :], (rows, cols, cout)).reshape(pixels, cout)
        from_left = jnp.where(col == 0, left_full, pltpu.roll(z_left, 1, 0))
        from_right = jnp.where(col == cols - 1, right_full, pltpu.roll(z_right, pixels - 1, 0))
        out_ref[band] = (z_mid + from_left + from_right).reshape(rows, cols, cout)
        if backward:
            margin_ref[band, 0] = z_right.reshape(rows, cols, cout)[:, 0, :]
            margin_ref[band, 1] = z_left.reshape(rows, cols, cout)[:, cols - 1, :]


def conv_pallas(pieces, first, width, sides, kernel, backward):
    source, before, after = pieces
    bands, rows, cols, _ = source.shape
    cout = kernel.shape[1] if backward else kernel.shape[2]
    if sides is None:
        sides = jnp.zeros((bands, 2, rows + 2, width), jnp.bfloat16)
    vmem = pl.BlockSpec(memory_space=pltpu.VMEM)
    out, margins = pl.pallas_call(
        functools.partial(conv_kernel, backward, first, width),
        in_specs=[vmem] * 5,
        out_specs=[vmem, vmem],
        out_shape=[
            jax.ShapeDtypeStruct((bands, rows, cols, cout), jnp.float32),
            jax.ShapeDtypeStruct((bands, 2, rows, cout), jnp.float32),
        ],
        compiler_params=pltpu.CompilerParams(vmem_limit_bytes=60 * 1024 * 1024),
    )(source, before, after, sides, kernel)
    return out, margins


def back_kernel(src_ref, before_ref, after_ref, k_ref, out_ref, margin_ref):
    band = pl.program_id(0)
    _, rows, cols, cout = out_ref.shape
    width = src_ref.shape[3]
    pixels = rows * cols
    col = lax.broadcasted_iota(jnp.int32, (rows, cols, cout), 1).reshape(pixels, cout)
    ext = jnp.concatenate([before_ref[0], src_ref[0], after_ref[0]], axis=0)
    lhs = jnp.concatenate([ext[dy : dy + rows].reshape(pixels, width) for dy in range(3)], axis=1)
    products = []
    for col_tap in range(3):
        taps = [k_ref[3 * (2 - dy + band * (2 * dy - 2)) + 2 - col_tap] for dy in range(3)]
        stack = jnp.concatenate(taps, axis=1)
        products.append(
            lax.dot_general(lhs, stack, (((1,), (1,)), ((), ())), preferred_element_type=jnp.float32)
        )
    z_left, z_mid, z_right = products
    from_left = jnp.where(col == 0, 0.0, pltpu.roll(z_left, 1, 0))
    from_right = jnp.where(col == cols - 1, 0.0, pltpu.roll(z_right, pixels - 1, 0))
    out_ref[0] = (z_mid + from_left + from_right).reshape(rows, cols, cout)
    margin_ref[0, 0] = z_right.reshape(rows, cols, cout)[:, 0, :]
    margin_ref[0, 1] = z_left.reshape(rows, cols, cout)[:, cols - 1, :]


def conv_back(pieces, first, width, kernel):
    source, before, after = pieces
    bands, rows, cols, _ = source.shape
    cout = kernel.shape[1]
    block = first // width
    return pl.pallas_call(
        back_kernel,
        grid=(bands,),
        in_specs=[
            pl.BlockSpec((1, rows, cols, width), lambda b: (b, 0, 0, block)),
            pl.BlockSpec((1, 1, cols, width), lambda b: (b, 0, 0, block)),
            pl.BlockSpec((1, 1, cols, width), lambda b: (b, 0, 0, block)),
            pl.BlockSpec(kernel.shape, lambda b: (0, 0, 0)),
        ],
        out_specs=[
            pl.BlockSpec((1, rows, cols, cout), lambda b: (b, 0, 0, 0)),
            pl.BlockSpec((1, 2, rows, cout), lambda b: (b, 0, 0, 0)),
        ],
        out_shape=[
            jax.ShapeDtypeStruct((bands, rows, cols, cout), jnp.float32),
            jax.ShapeDtypeStruct((bands, 2, rows, cout), jnp.float32),
        ],
        compiler_params=pltpu.CompilerParams(vmem_limit_bytes=60 * 1024 * 1024),
    )(source, before, after, kernel)


def conv_gather_kernel(count, block_ref, src_ref, before_ref, after_ref, k_ref,
                       out_ref, gathered_ref, landed, send_sems, recv_sems):
    step_at = pl.program_id(0)
    face = lax.axis_index("face")
    tile = lax.axis_index("tile")
    copies = []
    for step in range(1, count):
        peer = lax.rem(face + step, count)
        copies.append(
            pltpu.make_async_remote_copy(
                src_ref=block_ref,
                dst_ref=landed.at[step],
                send_sem=send_sems.at[step],
                recv_sem=recv_sems.at[step],
                device_id=(peer, tile),
                device_id_type=MESH_IDS,
            )
        )

    @pl.when(step_at == 0)
    def _():
        barrier = pltpu.get_barrier_semaphore()
        for step in range(1, count):
            peer = lax.rem(face + step, count)
            pl.semaphore_signal(barrier, inc=1, device_id=(peer, tile), device_id_type=MESH_IDS)
        pl.semaphore_wait(barrier, count - 1)
        for copy in copies:
            copy.start()
        gathered_ref[0] = block_ref[...]

    _, rows, cols, cout = out_ref.shape
    width = src_ref.shape[3]
    pixels = rows * cols
    col = lax.broadcasted_iota(jnp.int32, (rows, cols, cout), 1).reshape(pixels, cout)
    ext = jnp.concatenate([before_ref[0], src_ref[0], after_ref[0]], axis=0)
    lhs = jnp.concatenate([ext[dy : dy + rows].reshape(pixels, width) for dy in range(3)], axis=1)
    products = []
    for col_tap in range(3):
        taps = [k_ref[3 * (dy + step_at * (2 - 2 * dy)) + col_tap] for dy in range(3)]
        stack = jnp.concatenate(taps, axis=0)
        products.append(jnp.dot(lhs, stack, preferred_element_type=jnp.float32))
    z_left, z_mid, z_right = products
    from_left = jnp.where(col == 0, 0.0, pltpu.roll(z_left, 1, 0))
    from_right = jnp.where(col == cols - 1, 0.0, pltpu.roll(z_right, pixels - 1, 0))
    out_ref[0] = (z_mid + from_left + from_right).reshape(rows, cols, cout)

    @pl.when(step_at == pl.num_programs(0) - 1)
    def _():
        for copy in copies:
            copy.wait()
        for step in range(1, count):
            gathered_ref[step] = landed[step]


def conv_gather(pieces, first, width, block, kernel, gather_id):
    source, before, after = pieces
    bands, rows, cols, _ = source.shape
    cout = kernel.shape[2]
    count = lax.axis_size("face")
    block_rows, lanes = block.shape
    lane_block = first // width
    return pl.pallas_call(
        functools.partial(conv_gather_kernel, count),
        grid=(bands,),
        in_specs=[
            pl.BlockSpec((block_rows, lanes), lambda b: (0, 0)),
            pl.BlockSpec((1, rows, cols, width), lambda b: (b, 0, 0, lane_block)),
            pl.BlockSpec((1, 1, cols, width), lambda b: (b, 0, 0, lane_block)),
            pl.BlockSpec((1, 1, cols, width), lambda b: (b, 0, 0, lane_block)),
            pl.BlockSpec(kernel.shape, lambda b: (0, 0, 0)),
        ],
        out_specs=[
            pl.BlockSpec((1, rows, cols, cout), lambda b: (b, 0, 0, 0)),
            pl.BlockSpec((count, block_rows, lanes), lambda b: (0, 0, 0)),
        ],
        out_shape=[
            jax.ShapeDtypeStruct((bands, rows, cols, cout), jnp.float32),
            jax.ShapeDtypeStruct((count, block_rows, lanes), block.dtype),
        ],
        scratch_shapes=[
            pltpu.VMEM((count, block_rows, lanes), block.dtype),
            pltpu.SemaphoreType.DMA((count,)),
            pltpu.SemaphoreType.DMA((count,)),
        ],
        compiler_params=pltpu.CompilerParams(
            collective_id=gather_id, has_side_effects=True, vmem_limit_bytes=60 * 1024 * 1024
        ),
    )(block, source, before, after, kernel)


def side_terms(sides, kernel):
    bands, _, ext_rows, width = sides.shape
    rows = ext_rows - 2
    terms = []
    for band in range(bands):
        per_side = []
        for side, col_tap in ((0, 0), (1, 2)):
            stacked = jnp.concatenate([sides[band, side, dy : dy + rows] for dy in range(3)], axis=1)
            weights = jnp.concatenate(
                [kernel[tap_index(band, dy, col_tap, False)] for dy in range(3)], axis=0
            )
            per_side.append(jnp.dot(stacked, weights, preferred_element_type=jnp.float32))
        terms.append(jnp.stack(per_side))
    return jnp.stack(terms)


def at_edges(field, left_add, right_add):
    cols = field.shape[2]
    col = lax.broadcasted_iota(jnp.int32, field.shape, 2)
    return field + jnp.where(col == 0, left_add[:, :, None], 0.0) + jnp.where(
        col == cols - 1, right_add[:, :, None], 0.0
    )


def extend_rows(source, last_tile):
    count = lax.axis_size("tile")
    band_rows = source.shape[1]
    head = source[:, 0:1]
    tail = source[:, band_rows - 1 : band_rows]
    before = lax.ppermute(tail, "tile", [(i, i + 1) for i in range(count - 1)])
    after = lax.ppermute(head, "tile", [(i + 1, i) for i in range(count - 1)])
    after = jnp.where(last_tile, tail[::-1], after)
    return source, before, after


def edge_cols(pieces, first, width):
    extended = jnp.concatenate([piece[..., first : first + width] for piece in (pieces[1], pieces[0], pieces[2])], axis=1)
    return jnp.stack([extended[:, :, 0], extended[:, :, -1]], axis=2)


def pick_partner(gathered, matching_row):
    picked_sides = []
    for side_number in range(2):
        partner = matching_row[side_number, 0]
        their_side = matching_row[side_number, 1]
        flipped = matching_row[side_number, 2]
        chosen = lax.dynamic_index_in_dim(gathered, partner, 0, keepdims=False)
        column = jnp.where(their_side == 0, chosen[:, :, 0], chosen[:, :, 1])
        column = jnp.where(flipped == 1, column[::-1], column)
        picked_sides.append(column)
    return picked_sides


def pack_parts(parts):
    flat = jnp.concatenate([part.astype(jnp.float32).reshape(-1) for part in parts])
    return flat.reshape(-1, 128)


def unpack_parts(landed, parts):
    face_count = lax.axis_size("face")
    face_at = lax.axis_index("face")
    landed = landed.reshape(face_count, -1)
    slot_of_face = lax.rem(face_at - lax.iota(jnp.int32, face_count) + face_count, face_count)
    gathered = jnp.take(landed, slot_of_face, axis=0)
    pieces = []
    offset = 0
    for part in parts:
        size = part.size
        piece = gathered[:, offset : offset + size].reshape((face_count,) + part.shape)
        pieces.append(piece)
        offset += size
    return pieces


def side_columns(gathered_edges, matching_row):
    left_side, right_side = pick_partner(gathered_edges, matching_row)
    return jnp.stack([left_side, right_side], axis=1).astype(jnp.bfloat16)


def add_ends(field, first_add, last_add, axis):
    length = field.shape[axis]
    head = lax.slice_in_dim(field, 0, 1, axis=axis) + jnp.expand_dims(first_add, axis)
    middle = lax.slice_in_dim(field, 1, length - 1, axis=axis)
    tail = lax.slice_in_dim(field, length - 1, length, axis=axis) + jnp.expand_dims(last_add, axis)
    return jnp.concatenate([head, middle, tail], axis=axis)


def return_sides(inside, gathered_margins, matching_row):
    left_back, right_back = pick_partner(gathered_margins, matching_row)
    return at_edges(inside, left_back, right_back)


def route_observations(obs_values, obs_dest, obs_pixel, device_count):
    obs_rows = obs_values.shape[0]
    obs_width = obs_values.shape[1]
    capacity = 2 * obs_rows // device_count
    target = obs_dest[:, 0]
    positions = lax.iota(jnp.int32, obs_rows)
    same_target = (target[:, None] == target[None, :]) & (positions[None, :] < positions[:, None])
    rank_within = jnp.sum(same_target.astype(jnp.int32), axis=1)
    slot_index = target * capacity + rank_within
    slot_ids = lax.iota(jnp.int32, device_count * capacity)
    hits = slot_ids[:, None] == slot_index[None, :]
    value_slots = jnp.dot(
        hits.astype(jnp.bfloat16), obs_values, preferred_element_type=jnp.float32
    ).astype(jnp.bfloat16)
    pixel_slots = jnp.sum(jnp.where(hits, obs_pixel[None, :], 0), axis=1)
    high = (pixel_slots // 16).astype(jnp.bfloat16).reshape(device_count, capacity)
    low = (pixel_slots % 16).astype(jnp.bfloat16).reshape(device_count, capacity)
    pixel_row = jnp.concatenate(
        [high, low, jnp.zeros((device_count, obs_width - 2 * capacity), jnp.bfloat16)], axis=1
    )
    payload = jnp.concatenate(
        [value_slots.reshape(device_count, capacity, obs_width), pixel_row[:, None]], axis=1
    )
    arrived = lax.all_to_all(payload, ("face", "tile"), split_axis=0, concat_axis=0, tiled=True)
    got_values = arrived[:, :capacity].reshape(-1, obs_width)
    got_high = arrived[:, capacity, 0:capacity].astype(jnp.int32)
    got_low = arrived[:, capacity, capacity : 2 * capacity].astype(jnp.int32)
    got_pixels = (got_high * 16 + got_low).reshape(-1)
    return got_values, got_pixels


def per_device(
    state,
    obs_values,
    obs_dest,
    obs_pixel,
    matching,
    kernel_one,
    bias_one,
    kernel_two,
    bias_two,
    cotangent,
):
    base_field = state[0, 0]
    cot_field = cotangent[0, 0]
    band_rows = base_field.shape[1]
    column_count = base_field.shape[2]
    channels = base_field.shape[3]
    tile_count = lax.axis_size("tile")
    face_count = lax.axis_size("face")
    tile_at = lax.axis_index("tile")
    face_at = lax.axis_index("face")
    device_count = tile_count * face_count
    obs_width = obs_values.shape[1]


    last_tile = tile_at == tile_count - 1
    matching_row = lax.dynamic_index_in_dim(matching, face_at, 0, keepdims=False)

    lifted = kernel_one.shape[2]
    both = extend_rows(jnp.concatenate([base_field, cot_field], axis=3), last_tile)
    cot_back, cot_margins = conv_back(both, channels, channels, kernel_two)
    obs_values, cot_back = lax.optimization_barrier((obs_values, cot_back))
    got_values, got_pixels = route_observations(obs_values, obs_dest, obs_pixel, device_count)
    pixel_count = 2 * band_rows * column_count
    pixel_ids = lax.iota(jnp.int32, pixel_count)
    onehot = (pixel_ids[:, None] == got_pixels[None, :]).astype(jnp.bfloat16)
    gridded = jnp.dot(onehot, got_values, preferred_element_type=jnp.float32)
    gridded = gridded.reshape(2, band_rows, column_count, obs_width)
    parts = [edge_cols(both, 0, channels), jnp.swapaxes(cot_margins, 1, 2)]
    first_out, landed = conv_gather(both, 0, channels, pack_parts(parts), kernel_one, 0)
    base_edges, cot_gathered = unpack_parts(landed, parts)
    first_sides = side_terms(side_columns(base_edges, matching_row), kernel_one)

    pre_act = at_edges(first_out, first_sides[:, 0], first_sides[:, 1]) + bias_one + gridded
    inner = activation(pre_act).astype(jnp.bfloat16)
    grad_inner = return_sides(cot_back, cot_gathered, matching_row)
    grad_pre = jax.vjp(activation, pre_act)[1](grad_inner)[0].astype(jnp.bfloat16)

    pair = extend_rows(jnp.concatenate([inner, grad_pre], axis=3), last_tile)
    pre_back, pre_margins = conv_back(pair, lifted, lifted, kernel_one)
    parts = [edge_cols(pair, 0, lifted), jnp.swapaxes(pre_margins, 1, 2)]
    second_out, landed = conv_gather(pair, 0, lifted, pack_parts(parts), kernel_two, 1)
    inner_edges, pre_gathered = unpack_parts(landed, parts)
    second_sides = side_terms(side_columns(inner_edges, matching_row), kernel_two)

    second_out = at_edges(second_out, second_sides[:, 0], second_sides[:, 1])
    analysis = (base_field.astype(jnp.float32) + second_out + bias_two).astype(jnp.bfloat16)
    grad_base = cot_field.astype(jnp.float32) + return_sides(pre_back, pre_gathered, matching_row)
    return (analysis[None, None], grad_base[None, None])


def solution(mesh):
    return jax.shard_map(
        per_device,
        mesh=mesh,
        in_specs=(
            P("face", "tile", None, None, None, None),
            P(("face", "tile"), None),
            P(("face", "tile"), None),
            P(("face", "tile")),
            P(),
            P(),
            P(),
            P(),
            P(),
            P("face", "tile", None, None, None, None),
        ),
        out_specs=(
            P("face", "tile", None, None, None, None),
            P("face", "tile", None, None, None, None),
        ),
        check_vma=False,
    )
```

```python
import functools

import jax
import jax.numpy as jnp
from jax import lax
from jax.experimental import pallas as pl
from jax.experimental.pallas import tpu as pltpu
from jax.sharding import PartitionSpec as P

MESH_IDS = pl.DeviceIdType.MESH


def activation(values):
    return jax.nn.gelu(values, approximate=True)


def tap_index(band, row_tap, col_tap, backward):
    if backward:
        row = 2 - row_tap if band == 0 else row_tap
        return 3 * row + 2 - col_tap
    row = row_tap if band == 0 else 2 - row_tap
    return 3 * row + col_tap


def conv_kernel(backward, first, width, src_ref, before_ref, after_ref, side_ref, k_ref, out_ref, margin_ref):
    bands, rows, cols, cout = out_ref.shape
    pixels = rows * cols
    lanes = slice(first, first + width)
    col = lax.broadcasted_iota(jnp.int32, (rows, cols, cout), 1).reshape(pixels, cout)
    for band in range(bands):
        ext = jnp.concatenate(
            [before_ref[band, :, :, lanes], src_ref[band, :, :, lanes], after_ref[band, :, :, lanes]],
            axis=0,
        )
        lhs = jnp.concatenate(
            [ext[dy : dy + rows].reshape(pixels, width) for dy in range(3)], axis=1
        )
        stacks = []
        for col_tap in range(3):
            taps = [k_ref[tap_index(band, dy, col_tap, backward)] for dy in range(3)]
            if backward:
                stacks.append(jnp.concatenate(taps, axis=1))
            else:
                stacks.append(jnp.concatenate(taps, axis=0))

        def product(values, stack):
            if backward:
                return lax.dot_general(
                    values, stack, (((1,), (1,)), ((), ())), preferred_element_type=jnp.float32
                )
            return jnp.dot(values, stack, preferred_element_type=jnp.float32)

        z_left = product(lhs, stacks[0])
        z_mid = product(lhs, stacks[1])
        z_right = product(lhs, stacks[2])
        if backward or side_ref is None:
            left_full = jnp.zeros((pixels, cout), jnp.float32)
            right_full = left_full
        else:
            sides = side_ref[band]
            left = jnp.concatenate([sides[0, dy : dy + rows] for dy in range(3)], axis=1)
            right = jnp.concatenate([sides[1, dy : dy + rows] for dy in range(3)], axis=1)
            left_term = product(left, stacks[0])
            right_term = product(right, stacks[2])
            left_full = jnp.broadcast_to(left_term[:, None, :], (rows, cols, cout)).reshape(pixels, cout)
            right_full = jnp.broadcast_to(right_term[:, None, :], (rows, cols, cout)).reshape(pixels, cout)
        from_left = jnp.where(col == 0, left_full, pltpu.roll(z_left, 1, 0))
        from_right = jnp.where(col == cols - 1, right_full, pltpu.roll(z_right, pixels - 1, 0))
        out_ref[band] = (z_mid + from_left + from_right).reshape(rows, cols, cout)
        if backward:
            margin_ref[band, 0] = z_right.reshape(rows, cols, cout)[:, 0, :]
            margin_ref[band, 1] = z_left.reshape(rows, cols, cout)[:, cols - 1, :]


def conv_pallas(pieces, first, width, sides, kernel, backward):
    source, before, after = pieces
    bands, rows, cols, _ = source.shape
    cout = kernel.shape[1] if backward else kernel.shape[2]
    if sides is None:
        sides = jnp.zeros((bands, 2, rows + 2, width), jnp.bfloat16)
    vmem = pl.BlockSpec(memory_space=pltpu.VMEM)
    out, margins = pl.pallas_call(
        functools.partial(conv_kernel, backward, first, width),
        in_specs=[vmem] * 5,
        out_specs=[vmem, vmem],
        out_shape=[
            jax.ShapeDtypeStruct((bands, rows, cols, cout), jnp.float32),
            jax.ShapeDtypeStruct((bands, 2, rows, cout), jnp.float32),
        ],
        compiler_params=pltpu.CompilerParams(vmem_limit_bytes=60 * 1024 * 1024),
    )(source, before, after, sides, kernel)
    return out, margins


def back_kernel(src_ref, before_ref, after_ref, k_ref, out_ref, margin_ref):
    band = pl.program_id(0)
    _, rows, cols, cout = out_ref.shape
    width = src_ref.shape[3]
    pixels = rows * cols
    col = lax.broadcasted_iota(jnp.int32, (rows, cols, cout), 1).reshape(pixels, cout)
    ext = jnp.concatenate([before_ref[0], src_ref[0], after_ref[0]], axis=0)
    lhs = jnp.concatenate([ext[dy : dy + rows].reshape(pixels, width) for dy in range(3)], axis=1)
    products = []
    for col_tap in range(3):
        taps = [k_ref[3 * (2 - dy + band * (2 * dy - 2)) + 2 - col_tap] for dy in range(3)]
        stack = jnp.concatenate(taps, axis=1)
        products.append(
            lax.dot_general(lhs, stack, (((1,), (1,)), ((), ())), preferred_element_type=jnp.float32)
        )
    z_left, z_mid, z_right = products
    from_left = jnp.where(col == 0, 0.0, pltpu.roll(z_left, 1, 0))
    from_right = jnp.where(col == cols - 1, 0.0, pltpu.roll(z_right, pixels - 1, 0))
    out_ref[0] = (z_mid + from_left + from_right).reshape(rows, cols, cout)
    margin_ref[0, 0] = z_right.reshape(rows, cols, cout)[:, 0, :]
    margin_ref[0, 1] = z_left.reshape(rows, cols, cout)[:, cols - 1, :]


def conv_back(pieces, first, width, kernel):
    source, before, after = pieces
    bands, rows, cols, _ = source.shape
    cout = kernel.shape[1]
    block = first // width
    return pl.pallas_call(
        back_kernel,
        grid=(bands,),
        in_specs=[
            pl.BlockSpec((1, rows, cols, width), lambda b: (b, 0, 0, block)),
            pl.BlockSpec((1, 1, cols, width), lambda b: (b, 0, 0, block)),
            pl.BlockSpec((1, 1, cols, width), lambda b: (b, 0, 0, block)),
            pl.BlockSpec(kernel.shape, lambda b: (0, 0, 0)),
        ],
        out_specs=[
            pl.BlockSpec((1, rows, cols, cout), lambda b: (b, 0, 0, 0)),
            pl.BlockSpec((1, 2, rows, cout), lambda b: (b, 0, 0, 0)),
        ],
        out_shape=[
            jax.ShapeDtypeStruct((bands, rows, cols, cout), jnp.float32),
            jax.ShapeDtypeStruct((bands, 2, rows, cout), jnp.float32),
        ],
        compiler_params=pltpu.CompilerParams(vmem_limit_bytes=60 * 1024 * 1024),
    )(source, before, after, kernel)


def conv_gather_kernel(count, block_ref, src_ref, before_ref, after_ref, k_ref,
                       out_ref, gathered_ref, landed, send_sems, recv_sems):
    step_at = pl.program_id(0)
    face = lax.axis_index("face")
    tile = lax.axis_index("tile")
    copies = []
    for step in range(1, count):
        peer = lax.rem(face + step, count)
        copies.append(
            pltpu.make_async_remote_copy(
                src_ref=block_ref,
                dst_ref=landed.at[step],
                send_sem=send_sems.at[step],
                recv_sem=recv_sems.at[step],
                device_id=(peer, tile),
                device_id_type=MESH_IDS,
            )
        )

    @pl.when(step_at == 0)
    def _():
        barrier = pltpu.get_barrier_semaphore()
        for step in range(1, count):
            peer = lax.rem(face + step, count)
            pl.semaphore_signal(barrier, inc=1, device_id=(peer, tile), device_id_type=MESH_IDS)
        pl.semaphore_wait(barrier, count - 1)
        for copy in copies:
            copy.start()
        gathered_ref[0] = block_ref[...]

    _, rows, cols, cout = out_ref.shape
    width = src_ref.shape[3]
    pixels = rows * cols
    col = lax.broadcasted_iota(jnp.int32, (rows, cols, cout), 1).reshape(pixels, cout)
    ext = jnp.concatenate([before_ref[0], src_ref[0], after_ref[0]], axis=0)
    lhs = jnp.concatenate([ext[dy : dy + rows].reshape(pixels, width) for dy in range(3)], axis=1)
    products = []
    for col_tap in range(3):
        taps = [k_ref[3 * (dy + step_at * (2 - 2 * dy)) + col_tap] for dy in range(3)]
        stack = jnp.concatenate(taps, axis=0)
        products.append(jnp.dot(lhs, stack, preferred_element_type=jnp.float32))
    z_left, z_mid, z_right = products
    from_left = jnp.where(col == 0, 0.0, pltpu.roll(z_left, 1, 0))
    from_right = jnp.where(col == cols - 1, 0.0, pltpu.roll(z_right, pixels - 1, 0))
    out_ref[0] = (z_mid + from_left + from_right).reshape(rows, cols, cout)

    @pl.when(step_at == pl.num_programs(0) - 1)
    def _():
        for copy in copies:
            copy.wait()
        for step in range(1, count):
            gathered_ref[step] = landed[step]


def conv_gather(pieces, first, width, block, kernel, gather_id):
    source, before, after = pieces
    bands, rows, cols, _ = source.shape
    cout = kernel.shape[2]
    count = lax.axis_size("face")
    block_rows, lanes = block.shape
    lane_block = first // width
    return pl.pallas_call(
        functools.partial(conv_gather_kernel, count),
        grid=(bands,),
        in_specs=[
            pl.BlockSpec((block_rows, lanes), lambda b: (0, 0)),
            pl.BlockSpec((1, rows, cols, width), lambda b: (b, 0, 0, lane_block)),
            pl.BlockSpec((1, 1, cols, width), lambda b: (b, 0, 0, lane_block)),
            pl.BlockSpec((1, 1, cols, width), lambda b: (b, 0, 0, lane_block)),
            pl.BlockSpec(kernel.shape, lambda b: (0, 0, 0)),
        ],
        out_specs=[
            pl.BlockSpec((1, rows, cols, cout), lambda b: (b, 0, 0, 0)),
            pl.BlockSpec((count, block_rows, lanes), lambda b: (0, 0, 0)),
        ],
        out_shape=[
            jax.ShapeDtypeStruct((bands, rows, cols, cout), jnp.float32),
            jax.ShapeDtypeStruct((count, block_rows, lanes), block.dtype),
        ],
        scratch_shapes=[
            pltpu.VMEM((count, block_rows, lanes), block.dtype),
            pltpu.SemaphoreType.DMA((count,)),
            pltpu.SemaphoreType.DMA((count,)),
        ],
        compiler_params=pltpu.CompilerParams(
            collective_id=gather_id, has_side_effects=True, vmem_limit_bytes=60 * 1024 * 1024
        ),
    )(block, source, before, after, kernel)


def side_terms(sides, kernel):
    bands, _, ext_rows, width = sides.shape
    rows = ext_rows - 2
    terms = []
    for band in range(bands):
        per_side = []
        for side, col_tap in ((0, 0), (1, 2)):
            stacked = jnp.concatenate([sides[band, side, dy : dy + rows] for dy in range(3)], axis=1)
            weights = jnp.concatenate(
                [kernel[tap_index(band, dy, col_tap, False)] for dy in range(3)], axis=0
            )
            per_side.append(jnp.dot(stacked, weights, preferred_element_type=jnp.float32))
        terms.append(jnp.stack(per_side))
    return jnp.stack(terms)


def at_edges(field, left_add, right_add):
    cols = field.shape[2]
    col = lax.broadcasted_iota(jnp.int32, field.shape, 2)
    return field + jnp.where(col == 0, left_add[:, :, None], 0.0) + jnp.where(
        col == cols - 1, right_add[:, :, None], 0.0
    )


def extend_rows(source, last_tile):
    count = lax.axis_size("tile")
    band_rows = source.shape[1]
    head = source[:, 0:1]
    tail = source[:, band_rows - 1 : band_rows]
    before = lax.ppermute(tail, "tile", [(i, i + 1) for i in range(count - 1)])
    after = lax.ppermute(head, "tile", [(i + 1, i) for i in range(count - 1)])
    after = jnp.where(last_tile, tail[::-1], after)
    return source, before, after


def edge_cols(pieces, first, width):
    extended = jnp.concatenate([piece[..., first : first + width] for piece in (pieces[1], pieces[0], pieces[2])], axis=1)
    return jnp.stack([extended[:, :, 0], extended[:, :, -1]], axis=2)


def pick_partner(gathered, matching_row):
    picked_sides = []
    for side_number in range(2):
        partner = matching_row[side_number, 0]
        their_side = matching_row[side_number, 1]
        flipped = matching_row[side_number, 2]
        chosen = lax.dynamic_index_in_dim(gathered, partner, 0, keepdims=False)
        column = jnp.where(their_side == 0, chosen[:, :, 0], chosen[:, :, 1])
        column = jnp.where(flipped == 1, column[::-1], column)
        picked_sides.append(column)
    return picked_sides


def pack_parts(parts):
    flat = jnp.concatenate([part.astype(jnp.float32).reshape(-1) for part in parts])
    return flat.reshape(-1, 128)


def unpack_parts(landed, parts):
    face_count = lax.axis_size("face")
    face_at = lax.axis_index("face")
    landed = landed.reshape(face_count, -1)
    slot_of_face = lax.rem(face_at - lax.iota(jnp.int32, face_count) + face_count, face_count)
    gathered = jnp.take(landed, slot_of_face, axis=0)
    pieces = []
    offset = 0
    for part in parts:
        size = part.size
        piece = gathered[:, offset : offset + size].reshape((face_count,) + part.shape)
        pieces.append(piece)
        offset += size
    return pieces


def side_columns(gathered_edges, matching_row):
    left_side, right_side = pick_partner(gathered_edges, matching_row)
    return jnp.stack([left_side, right_side], axis=1).astype(jnp.bfloat16)


def add_ends(field, first_add, last_add, axis):
    length = field.shape[axis]
    head = lax.slice_in_dim(field, 0, 1, axis=axis) + jnp.expand_dims(first_add, axis)
    middle = lax.slice_in_dim(field, 1, length - 1, axis=axis)
    tail = lax.slice_in_dim(field, length - 1, length, axis=axis) + jnp.expand_dims(last_add, axis)
    return jnp.concatenate([head, middle, tail], axis=axis)


def return_sides(inside, gathered_margins, matching_row):
    left_back, right_back = pick_partner(gathered_margins, matching_row)
    return at_edges(inside, left_back, right_back)


def route_observations(obs_values, obs_dest, obs_pixel, device_count):
    obs_rows = obs_values.shape[0]
    obs_width = obs_values.shape[1]
    capacity = 2 * obs_rows // device_count
    target = obs_dest[:, 0]
    positions = lax.iota(jnp.int32, obs_rows)
    same_target = (target[:, None] == target[None, :]) & (positions[None, :] < positions[:, None])
    rank_within = jnp.sum(same_target.astype(jnp.int32), axis=1)
    slot_index = target * capacity + rank_within
    slot_ids = lax.iota(jnp.int32, device_count * capacity)
    hits = slot_ids[:, None] == slot_index[None, :]
    value_slots = jnp.dot(
        hits.astype(jnp.bfloat16), obs_values, preferred_element_type=jnp.float32
    ).astype(jnp.bfloat16)
    pixel_slots = jnp.sum(jnp.where(hits, obs_pixel[None, :], 0), axis=1)
    high = (pixel_slots // 16).astype(jnp.bfloat16).reshape(device_count, capacity)
    low = (pixel_slots % 16).astype(jnp.bfloat16).reshape(device_count, capacity)
    pixel_row = jnp.concatenate(
        [high, low, jnp.zeros((device_count, obs_width - 2 * capacity), jnp.bfloat16)], axis=1
    )
    payload = jnp.concatenate(
        [value_slots.reshape(device_count, capacity, obs_width), pixel_row[:, None]], axis=1
    )
    arrived = lax.all_to_all(payload, ("face", "tile"), split_axis=0, concat_axis=0, tiled=True)
    got_values = arrived[:, :capacity].reshape(-1, obs_width)
    got_high = arrived[:, capacity, 0:capacity].astype(jnp.int32)
    got_low = arrived[:, capacity, capacity : 2 * capacity].astype(jnp.int32)
    got_pixels = (got_high * 16 + got_low).reshape(-1)
    return got_values, got_pixels


def per_device(
    state,
    obs_values,
    obs_dest,
    obs_pixel,
    matching,
    kernel_one,
    bias_one,
    kernel_two,
    bias_two,
    cotangent,
):
    base_field = state[0, 0]
    cot_field = cotangent[0, 0]
    band_rows = base_field.shape[1]
    column_count = base_field.shape[2]
    channels = base_field.shape[3]
    tile_count = lax.axis_size("tile")
    face_count = lax.axis_size("face")
    tile_at = lax.axis_index("tile")
    face_at = lax.axis_index("face")
    device_count = tile_count * face_count
    obs_width = obs_values.shape[1]

    got_values, got_pixels = route_observations(obs_values, obs_dest, obs_pixel, device_count)
    pixel_count = 2 * band_rows * column_count
    pixel_ids = lax.iota(jnp.int32, pixel_count)
    onehot = (pixel_ids[:, None] == got_pixels[None, :]).astype(jnp.bfloat16)
    gridded = jnp.dot(onehot, got_values, preferred_element_type=jnp.float32)
    gridded = gridded.reshape(2, band_rows, column_count, obs_width)

    last_tile = tile_at == tile_count - 1
    matching_row = lax.dynamic_index_in_dim(matching, face_at, 0, keepdims=False)

    lifted = kernel_one.shape[2]
    fields, got_values = lax.optimization_barrier(
        (jnp.concatenate([base_field, cot_field], axis=3), got_values)
    )
    both = extend_rows(fields, last_tile)
    cot_back, cot_margins = conv_back(both, channels, channels, kernel_two)
    parts = [edge_cols(both, 0, channels), jnp.swapaxes(cot_margins, 1, 2)]
    first_out, landed = conv_gather(both, 0, channels, pack_parts(parts), kernel_one, 0)
    base_edges, cot_gathered = unpack_parts(landed, parts)
    first_sides = side_terms(side_columns(base_edges, matching_row), kernel_one)

    pre_act = at_edges(first_out, first_sides[:, 0], first_sides[:, 1]) + bias_one + gridded
    inner = activation(pre_act).astype(jnp.bfloat16)
    grad_inner = return_sides(cot_back, cot_gathered, matching_row)
    grad_pre = jax.vjp(activation, pre_act)[1](grad_inner)[0].astype(jnp.bfloat16)

    pair = extend_rows(jnp.concatenate([inner, grad_pre], axis=3), last_tile)
    pre_back, pre_margins = conv_back(pair, lifted, lifted, kernel_one)
    parts = [edge_cols(pair, 0, lifted), jnp.swapaxes(pre_margins, 1, 2)]
    second_out, landed = conv_gather(pair, 0, lifted, pack_parts(parts), kernel_two, 1)
    inner_edges, pre_gathered = unpack_parts(landed, parts)
    second_sides = side_terms(side_columns(inner_edges, matching_row), kernel_two)

    second_out = at_edges(second_out, second_sides[:, 0], second_sides[:, 1])
    analysis = (base_field.astype(jnp.float32) + second_out + bias_two).astype(jnp.bfloat16)
    grad_base = cot_field.astype(jnp.float32) + return_sides(pre_back, pre_gathered, matching_row)
    return (analysis[None, None], grad_base[None, None])


def solution(mesh):
    return jax.shard_map(
        per_device,
        mesh=mesh,
        in_specs=(
            P("face", "tile", None, None, None, None),
            P(("face", "tile"), None),
            P(("face", "tile"), None),
            P(("face", "tile")),
            P(),
            P(),
            P(),
            P(),
            P(),
            P("face", "tile", None, None, None, None),
        ),
        out_specs=(
            P("face", "tile", None, None, None, None),
            P("face", "tile", None, None, None, None),
        ),
        check_vma=False,
    )
```

```python
import functools

import jax
import jax.numpy as jnp
from jax import lax
from jax.experimental import pallas as pl
from jax.experimental.pallas import tpu as pltpu
from jax.sharding import PartitionSpec as P

MESH_IDS = pl.DeviceIdType.MESH


def activation(values):
    return jax.nn.gelu(values, approximate=True)


def tap_index(band, row_tap, col_tap, backward):
    if backward:
        row = 2 - row_tap if band == 0 else row_tap
        return 3 * row + 2 - col_tap
    row = row_tap if band == 0 else 2 - row_tap
    return 3 * row + col_tap


def conv_kernel(backward, first, width, src_ref, before_ref, after_ref, side_ref, k_ref, out_ref, margin_ref):
    bands, rows, cols, cout = out_ref.shape
    pixels = rows * cols
    lanes = slice(first, first + width)
    col = lax.broadcasted_iota(jnp.int32, (rows, cols, cout), 1).reshape(pixels, cout)
    for band in range(bands):
        ext = jnp.concatenate(
            [before_ref[band, :, :, lanes], src_ref[band, :, :, lanes], after_ref[band, :, :, lanes]],
            axis=0,
        )
        lhs = jnp.concatenate(
            [ext[dy : dy + rows].reshape(pixels, width) for dy in range(3)], axis=1
        )
        stacks = []
        for col_tap in range(3):
            taps = [k_ref[tap_index(band, dy, col_tap, backward)] for dy in range(3)]
            if backward:
                stacks.append(jnp.concatenate(taps, axis=1))
            else:
                stacks.append(jnp.concatenate(taps, axis=0))

        def product(values, stack):
            if backward:
                return lax.dot_general(
                    values, stack, (((1,), (1,)), ((), ())), preferred_element_type=jnp.float32
                )
            return jnp.dot(values, stack, preferred_element_type=jnp.float32)

        z_left = product(lhs, stacks[0])
        z_mid = product(lhs, stacks[1])
        z_right = product(lhs, stacks[2])
        if backward or side_ref is None:
            left_full = jnp.zeros((pixels, cout), jnp.float32)
            right_full = left_full
        else:
            sides = side_ref[band]
            left = jnp.concatenate([sides[0, dy : dy + rows] for dy in range(3)], axis=1)
            right = jnp.concatenate([sides[1, dy : dy + rows] for dy in range(3)], axis=1)
            left_term = product(left, stacks[0])
            right_term = product(right, stacks[2])
            left_full = jnp.broadcast_to(left_term[:, None, :], (rows, cols, cout)).reshape(pixels, cout)
            right_full = jnp.broadcast_to(right_term[:, None, :], (rows, cols, cout)).reshape(pixels, cout)
        from_left = jnp.where(col == 0, left_full, pltpu.roll(z_left, 1, 0))
        from_right = jnp.where(col == cols - 1, right_full, pltpu.roll(z_right, pixels - 1, 0))
        out_ref[band] = (z_mid + from_left + from_right).reshape(rows, cols, cout)
        if backward:
            margin_ref[band, 0] = z_right.reshape(rows, cols, cout)[:, 0, :]
            margin_ref[band, 1] = z_left.reshape(rows, cols, cout)[:, cols - 1, :]


def conv_pallas(pieces, first, width, sides, kernel, backward):
    source, before, after = pieces
    bands, rows, cols, _ = source.shape
    cout = kernel.shape[1] if backward else kernel.shape[2]
    if sides is None:
        sides = jnp.zeros((bands, 2, rows + 2, width), jnp.bfloat16)
    vmem = pl.BlockSpec(memory_space=pltpu.VMEM)
    out, margins = pl.pallas_call(
        functools.partial(conv_kernel, backward, first, width),
        in_specs=[vmem] * 5,
        out_specs=[vmem, vmem],
        out_shape=[
            jax.ShapeDtypeStruct((bands, rows, cols, cout), jnp.float32),
            jax.ShapeDtypeStruct((bands, 2, rows, cout), jnp.float32),
        ],
        compiler_params=pltpu.CompilerParams(vmem_limit_bytes=60 * 1024 * 1024),
    )(source, before, after, sides, kernel)
    return out, margins


def back_kernel(src_ref, before_ref, after_ref, k_ref, out_ref, margin_ref):
    band = pl.program_id(0)
    _, rows, cols, cout = out_ref.shape
    width = src_ref.shape[3]
    pixels = rows * cols
    col = lax.broadcasted_iota(jnp.int32, (rows, cols, cout), 1).reshape(pixels, cout)
    ext = jnp.concatenate([before_ref[0], src_ref[0], after_ref[0]], axis=0)
    lhs = jnp.concatenate([ext[dy : dy + rows].reshape(pixels, width) for dy in range(3)], axis=1)
    stacks = []
    for col_tap in range(3):
        taps = [k_ref[3 * (2 - dy + band * (2 * dy - 2)) + 2 - col_tap] for dy in range(3)]
        stacks.append(jnp.concatenate(taps, axis=1))
    joined = lax.dot_general(
        lhs, jnp.concatenate(stacks, axis=0), (((1,), (1,)), ((), ())), preferred_element_type=jnp.float32
    )
    z_left, z_mid, z_right = [joined[:, i * cout : (i + 1) * cout] for i in range(3)]
    from_left = jnp.where(col == 0, 0.0, pltpu.roll(z_left, 1, 0))
    from_right = jnp.where(col == cols - 1, 0.0, pltpu.roll(z_right, pixels - 1, 0))
    out_ref[0] = (z_mid + from_left + from_right).reshape(rows, cols, cout)
    margin_ref[0, 0] = z_right.reshape(rows, cols, cout)[:, 0, :]
    margin_ref[0, 1] = z_left.reshape(rows, cols, cout)[:, cols - 1, :]


def conv_back(pieces, first, width, kernel):
    source, before, after = pieces
    bands, rows, cols, _ = source.shape
    cout = kernel.shape[1]
    block = first // width
    return pl.pallas_call(
        back_kernel,
        grid=(bands,),
        in_specs=[
            pl.BlockSpec((1, rows, cols, width), lambda b: (b, 0, 0, block)),
            pl.BlockSpec((1, 1, cols, width), lambda b: (b, 0, 0, block)),
            pl.BlockSpec((1, 1, cols, width), lambda b: (b, 0, 0, block)),
            pl.BlockSpec(kernel.shape, lambda b: (0, 0, 0)),
        ],
        out_specs=[
            pl.BlockSpec((1, rows, cols, cout), lambda b: (b, 0, 0, 0)),
            pl.BlockSpec((1, 2, rows, cout), lambda b: (b, 0, 0, 0)),
        ],
        out_shape=[
            jax.ShapeDtypeStruct((bands, rows, cols, cout), jnp.float32),
            jax.ShapeDtypeStruct((bands, 2, rows, cout), jnp.float32),
        ],
        compiler_params=pltpu.CompilerParams(vmem_limit_bytes=60 * 1024 * 1024),
    )(source, before, after, kernel)


def conv_gather_kernel(count, block_ref, src_ref, before_ref, after_ref, k_ref,
                       out_ref, gathered_ref, landed, send_sems, recv_sems):
    step_at = pl.program_id(0)
    face = lax.axis_index("face")
    tile = lax.axis_index("tile")
    copies = []
    for step in range(1, count):
        peer = lax.rem(face + step, count)
        copies.append(
            pltpu.make_async_remote_copy(
                src_ref=block_ref,
                dst_ref=landed.at[step],
                send_sem=send_sems.at[step],
                recv_sem=recv_sems.at[step],
                device_id=(peer, tile),
                device_id_type=MESH_IDS,
            )
        )

    @pl.when(step_at == 0)
    def _():
        barrier = pltpu.get_barrier_semaphore()
        for step in range(1, count):
            peer = lax.rem(face + step, count)
            pl.semaphore_signal(barrier, inc=1, device_id=(peer, tile), device_id_type=MESH_IDS)
        pl.semaphore_wait(barrier, count - 1)
        for copy in copies:
            copy.start()
        gathered_ref[0] = block_ref[...]

    _, rows, cols, cout = out_ref.shape
    width = src_ref.shape[3]
    pixels = rows * cols
    col = lax.broadcasted_iota(jnp.int32, (rows, cols, cout), 1).reshape(pixels, cout)
    ext = jnp.concatenate([before_ref[0], src_ref[0], after_ref[0]], axis=0)
    lhs = jnp.concatenate([ext[dy : dy + rows].reshape(pixels, width) for dy in range(3)], axis=1)
    stacks = []
    for col_tap in range(3):
        taps = [k_ref[3 * (dy + step_at * (2 - 2 * dy)) + col_tap] for dy in range(3)]
        stacks.append(jnp.concatenate(taps, axis=0))
    joined = jnp.dot(lhs, jnp.concatenate(stacks, axis=1), preferred_element_type=jnp.float32)
    z_left, z_mid, z_right = [joined[:, i * cout : (i + 1) * cout] for i in range(3)]
    from_left = jnp.where(col == 0, 0.0, pltpu.roll(z_left, 1, 0))
    from_right = jnp.where(col == cols - 1, 0.0, pltpu.roll(z_right, pixels - 1, 0))
    out_ref[0] = (z_mid + from_left + from_right).reshape(rows, cols, cout)

    @pl.when(step_at == pl.num_programs(0) - 1)
    def _():
        for copy in copies:
            copy.wait()
        for step in range(1, count):
            gathered_ref[step] = landed[step]


def conv_gather(pieces, first, width, block, kernel, gather_id):
    source, before, after = pieces
    bands, rows, cols, _ = source.shape
    cout = kernel.shape[2]
    count = lax.axis_size("face")
    block_rows, lanes = block.shape
    lane_block = first // width
    return pl.pallas_call(
        functools.partial(conv_gather_kernel, count),
        grid=(bands,),
        in_specs=[
            pl.BlockSpec((block_rows, lanes), lambda b: (0, 0)),
            pl.BlockSpec((1, rows, cols, width), lambda b: (b, 0, 0, lane_block)),
            pl.BlockSpec((1, 1, cols, width), lambda b: (b, 0, 0, lane_block)),
            pl.BlockSpec((1, 1, cols, width), lambda b: (b, 0, 0, lane_block)),
            pl.BlockSpec(kernel.shape, lambda b: (0, 0, 0)),
        ],
        out_specs=[
            pl.BlockSpec((1, rows, cols, cout), lambda b: (b, 0, 0, 0)),
            pl.BlockSpec((count, block_rows, lanes), lambda b: (0, 0, 0)),
        ],
        out_shape=[
            jax.ShapeDtypeStruct((bands, rows, cols, cout), jnp.float32),
            jax.ShapeDtypeStruct((count, block_rows, lanes), block.dtype),
        ],
        scratch_shapes=[
            pltpu.VMEM((count, block_rows, lanes), block.dtype),
            pltpu.SemaphoreType.DMA((count,)),
            pltpu.SemaphoreType.DMA((count,)),
        ],
        compiler_params=pltpu.CompilerParams(
            collective_id=gather_id, has_side_effects=True, vmem_limit_bytes=60 * 1024 * 1024
        ),
    )(block, source, before, after, kernel)


def side_terms(sides, kernel):
    bands, _, ext_rows, width = sides.shape
    rows = ext_rows - 2
    terms = []
    for band in range(bands):
        per_side = []
        for side, col_tap in ((0, 0), (1, 2)):
            stacked = jnp.concatenate([sides[band, side, dy : dy + rows] for dy in range(3)], axis=1)
            weights = jnp.concatenate(
                [kernel[tap_index(band, dy, col_tap, False)] for dy in range(3)], axis=0
            )
            per_side.append(jnp.dot(stacked, weights, preferred_element_type=jnp.float32))
        terms.append(jnp.stack(per_side))
    return jnp.stack(terms)


def at_edges(field, left_add, right_add):
    cols = field.shape[2]
    col = lax.broadcasted_iota(jnp.int32, field.shape, 2)
    return field + jnp.where(col == 0, left_add[:, :, None], 0.0) + jnp.where(
        col == cols - 1, right_add[:, :, None], 0.0
    )


def extend_rows(source, last_tile):
    count = lax.axis_size("tile")
    band_rows = source.shape[1]
    head = source[:, 0:1]
    tail = source[:, band_rows - 1 : band_rows]
    before = lax.ppermute(tail, "tile", [(i, i + 1) for i in range(count - 1)])
    after = lax.ppermute(head, "tile", [(i + 1, i) for i in range(count - 1)])
    after = jnp.where(last_tile, tail[::-1], after)
    return source, before, after


def edge_cols(pieces, first, width):
    extended = jnp.concatenate([piece[..., first : first + width] for piece in (pieces[1], pieces[0], pieces[2])], axis=1)
    return jnp.stack([extended[:, :, 0], extended[:, :, -1]], axis=2)


def pick_partner(gathered, matching_row):
    picked_sides = []
    for side_number in range(2):
        partner = matching_row[side_number, 0]
        their_side = matching_row[side_number, 1]
        flipped = matching_row[side_number, 2]
        chosen = lax.dynamic_index_in_dim(gathered, partner, 0, keepdims=False)
        column = jnp.where(their_side == 0, chosen[:, :, 0], chosen[:, :, 1])
        column = jnp.where(flipped == 1, column[::-1], column)
        picked_sides.append(column)
    return picked_sides


def pack_parts(parts):
    flat = jnp.concatenate([part.astype(jnp.float32).reshape(-1) for part in parts])
    return flat.reshape(-1, 128)


def unpack_parts(landed, parts):
    face_count = lax.axis_size("face")
    face_at = lax.axis_index("face")
    landed = landed.reshape(face_count, -1)
    slot_of_face = lax.rem(face_at - lax.iota(jnp.int32, face_count) + face_count, face_count)
    gathered = jnp.take(landed, slot_of_face, axis=0)
    pieces = []
    offset = 0
    for part in parts:
        size = part.size
        piece = gathered[:, offset : offset + size].reshape((face_count,) + part.shape)
        pieces.append(piece)
        offset += size
    return pieces


def side_columns(gathered_edges, matching_row):
    left_side, right_side = pick_partner(gathered_edges, matching_row)
    return jnp.stack([left_side, right_side], axis=1).astype(jnp.bfloat16)


def add_ends(field, first_add, last_add, axis):
    length = field.shape[axis]
    head = lax.slice_in_dim(field, 0, 1, axis=axis) + jnp.expand_dims(first_add, axis)
    middle = lax.slice_in_dim(field, 1, length - 1, axis=axis)
    tail = lax.slice_in_dim(field, length - 1, length, axis=axis) + jnp.expand_dims(last_add, axis)
    return jnp.concatenate([head, middle, tail], axis=axis)


def return_sides(inside, gathered_margins, matching_row):
    left_back, right_back = pick_partner(gathered_margins, matching_row)
    return at_edges(inside, left_back, right_back)


def route_observations(obs_values, obs_dest, obs_pixel, device_count):
    obs_rows = obs_values.shape[0]
    obs_width = obs_values.shape[1]
    capacity = 2 * obs_rows // device_count
    target = obs_dest[:, 0]
    positions = lax.iota(jnp.int32, obs_rows)
    same_target = (target[:, None] == target[None, :]) & (positions[None, :] < positions[:, None])
    rank_within = jnp.sum(same_target.astype(jnp.int32), axis=1)
    slot_index = target * capacity + rank_within
    slot_ids = lax.iota(jnp.int32, device_count * capacity)
    hits = slot_ids[:, None] == slot_index[None, :]
    value_slots = jnp.dot(
        hits.astype(jnp.bfloat16), obs_values, preferred_element_type=jnp.float32
    ).astype(jnp.bfloat16)
    pixel_slots = jnp.sum(jnp.where(hits, obs_pixel[None, :], 0), axis=1)
    high = (pixel_slots // 16).astype(jnp.bfloat16).reshape(device_count, capacity)
    low = (pixel_slots % 16).astype(jnp.bfloat16).reshape(device_count, capacity)
    pixel_row = jnp.concatenate(
        [high, low, jnp.zeros((device_count, obs_width - 2 * capacity), jnp.bfloat16)], axis=1
    )
    payload = jnp.concatenate(
        [value_slots.reshape(device_count, capacity, obs_width), pixel_row[:, None]], axis=1
    )
    arrived = lax.all_to_all(payload, ("face", "tile"), split_axis=0, concat_axis=0, tiled=True)
    got_values = arrived[:, :capacity].reshape(-1, obs_width)
    got_high = arrived[:, capacity, 0:capacity].astype(jnp.int32)
    got_low = arrived[:, capacity, capacity : 2 * capacity].astype(jnp.int32)
    got_pixels = (got_high * 16 + got_low).reshape(-1)
    return got_values, got_pixels


def per_device(
    state,
    obs_values,
    obs_dest,
    obs_pixel,
    matching,
    kernel_one,
    bias_one,
    kernel_two,
    bias_two,
    cotangent,
):
    base_field = state[0, 0]
    cot_field = cotangent[0, 0]
    band_rows = base_field.shape[1]
    column_count = base_field.shape[2]
    channels = base_field.shape[3]
    tile_count = lax.axis_size("tile")
    face_count = lax.axis_size("face")
    tile_at = lax.axis_index("tile")
    face_at = lax.axis_index("face")
    device_count = tile_count * face_count
    obs_width = obs_values.shape[1]

    got_values, got_pixels = route_observations(obs_values, obs_dest, obs_pixel, device_count)
    pixel_count = 2 * band_rows * column_count
    pixel_ids = lax.iota(jnp.int32, pixel_count)
    onehot = (pixel_ids[:, None] == got_pixels[None, :]).astype(jnp.bfloat16)
    gridded = jnp.dot(onehot, got_values, preferred_element_type=jnp.float32)
    gridded = gridded.reshape(2, band_rows, column_count, obs_width)

    last_tile = tile_at == tile_count - 1
    matching_row = lax.dynamic_index_in_dim(matching, face_at, 0, keepdims=False)

    lifted = kernel_one.shape[2]
    fields, got_values = lax.optimization_barrier(
        (jnp.concatenate([base_field, cot_field], axis=3), got_values)
    )
    both = extend_rows(fields, last_tile)
    cot_back, cot_margins = conv_back(both, channels, channels, kernel_two)
    parts = [edge_cols(both, 0, channels), jnp.swapaxes(cot_margins, 1, 2)]
    first_out, landed = conv_gather(both, 0, channels, pack_parts(parts), kernel_one, 0)
    base_edges, cot_gathered = unpack_parts(landed, parts)
    first_sides = side_terms(side_columns(base_edges, matching_row), kernel_one)

    pre_act = at_edges(first_out, first_sides[:, 0], first_sides[:, 1]) + bias_one + gridded
    inner = activation(pre_act).astype(jnp.bfloat16)
    grad_inner = return_sides(cot_back, cot_gathered, matching_row)
    grad_pre = jax.vjp(activation, pre_act)[1](grad_inner)[0].astype(jnp.bfloat16)

    pair = extend_rows(jnp.concatenate([inner, grad_pre], axis=3), last_tile)
    pre_back, pre_margins = conv_back(pair, lifted, lifted, kernel_one)
    parts = [edge_cols(pair, 0, lifted), jnp.swapaxes(pre_margins, 1, 2)]
    second_out, landed = conv_gather(pair, 0, lifted, pack_parts(parts), kernel_two, 1)
    inner_edges, pre_gathered = unpack_parts(landed, parts)
    second_sides = side_terms(side_columns(inner_edges, matching_row), kernel_two)

    second_out = at_edges(second_out, second_sides[:, 0], second_sides[:, 1])
    analysis = (base_field.astype(jnp.float32) + second_out + bias_two).astype(jnp.bfloat16)
    grad_base = cot_field.astype(jnp.float32) + return_sides(pre_back, pre_gathered, matching_row)
    return (analysis[None, None], grad_base[None, None])


def solution(mesh):
    return jax.shard_map(
        per_device,
        mesh=mesh,
        in_specs=(
            P("face", "tile", None, None, None, None),
            P(("face", "tile"), None),
            P(("face", "tile"), None),
            P(("face", "tile")),
            P(),
            P(),
            P(),
            P(),
            P(),
            P("face", "tile", None, None, None, None),
        ),
        out_specs=(
            P("face", "tile", None, None, None, None),
            P("face", "tile", None, None, None, None),
        ),
        check_vma=False,
    )
```

```python
import functools

import jax
import jax.numpy as jnp
from jax import lax
from jax.experimental import pallas as pl
from jax.experimental.pallas import tpu as pltpu
from jax.sharding import PartitionSpec as P

MESH_IDS = pl.DeviceIdType.MESH


def activation(values):
    return jax.nn.gelu(values, approximate=True)


def tap_index(band, row_tap, col_tap, backward):
    if backward:
        row = 2 - row_tap if band == 0 else row_tap
        return 3 * row + 2 - col_tap
    row = row_tap if band == 0 else 2 - row_tap
    return 3 * row + col_tap


def conv_kernel(backward, first, width, src_ref, before_ref, after_ref, side_ref, k_ref, out_ref, margin_ref):
    bands, rows, cols, cout = out_ref.shape
    pixels = rows * cols
    lanes = slice(first, first + width)
    col = lax.broadcasted_iota(jnp.int32, (rows, cols, cout), 1).reshape(pixels, cout)
    for band in range(bands):
        ext = jnp.concatenate(
            [before_ref[band, :, :, lanes], src_ref[band, :, :, lanes], after_ref[band, :, :, lanes]],
            axis=0,
        )
        lhs = jnp.concatenate(
            [ext[dy : dy + rows].reshape(pixels, width) for dy in range(3)], axis=1
        )
        stacks = []
        for col_tap in range(3):
            taps = [k_ref[tap_index(band, dy, col_tap, backward)] for dy in range(3)]
            if backward:
                stacks.append(jnp.concatenate(taps, axis=1))
            else:
                stacks.append(jnp.concatenate(taps, axis=0))

        def product(values, stack):
            if backward:
                return lax.dot_general(
                    values, stack, (((1,), (1,)), ((), ())), preferred_element_type=jnp.float32
                )
            return jnp.dot(values, stack, preferred_element_type=jnp.float32)

        z_left = product(lhs, stacks[0])
        z_mid = product(lhs, stacks[1])
        z_right = product(lhs, stacks[2])
        if backward or side_ref is None:
            left_full = jnp.zeros((pixels, cout), jnp.float32)
            right_full = left_full
        else:
            sides = side_ref[band]
            left = jnp.concatenate([sides[0, dy : dy + rows] for dy in range(3)], axis=1)
            right = jnp.concatenate([sides[1, dy : dy + rows] for dy in range(3)], axis=1)
            left_term = product(left, stacks[0])
            right_term = product(right, stacks[2])
            left_full = jnp.broadcast_to(left_term[:, None, :], (rows, cols, cout)).reshape(pixels, cout)
            right_full = jnp.broadcast_to(right_term[:, None, :], (rows, cols, cout)).reshape(pixels, cout)
        from_left = jnp.where(col == 0, left_full, pltpu.roll(z_left, 1, 0))
        from_right = jnp.where(col == cols - 1, right_full, pltpu.roll(z_right, pixels - 1, 0))
        out_ref[band] = (z_mid + from_left + from_right).reshape(rows, cols, cout)
        if backward:
            margin_ref[band, 0] = z_right.reshape(rows, cols, cout)[:, 0, :]
            margin_ref[band, 1] = z_left.reshape(rows, cols, cout)[:, cols - 1, :]


def conv_pallas(pieces, first, width, sides, kernel, backward):
    source, before, after = pieces
    bands, rows, cols, _ = source.shape
    cout = kernel.shape[1] if backward else kernel.shape[2]
    if sides is None:
        sides = jnp.zeros((bands, 2, rows + 2, width), jnp.bfloat16)
    vmem = pl.BlockSpec(memory_space=pltpu.VMEM)
    out, margins = pl.pallas_call(
        functools.partial(conv_kernel, backward, first, width),
        in_specs=[vmem] * 5,
        out_specs=[vmem, vmem],
        out_shape=[
            jax.ShapeDtypeStruct((bands, rows, cols, cout), jnp.float32),
            jax.ShapeDtypeStruct((bands, 2, rows, cout), jnp.float32),
        ],
        compiler_params=pltpu.CompilerParams(vmem_limit_bytes=60 * 1024 * 1024),
    )(source, before, after, sides, kernel)
    return out, margins


def back_kernel(src_ref, before_ref, after_ref, k_ref, out_ref, margin_ref):
    band = pl.program_id(0)
    _, rows, cols, cout = out_ref.shape
    width = src_ref.shape[3]
    pixels = rows * cols
    col = lax.broadcasted_iota(jnp.int32, (rows, cols, cout), 1).reshape(pixels, cout)
    ext = jnp.concatenate([before_ref[0], src_ref[0], after_ref[0]], axis=0)
    lhs = jnp.concatenate([ext[dy : dy + rows].reshape(pixels, width) for dy in range(3)], axis=1)
    stacks = []
    for col_tap in range(3):
        taps = [k_ref[3 * (2 - dy + band * (2 * dy - 2)) + 2 - col_tap] for dy in range(3)]
        stacks.append(jnp.concatenate(taps, axis=1))
    joined = lax.dot_general(
        lhs, jnp.concatenate(stacks, axis=0), (((1,), (1,)), ((), ())), preferred_element_type=jnp.float32
    )
    z_left, z_mid, z_right = [joined[:, i * cout : (i + 1) * cout] for i in range(3)]
    from_left = jnp.where(col == 0, 0.0, pltpu.roll(z_left, 1, 0))
    from_right = jnp.where(col == cols - 1, 0.0, pltpu.roll(z_right, pixels - 1, 0))
    out_ref[0] = (z_mid + from_left + from_right).reshape(rows, cols, cout)
    margin_ref[0, 0] = z_right.reshape(rows, cols, cout)[:, 0, :]
    margin_ref[0, 1] = z_left.reshape(rows, cols, cout)[:, cols - 1, :]


def conv_back(pieces, first, width, kernel):
    source, before, after = pieces
    bands, rows, cols, _ = source.shape
    cout = kernel.shape[1]
    block = first // width
    return pl.pallas_call(
        back_kernel,
        grid=(bands,),
        in_specs=[
            pl.BlockSpec((1, rows, cols, width), lambda b: (b, 0, 0, block)),
            pl.BlockSpec((1, 1, cols, width), lambda b: (b, 0, 0, block)),
            pl.BlockSpec((1, 1, cols, width), lambda b: (b, 0, 0, block)),
            pl.BlockSpec(kernel.shape, lambda b: (0, 0, 0)),
        ],
        out_specs=[
            pl.BlockSpec((1, rows, cols, cout), lambda b: (b, 0, 0, 0)),
            pl.BlockSpec((1, 2, rows, cout), lambda b: (b, 0, 0, 0)),
        ],
        out_shape=[
            jax.ShapeDtypeStruct((bands, rows, cols, cout), jnp.float32),
            jax.ShapeDtypeStruct((bands, 2, rows, cout), jnp.float32),
        ],
        compiler_params=pltpu.CompilerParams(vmem_limit_bytes=60 * 1024 * 1024),
    )(source, before, after, kernel)


def conv_gather_kernel(count, block_ref, src_ref, before_ref, after_ref, k_ref, *rest):
    if len(rest) == 7:
        values_ref, pixels_ref = rest[:2]
        rest = rest[2:]
    else:
        values_ref = None
    out_ref, gathered_ref, landed, send_sems, recv_sems = rest
    step_at = pl.program_id(0)
    face = lax.axis_index("face")
    tile = lax.axis_index("tile")
    copies = []
    for step in range(1, count):
        peer = lax.rem(face + step, count)
        copies.append(
            pltpu.make_async_remote_copy(
                src_ref=block_ref,
                dst_ref=landed.at[step],
                send_sem=send_sems.at[step],
                recv_sem=recv_sems.at[step],
                device_id=(peer, tile),
                device_id_type=MESH_IDS,
            )
        )

    @pl.when(step_at == 0)
    def _():
        barrier = pltpu.get_barrier_semaphore()
        for step in range(1, count):
            peer = lax.rem(face + step, count)
            pl.semaphore_signal(barrier, inc=1, device_id=(peer, tile), device_id_type=MESH_IDS)
        pl.semaphore_wait(barrier, count - 1)
        for copy in copies:
            copy.start()
        gathered_ref[0] = block_ref[...]

    _, rows, cols, cout = out_ref.shape
    width = src_ref.shape[3]
    pixels = rows * cols
    col = lax.broadcasted_iota(jnp.int32, (rows, cols, cout), 1).reshape(pixels, cout)
    ext = jnp.concatenate([before_ref[0], src_ref[0], after_ref[0]], axis=0)
    lhs = jnp.concatenate([ext[dy : dy + rows].reshape(pixels, width) for dy in range(3)], axis=1)
    stacks = []
    for col_tap in range(3):
        taps = [k_ref[3 * (dy + step_at * (2 - 2 * dy)) + col_tap] for dy in range(3)]
        stacks.append(jnp.concatenate(taps, axis=0))
    joined = jnp.dot(lhs, jnp.concatenate(stacks, axis=1), preferred_element_type=jnp.float32)
    z_left, z_mid, z_right = [joined[:, i * cout : (i + 1) * cout] for i in range(3)]
    from_left = jnp.where(col == 0, 0.0, pltpu.roll(z_left, 1, 0))
    from_right = jnp.where(col == cols - 1, 0.0, pltpu.roll(z_right, pixels - 1, 0))
    total = z_mid + from_left + from_right
    if values_ref is not None:
        slots = values_ref.shape[0]
        chunk = 512
        pixel_ids = step_at * pixels + lax.broadcasted_iota(jnp.int32, (pixels, chunk), 0)
        for start in range(0, slots, chunk):
            hits = pixel_ids == pixels_ref[:, start : start + chunk]
            onehot = jnp.where(hits, 1.0, 0.0).astype(jnp.bfloat16)
            total = total + jnp.dot(
                onehot, values_ref[start : start + chunk], preferred_element_type=jnp.float32
            )
    out_ref[0] = total.reshape(rows, cols, cout)

    @pl.when(step_at == pl.num_programs(0) - 1)
    def _():
        for copy in copies:
            copy.wait()
        for step in range(1, count):
            gathered_ref[step] = landed[step]


def conv_gather(pieces, first, width, block, kernel, gather_id, observed=None):
    source, before, after = pieces
    extra_specs = []
    extra_args = ()
    if observed is not None:
        extra_specs = [
            pl.BlockSpec(observed[0].shape, lambda b: (0, 0)),
            pl.BlockSpec(observed[1].shape, lambda b: (0, 0)),
        ]
        extra_args = observed
    bands, rows, cols, _ = source.shape
    cout = kernel.shape[2]
    count = lax.axis_size("face")
    block_rows, lanes = block.shape
    lane_block = first // width
    return pl.pallas_call(
        functools.partial(conv_gather_kernel, count),
        grid=(bands,),
        in_specs=[
            pl.BlockSpec((block_rows, lanes), lambda b: (0, 0)),
            pl.BlockSpec((1, rows, cols, width), lambda b: (b, 0, 0, lane_block)),
            pl.BlockSpec((1, 1, cols, width), lambda b: (b, 0, 0, lane_block)),
            pl.BlockSpec((1, 1, cols, width), lambda b: (b, 0, 0, lane_block)),
            pl.BlockSpec(kernel.shape, lambda b: (0, 0, 0)),
        ]
        + extra_specs,
        out_specs=[
            pl.BlockSpec((1, rows, cols, cout), lambda b: (b, 0, 0, 0)),
            pl.BlockSpec((count, block_rows, lanes), lambda b: (0, 0, 0)),
        ],
        out_shape=[
            jax.ShapeDtypeStruct((bands, rows, cols, cout), jnp.float32),
            jax.ShapeDtypeStruct((count, block_rows, lanes), block.dtype),
        ],
        scratch_shapes=[
            pltpu.VMEM((count, block_rows, lanes), block.dtype),
            pltpu.SemaphoreType.DMA((count,)),
            pltpu.SemaphoreType.DMA((count,)),
        ],
        compiler_params=pltpu.CompilerParams(
            collective_id=gather_id, has_side_effects=True, vmem_limit_bytes=60 * 1024 * 1024
        ),
    )(block, source, before, after, kernel, *extra_args)


def side_terms(sides, kernel):
    bands, _, ext_rows, width = sides.shape
    rows = ext_rows - 2
    terms = []
    for band in range(bands):
        per_side = []
        for side, col_tap in ((0, 0), (1, 2)):
            stacked = jnp.concatenate([sides[band, side, dy : dy + rows] for dy in range(3)], axis=1)
            weights = jnp.concatenate(
                [kernel[tap_index(band, dy, col_tap, False)] for dy in range(3)], axis=0
            )
            per_side.append(jnp.dot(stacked, weights, preferred_element_type=jnp.float32))
        terms.append(jnp.stack(per_side))
    return jnp.stack(terms)


def at_edges(field, left_add, right_add):
    cols = field.shape[2]
    col = lax.broadcasted_iota(jnp.int32, field.shape, 2)
    return field + jnp.where(col == 0, left_add[:, :, None], 0.0) + jnp.where(
        col == cols - 1, right_add[:, :, None], 0.0
    )


def extend_rows(source, last_tile):
    count = lax.axis_size("tile")
    band_rows = source.shape[1]
    head = source[:, 0:1]
    tail = source[:, band_rows - 1 : band_rows]
    before = lax.ppermute(tail, "tile", [(i, i + 1) for i in range(count - 1)])
    after = lax.ppermute(head, "tile", [(i + 1, i) for i in range(count - 1)])
    after = jnp.where(last_tile, tail[::-1], after)
    return source, before, after


def edge_cols(pieces, first, width):
    extended = jnp.concatenate([piece[..., first : first + width] for piece in (pieces[1], pieces[0], pieces[2])], axis=1)
    return jnp.stack([extended[:, :, 0], extended[:, :, -1]], axis=2)


def pick_partner(gathered, matching_row):
    picked_sides = []
    for side_number in range(2):
        partner = matching_row[side_number, 0]
        their_side = matching_row[side_number, 1]
        flipped = matching_row[side_number, 2]
        chosen = lax.dynamic_index_in_dim(gathered, partner, 0, keepdims=False)
        column = jnp.where(their_side == 0, chosen[:, :, 0], chosen[:, :, 1])
        column = jnp.where(flipped == 1, column[::-1], column)
        picked_sides.append(column)
    return picked_sides


def pack_parts(parts):
    flat = jnp.concatenate([part.astype(jnp.float32).reshape(-1) for part in parts])
    return flat.reshape(-1, 128)


def unpack_parts(landed, parts):
    face_count = lax.axis_size("face")
    face_at = lax.axis_index("face")
    landed = landed.reshape(face_count, -1)
    slot_of_face = lax.rem(face_at - lax.iota(jnp.int32, face_count) + face_count, face_count)
    gathered = jnp.take(landed, slot_of_face, axis=0)
    pieces = []
    offset = 0
    for part in parts:
        size = part.size
        piece = gathered[:, offset : offset + size].reshape((face_count,) + part.shape)
        pieces.append(piece)
        offset += size
    return pieces


def side_columns(gathered_edges, matching_row):
    left_side, right_side = pick_partner(gathered_edges, matching_row)
    return jnp.stack([left_side, right_side], axis=1).astype(jnp.bfloat16)


def add_ends(field, first_add, last_add, axis):
    length = field.shape[axis]
    head = lax.slice_in_dim(field, 0, 1, axis=axis) + jnp.expand_dims(first_add, axis)
    middle = lax.slice_in_dim(field, 1, length - 1, axis=axis)
    tail = lax.slice_in_dim(field, length - 1, length, axis=axis) + jnp.expand_dims(last_add, axis)
    return jnp.concatenate([head, middle, tail], axis=axis)


def return_sides(inside, gathered_margins, matching_row):
    left_back, right_back = pick_partner(gathered_margins, matching_row)
    return at_edges(inside, left_back, right_back)


def route_observations(obs_values, obs_dest, obs_pixel, device_count):
    obs_rows = obs_values.shape[0]
    obs_width = obs_values.shape[1]
    capacity = 2 * obs_rows // device_count
    target = obs_dest[:, 0]
    positions = lax.iota(jnp.int32, obs_rows)
    same_target = (target[:, None] == target[None, :]) & (positions[None, :] < positions[:, None])
    rank_within = jnp.sum(same_target.astype(jnp.int32), axis=1)
    slot_index = target * capacity + rank_within
    slot_ids = lax.iota(jnp.int32, device_count * capacity)
    hits = slot_ids[:, None] == slot_index[None, :]
    value_slots = jnp.dot(
        hits.astype(jnp.bfloat16), obs_values, preferred_element_type=jnp.float32
    ).astype(jnp.bfloat16)
    pixel_slots = jnp.sum(jnp.where(hits, obs_pixel[None, :], 0), axis=1)
    high = (pixel_slots // 16).astype(jnp.bfloat16).reshape(device_count, capacity)
    low = (pixel_slots % 16).astype(jnp.bfloat16).reshape(device_count, capacity)
    pixel_row = jnp.concatenate(
        [high, low, jnp.zeros((device_count, obs_width - 2 * capacity), jnp.bfloat16)], axis=1
    )
    payload = jnp.concatenate(
        [value_slots.reshape(device_count, capacity, obs_width), pixel_row[:, None]], axis=1
    )
    arrived = lax.all_to_all(payload, ("face", "tile"), split_axis=0, concat_axis=0, tiled=True)
    got_values = arrived[:, :capacity].reshape(-1, obs_width)
    got_high = arrived[:, capacity, 0:capacity].astype(jnp.int32)
    got_low = arrived[:, capacity, capacity : 2 * capacity].astype(jnp.int32)
    got_pixels = (got_high * 16 + got_low).reshape(-1)
    return got_values, got_pixels


def per_device(
    state,
    obs_values,
    obs_dest,
    obs_pixel,
    matching,
    kernel_one,
    bias_one,
    kernel_two,
    bias_two,
    cotangent,
):
    base_field = state[0, 0]
    cot_field = cotangent[0, 0]
    band_rows = base_field.shape[1]
    column_count = base_field.shape[2]
    channels = base_field.shape[3]
    tile_count = lax.axis_size("tile")
    face_count = lax.axis_size("face")
    tile_at = lax.axis_index("tile")
    face_at = lax.axis_index("face")
    device_count = tile_count * face_count
    obs_width = obs_values.shape[1]

    got_values, got_pixels = route_observations(obs_values, obs_dest, obs_pixel, device_count)

    last_tile = tile_at == tile_count - 1
    matching_row = lax.dynamic_index_in_dim(matching, face_at, 0, keepdims=False)

    lifted = kernel_one.shape[2]
    fields, got_values = lax.optimization_barrier(
        (jnp.concatenate([base_field, cot_field], axis=3), got_values)
    )
    both = extend_rows(fields, last_tile)
    cot_back, cot_margins = conv_back(both, channels, channels, kernel_two)
    parts = [edge_cols(both, 0, channels), jnp.swapaxes(cot_margins, 1, 2)]
    first_out, landed = conv_gather(
        both, 0, channels, pack_parts(parts), kernel_one, 0, (got_values, got_pixels.reshape(1, -1))
    )
    base_edges, cot_gathered = unpack_parts(landed, parts)
    first_sides = side_terms(side_columns(base_edges, matching_row), kernel_one)

    pre_act = at_edges(first_out, first_sides[:, 0], first_sides[:, 1]) + bias_one
    inner = activation(pre_act).astype(jnp.bfloat16)
    grad_inner = return_sides(cot_back, cot_gathered, matching_row)
    grad_pre = jax.vjp(activation, pre_act)[1](grad_inner)[0].astype(jnp.bfloat16)

    pair = extend_rows(jnp.concatenate([inner, grad_pre], axis=3), last_tile)
    pre_back, pre_margins = conv_back(pair, lifted, lifted, kernel_one)
    parts = [edge_cols(pair, 0, lifted), jnp.swapaxes(pre_margins, 1, 2)]
    second_out, landed = conv_gather(pair, 0, lifted, pack_parts(parts), kernel_two, 1)
    inner_edges, pre_gathered = unpack_parts(landed, parts)
    second_sides = side_terms(side_columns(inner_edges, matching_row), kernel_two)

    second_out = at_edges(second_out, second_sides[:, 0], second_sides[:, 1])
    analysis = (base_field.astype(jnp.float32) + second_out + bias_two).astype(jnp.bfloat16)
    grad_base = cot_field.astype(jnp.float32) + return_sides(pre_back, pre_gathered, matching_row)
    return (analysis[None, None], grad_base[None, None])


def solution(mesh):
    return jax.shard_map(
        per_device,
        mesh=mesh,
        in_specs=(
            P("face", "tile", None, None, None, None),
            P(("face", "tile"), None),
            P(("face", "tile"), None),
            P(("face", "tile")),
            P(),
            P(),
            P(),
            P(),
            P(),
            P("face", "tile", None, None, None, None),
        ),
        out_specs=(
            P("face", "tile", None, None, None, None),
            P("face", "tile", None, None, None, None),
        ),
        check_vma=False,
    )
```

```python
import functools

import jax
import jax.numpy as jnp
from jax import lax
from jax.experimental import pallas as pl
from jax.experimental.pallas import tpu as pltpu
from jax.sharding import PartitionSpec as P

MESH_IDS = pl.DeviceIdType.MESH


def activation(values):
    return jax.nn.gelu(values, approximate=True)


def tap_index(band, row_tap, col_tap, backward):
    if backward:
        row = 2 - row_tap if band == 0 else row_tap
        return 3 * row + 2 - col_tap
    row = row_tap if band == 0 else 2 - row_tap
    return 3 * row + col_tap


def conv_kernel(backward, first, width, src_ref, before_ref, after_ref, side_ref, k_ref, out_ref, margin_ref):
    bands, rows, cols, cout = out_ref.shape
    pixels = rows * cols
    lanes = slice(first, first + width)
    col = lax.broadcasted_iota(jnp.int32, (rows, cols, cout), 1).reshape(pixels, cout)
    for band in range(bands):
        ext = jnp.concatenate(
            [before_ref[band, :, :, lanes], src_ref[band, :, :, lanes], after_ref[band, :, :, lanes]],
            axis=0,
        )
        lhs = jnp.concatenate(
            [ext[dy : dy + rows].reshape(pixels, width) for dy in range(3)], axis=1
        )
        stacks = []
        for col_tap in range(3):
            taps = [k_ref[tap_index(band, dy, col_tap, backward)] for dy in range(3)]
            if backward:
                stacks.append(jnp.concatenate(taps, axis=1))
            else:
                stacks.append(jnp.concatenate(taps, axis=0))

        def product(values, stack):
            if backward:
                return lax.dot_general(
                    values, stack, (((1,), (1,)), ((), ())), preferred_element_type=jnp.float32
                )
            return jnp.dot(values, stack, preferred_element_type=jnp.float32)

        z_left = product(lhs, stacks[0])
        z_mid = product(lhs, stacks[1])
        z_right = product(lhs, stacks[2])
        if backward or side_ref is None:
            left_full = jnp.zeros((pixels, cout), jnp.float32)
            right_full = left_full
        else:
            sides = side_ref[band]
            left = jnp.concatenate([sides[0, dy : dy + rows] for dy in range(3)], axis=1)
            right = jnp.concatenate([sides[1, dy : dy + rows] for dy in range(3)], axis=1)
            left_term = product(left, stacks[0])
            right_term = product(right, stacks[2])
            left_full = jnp.broadcast_to(left_term[:, None, :], (rows, cols, cout)).reshape(pixels, cout)
            right_full = jnp.broadcast_to(right_term[:, None, :], (rows, cols, cout)).reshape(pixels, cout)
        from_left = jnp.where(col == 0, left_full, pltpu.roll(z_left, 1, 0))
        from_right = jnp.where(col == cols - 1, right_full, pltpu.roll(z_right, pixels - 1, 0))
        out_ref[band] = (z_mid + from_left + from_right).reshape(rows, cols, cout)
        if backward:
            margin_ref[band, 0] = z_right.reshape(rows, cols, cout)[:, 0, :]
            margin_ref[band, 1] = z_left.reshape(rows, cols, cout)[:, cols - 1, :]


def conv_pallas(pieces, first, width, sides, kernel, backward):
    source, before, after = pieces
    bands, rows, cols, _ = source.shape
    cout = kernel.shape[1] if backward else kernel.shape[2]
    if sides is None:
        sides = jnp.zeros((bands, 2, rows + 2, width), jnp.bfloat16)
    vmem = pl.BlockSpec(memory_space=pltpu.VMEM)
    out, margins = pl.pallas_call(
        functools.partial(conv_kernel, backward, first, width),
        in_specs=[vmem] * 5,
        out_specs=[vmem, vmem],
        out_shape=[
            jax.ShapeDtypeStruct((bands, rows, cols, cout), jnp.float32),
            jax.ShapeDtypeStruct((bands, 2, rows, cout), jnp.float32),
        ],
        compiler_params=pltpu.CompilerParams(vmem_limit_bytes=60 * 1024 * 1024),
    )(source, before, after, sides, kernel)
    return out, margins


def back_kernel(src_ref, before_ref, after_ref, k_ref, out_ref, margin_ref):
    band = pl.program_id(0)
    _, rows, cols, cout = out_ref.shape
    width = src_ref.shape[3]
    pixels = rows * cols
    col = lax.broadcasted_iota(jnp.int32, (rows, cols, cout), 1).reshape(pixels, cout)
    ext = jnp.concatenate([before_ref[0], src_ref[0], after_ref[0]], axis=0)
    lhs = jnp.concatenate([ext[dy : dy + rows].reshape(pixels, width) for dy in range(3)], axis=1)
    stacks = []
    for col_tap in range(3):
        taps = [k_ref[3 * (2 - dy + band * (2 * dy - 2)) + 2 - col_tap] for dy in range(3)]
        stacks.append(jnp.concatenate(taps, axis=1))
    joined = lax.dot_general(
        lhs, jnp.concatenate(stacks, axis=0), (((1,), (1,)), ((), ())), preferred_element_type=jnp.float32
    )
    z_left, z_mid, z_right = [joined[:, i * cout : (i + 1) * cout] for i in range(3)]
    from_left = jnp.where(col == 0, 0.0, pltpu.roll(z_left, 1, 0))
    from_right = jnp.where(col == cols - 1, 0.0, pltpu.roll(z_right, pixels - 1, 0))
    out_ref[0] = (z_mid + from_left + from_right).reshape(rows, cols, cout)
    margin_ref[0, 0] = z_right.reshape(rows, cols, cout)[:, 0, :]
    margin_ref[0, 1] = z_left.reshape(rows, cols, cout)[:, cols - 1, :]


def conv_back(pieces, first, width, kernel):
    source, before, after = pieces
    bands, rows, cols, _ = source.shape
    cout = kernel.shape[1]
    block = first // width
    return pl.pallas_call(
        back_kernel,
        grid=(bands,),
        in_specs=[
            pl.BlockSpec((1, rows, cols, width), lambda b: (b, 0, 0, block)),
            pl.BlockSpec((1, 1, cols, width), lambda b: (b, 0, 0, block)),
            pl.BlockSpec((1, 1, cols, width), lambda b: (b, 0, 0, block)),
            pl.BlockSpec(kernel.shape, lambda b: (0, 0, 0)),
        ],
        out_specs=[
            pl.BlockSpec((1, rows, cols, cout), lambda b: (b, 0, 0, 0)),
            pl.BlockSpec((1, 2, rows, cout), lambda b: (b, 0, 0, 0)),
        ],
        out_shape=[
            jax.ShapeDtypeStruct((bands, rows, cols, cout), jnp.float32),
            jax.ShapeDtypeStruct((bands, 2, rows, cout), jnp.float32),
        ],
        compiler_params=pltpu.CompilerParams(vmem_limit_bytes=60 * 1024 * 1024),
    )(source, before, after, kernel)


def conv_gather_kernel(count, block_ref, src_ref, before_ref, after_ref, k_ref, *rest):
    if len(rest) == 7:
        values_ref, pixels_ref = rest[:2]
        rest = rest[2:]
    else:
        values_ref = None
    out_ref, gathered_ref, landed, send_sems, recv_sems = rest
    step_at = pl.program_id(0)
    face = lax.axis_index("face")
    tile = lax.axis_index("tile")
    copies = []
    for step in range(1, count):
        peer = lax.rem(face + step, count)
        copies.append(
            pltpu.make_async_remote_copy(
                src_ref=block_ref,
                dst_ref=landed.at[step],
                send_sem=send_sems.at[step],
                recv_sem=recv_sems.at[step],
                device_id=(peer, tile),
                device_id_type=MESH_IDS,
            )
        )

    @pl.when(step_at == 0)
    def _():
        barrier = pltpu.get_barrier_semaphore()
        for step in range(1, count):
            peer = lax.rem(face + step, count)
            pl.semaphore_signal(barrier, inc=1, device_id=(peer, tile), device_id_type=MESH_IDS)
        pl.semaphore_wait(barrier, count - 1)
        for copy in copies:
            copy.start()
        gathered_ref[0] = block_ref[...]

    _, rows, cols, cout = out_ref.shape
    width = src_ref.shape[3]
    pixels = rows * cols
    col = lax.broadcasted_iota(jnp.int32, (rows, cols, cout), 1).reshape(pixels, cout)
    ext = jnp.concatenate([before_ref[0], src_ref[0], after_ref[0]], axis=0)
    lhs = jnp.concatenate([ext[dy : dy + rows].reshape(pixels, width) for dy in range(3)], axis=1)
    stacks = []
    for col_tap in range(3):
        taps = [k_ref[3 * (dy + step_at * (2 - 2 * dy)) + col_tap] for dy in range(3)]
        stacks.append(jnp.concatenate(taps, axis=0))
    joined = jnp.dot(lhs, jnp.concatenate(stacks, axis=1), preferred_element_type=jnp.float32)
    z_left, z_mid, z_right = [joined[:, i * cout : (i + 1) * cout] for i in range(3)]
    from_left = jnp.where(col == 0, 0.0, pltpu.roll(z_left, 1, 0))
    from_right = jnp.where(col == cols - 1, 0.0, pltpu.roll(z_right, pixels - 1, 0))
    total = z_mid + from_left + from_right
    if values_ref is not None:
        slots = values_ref.shape[0]
        chunk = 512
        pixel_ids = step_at * pixels + lax.broadcasted_iota(jnp.int32, (pixels, chunk), 0)
        for start in range(0, slots, chunk):
            hits = pixel_ids == pixels_ref[:, start : start + chunk]
            onehot = jnp.where(hits, 1.0, 0.0).astype(jnp.bfloat16)
            total = total + jnp.dot(
                onehot, values_ref[start : start + chunk], preferred_element_type=jnp.float32
            )
    out_ref[0] = total.reshape(rows, cols, cout)

    @pl.when(step_at == pl.num_programs(0) - 1)
    def _():
        for copy in copies:
            copy.wait()
        for step in range(1, count):
            gathered_ref[step] = landed[step]


def conv_gather(pieces, first, width, block, kernel, gather_id, observed=None):
    source, before, after = pieces
    extra_specs = []
    extra_args = ()
    if observed is not None:
        extra_specs = [
            pl.BlockSpec(observed[0].shape, lambda b: (0, 0)),
            pl.BlockSpec(observed[1].shape, lambda b: (0, 0)),
        ]
        extra_args = observed
    bands, rows, cols, _ = source.shape
    cout = kernel.shape[2]
    count = lax.axis_size("face")
    block_rows, lanes = block.shape
    lane_block = first // width
    return pl.pallas_call(
        functools.partial(conv_gather_kernel, count),
        grid=(bands,),
        in_specs=[
            pl.BlockSpec((block_rows, lanes), lambda b: (0, 0)),
            pl.BlockSpec((1, rows, cols, width), lambda b: (b, 0, 0, lane_block)),
            pl.BlockSpec((1, 1, cols, width), lambda b: (b, 0, 0, lane_block)),
            pl.BlockSpec((1, 1, cols, width), lambda b: (b, 0, 0, lane_block)),
            pl.BlockSpec(kernel.shape, lambda b: (0, 0, 0)),
        ]
        + extra_specs,
        out_specs=[
            pl.BlockSpec((1, rows, cols, cout), lambda b: (b, 0, 0, 0)),
            pl.BlockSpec((count, block_rows, lanes), lambda b: (0, 0, 0)),
        ],
        out_shape=[
            jax.ShapeDtypeStruct((bands, rows, cols, cout), jnp.float32),
            jax.ShapeDtypeStruct((count, block_rows, lanes), block.dtype),
        ],
        scratch_shapes=[
            pltpu.VMEM((count, block_rows, lanes), block.dtype),
            pltpu.SemaphoreType.DMA((count,)),
            pltpu.SemaphoreType.DMA((count,)),
        ],
        compiler_params=pltpu.CompilerParams(
            collective_id=gather_id, has_side_effects=True, vmem_limit_bytes=60 * 1024 * 1024
        ),
    )(block, source, before, after, kernel, *extra_args)


def side_terms(sides, kernel):
    bands, _, ext_rows, width = sides.shape
    rows = ext_rows - 2
    terms = []
    for band in range(bands):
        per_side = []
        for side, col_tap in ((0, 0), (1, 2)):
            stacked = jnp.concatenate([sides[band, side, dy : dy + rows] for dy in range(3)], axis=1)
            weights = jnp.concatenate(
                [kernel[tap_index(band, dy, col_tap, False)] for dy in range(3)], axis=0
            )
            per_side.append(jnp.dot(stacked, weights, preferred_element_type=jnp.float32))
        terms.append(jnp.stack(per_side))
    return jnp.stack(terms)


def at_edges(field, left_add, right_add):
    cols = field.shape[2]
    col = lax.broadcasted_iota(jnp.int32, field.shape, 2)
    return field + jnp.where(col == 0, left_add[:, :, None], 0.0) + jnp.where(
        col == cols - 1, right_add[:, :, None], 0.0
    )


def extend_rows(source, last_tile):
    count = lax.axis_size("tile")
    band_rows = source.shape[1]
    head = source[:, 0:1]
    tail = source[:, band_rows - 1 : band_rows]
    before = lax.ppermute(tail, "tile", [(i, i + 1) for i in range(count - 1)])
    after = lax.ppermute(head, "tile", [(i + 1, i) for i in range(count - 1)])
    after = jnp.where(last_tile, tail[::-1], after)
    return source, before, after


def edge_cols(pieces, first, width):
    extended = jnp.concatenate([piece[..., first : first + width] for piece in (pieces[1], pieces[0], pieces[2])], axis=1)
    return jnp.stack([extended[:, :, 0], extended[:, :, -1]], axis=2)


def pick_partner(gathered, matching_row):
    picked_sides = []
    for side_number in range(2):
        partner = matching_row[side_number, 0]
        their_side = matching_row[side_number, 1]
        flipped = matching_row[side_number, 2]
        chosen = lax.dynamic_index_in_dim(gathered, partner, 0, keepdims=False)
        column = jnp.where(their_side == 0, chosen[:, :, 0], chosen[:, :, 1])
        column = jnp.where(flipped == 1, column[::-1], column)
        picked_sides.append(column)
    return picked_sides


def pack_parts(parts):
    flat = jnp.concatenate([part.astype(jnp.float32).reshape(-1) for part in parts])
    return flat.reshape(-1, 128)


def unpack_parts(landed, parts):
    face_count = lax.axis_size("face")
    face_at = lax.axis_index("face")
    landed = landed.reshape(face_count, -1)
    slot_of_face = lax.rem(face_at - lax.iota(jnp.int32, face_count) + face_count, face_count)
    gathered = jnp.take(landed, slot_of_face, axis=0)
    pieces = []
    offset = 0
    for part in parts:
        size = part.size
        piece = gathered[:, offset : offset + size].reshape((face_count,) + part.shape)
        pieces.append(piece)
        offset += size
    return pieces


def side_columns(gathered_edges, matching_row):
    left_side, right_side = pick_partner(gathered_edges, matching_row)
    return jnp.stack([left_side, right_side], axis=1).astype(jnp.bfloat16)


def add_ends(field, first_add, last_add, axis):
    length = field.shape[axis]
    head = lax.slice_in_dim(field, 0, 1, axis=axis) + jnp.expand_dims(first_add, axis)
    middle = lax.slice_in_dim(field, 1, length - 1, axis=axis)
    tail = lax.slice_in_dim(field, length - 1, length, axis=axis) + jnp.expand_dims(last_add, axis)
    return jnp.concatenate([head, middle, tail], axis=axis)


def return_sides(inside, gathered_margins, matching_row):
    left_back, right_back = pick_partner(gathered_margins, matching_row)
    return at_edges(inside, left_back, right_back)


def route_observations(obs_values, obs_dest, obs_pixel, device_count):
    obs_rows = obs_values.shape[0]
    obs_width = obs_values.shape[1]
    capacity = 2 * obs_rows // device_count
    target = obs_dest[:, 0]
    positions = lax.iota(jnp.int32, obs_rows)
    same_target = (target[:, None] == target[None, :]) & (positions[None, :] < positions[:, None])
    rank_within = jnp.sum(same_target.astype(jnp.int32), axis=1)
    slot_index = target * capacity + rank_within
    slot_ids = lax.iota(jnp.int32, device_count * capacity)
    hits = slot_ids[:, None] == slot_index[None, :]
    value_slots = jnp.dot(
        hits.astype(jnp.bfloat16), obs_values, preferred_element_type=jnp.float32
    ).astype(jnp.bfloat16)
    pixel_slots = jnp.sum(jnp.where(hits, obs_pixel[None, :], 0), axis=1)
    high = (pixel_slots // 16).astype(jnp.bfloat16).reshape(device_count, capacity)
    low = (pixel_slots % 16).astype(jnp.bfloat16).reshape(device_count, capacity)
    pixel_row = jnp.concatenate(
        [high, low, jnp.zeros((device_count, obs_width - 2 * capacity), jnp.bfloat16)], axis=1
    )
    payload = jnp.concatenate(
        [value_slots.reshape(device_count, capacity, obs_width), pixel_row[:, None]], axis=1
    )
    arrived = lax.all_to_all(payload, ("face", "tile"), split_axis=0, concat_axis=0, tiled=True)
    got_values = arrived[:, :capacity].reshape(-1, obs_width)
    got_high = arrived[:, capacity, 0:capacity].astype(jnp.int32)
    got_low = arrived[:, capacity, capacity : 2 * capacity].astype(jnp.int32)
    got_pixels = (got_high * 16 + got_low).reshape(-1)
    return got_values, got_pixels


def per_device(
    state,
    obs_values,
    obs_dest,
    obs_pixel,
    matching,
    kernel_one,
    bias_one,
    kernel_two,
    bias_two,
    cotangent,
):
    base_field = state[0, 0]
    cot_field = cotangent[0, 0]
    band_rows = base_field.shape[1]
    column_count = base_field.shape[2]
    channels = base_field.shape[3]
    tile_count = lax.axis_size("tile")
    face_count = lax.axis_size("face")
    tile_at = lax.axis_index("tile")
    face_at = lax.axis_index("face")
    device_count = tile_count * face_count
    obs_width = obs_values.shape[1]

    got_values, got_pixels = route_observations(obs_values, obs_dest, obs_pixel, device_count)

    last_tile = tile_at == tile_count - 1
    matching_row = lax.dynamic_index_in_dim(matching, face_at, 0, keepdims=False)

    lifted = kernel_one.shape[2]
    both = extend_rows(jnp.concatenate([base_field, cot_field], axis=3), last_tile)
    cot_back, cot_margins = conv_back(both, channels, channels, kernel_two)
    parts = [edge_cols(both, 0, channels), jnp.swapaxes(cot_margins, 1, 2)]
    first_out, landed = conv_gather(
        both, 0, channels, pack_parts(parts), kernel_one, 0, (got_values, got_pixels.reshape(1, -1))
    )
    base_edges, cot_gathered = unpack_parts(landed, parts)
    first_sides = side_terms(side_columns(base_edges, matching_row), kernel_one)

    pre_act = at_edges(first_out, first_sides[:, 0], first_sides[:, 1]) + bias_one
    inner = activation(pre_act).astype(jnp.bfloat16)
    grad_inner = return_sides(cot_back, cot_gathered, matching_row)
    grad_pre = jax.vjp(activation, pre_act)[1](grad_inner)[0].astype(jnp.bfloat16)

    pair = extend_rows(jnp.concatenate([inner, grad_pre], axis=3), last_tile)
    pre_back, pre_margins = conv_back(pair, lifted, lifted, kernel_one)
    parts = [edge_cols(pair, 0, lifted), jnp.swapaxes(pre_margins, 1, 2)]
    second_out, landed = conv_gather(pair, 0, lifted, pack_parts(parts), kernel_two, 1)
    inner_edges, pre_gathered = unpack_parts(landed, parts)
    second_sides = side_terms(side_columns(inner_edges, matching_row), kernel_two)

    second_out = at_edges(second_out, second_sides[:, 0], second_sides[:, 1])
    analysis = (base_field.astype(jnp.float32) + second_out + bias_two).astype(jnp.bfloat16)
    grad_base = cot_field.astype(jnp.float32) + return_sides(pre_back, pre_gathered, matching_row)
    return (analysis[None, None], grad_base[None, None])


def solution(mesh):
    return jax.shard_map(
        per_device,
        mesh=mesh,
        in_specs=(
            P("face", "tile", None, None, None, None),
            P(("face", "tile"), None),
            P(("face", "tile"), None),
            P(("face", "tile")),
            P(),
            P(),
            P(),
            P(),
            P(),
            P("face", "tile", None, None, None, None),
        ),
        out_specs=(
            P("face", "tile", None, None, None, None),
            P("face", "tile", None, None, None, None),
        ),
        check_vma=False,
    )
```

```python
import functools

import jax
import jax.numpy as jnp
from jax import lax
from jax.experimental import pallas as pl
from jax.experimental.pallas import tpu as pltpu
from jax.sharding import PartitionSpec as P

MESH_IDS = pl.DeviceIdType.MESH


def activation(values):
    return jax.nn.gelu(values, approximate=True)


def tap_index(band, row_tap, col_tap, backward):
    if backward:
        row = 2 - row_tap if band == 0 else row_tap
        return 3 * row + 2 - col_tap
    row = row_tap if band == 0 else 2 - row_tap
    return 3 * row + col_tap


def conv_kernel(backward, first, width, src_ref, before_ref, after_ref, side_ref, k_ref, out_ref, margin_ref):
    bands, rows, cols, cout = out_ref.shape
    pixels = rows * cols
    lanes = slice(first, first + width)
    col = lax.broadcasted_iota(jnp.int32, (rows, cols, cout), 1).reshape(pixels, cout)
    for band in range(bands):
        ext = jnp.concatenate(
            [before_ref[band, :, :, lanes], src_ref[band, :, :, lanes], after_ref[band, :, :, lanes]],
            axis=0,
        )
        lhs = jnp.concatenate(
            [ext[dy : dy + rows].reshape(pixels, width) for dy in range(3)], axis=1
        )
        stacks = []
        for col_tap in range(3):
            taps = [k_ref[tap_index(band, dy, col_tap, backward)] for dy in range(3)]
            if backward:
                stacks.append(jnp.concatenate(taps, axis=1))
            else:
                stacks.append(jnp.concatenate(taps, axis=0))

        def product(values, stack):
            if backward:
                return lax.dot_general(
                    values, stack, (((1,), (1,)), ((), ())), preferred_element_type=jnp.float32
                )
            return jnp.dot(values, stack, preferred_element_type=jnp.float32)

        z_left = product(lhs, stacks[0])
        z_mid = product(lhs, stacks[1])
        z_right = product(lhs, stacks[2])
        if backward or side_ref is None:
            left_full = jnp.zeros((pixels, cout), jnp.float32)
            right_full = left_full
        else:
            sides = side_ref[band]
            left = jnp.concatenate([sides[0, dy : dy + rows] for dy in range(3)], axis=1)
            right = jnp.concatenate([sides[1, dy : dy + rows] for dy in range(3)], axis=1)
            left_term = product(left, stacks[0])
            right_term = product(right, stacks[2])
            left_full = jnp.broadcast_to(left_term[:, None, :], (rows, cols, cout)).reshape(pixels, cout)
            right_full = jnp.broadcast_to(right_term[:, None, :], (rows, cols, cout)).reshape(pixels, cout)
        from_left = jnp.where(col == 0, left_full, pltpu.roll(z_left, 1, 0))
        from_right = jnp.where(col == cols - 1, right_full, pltpu.roll(z_right, pixels - 1, 0))
        out_ref[band] = (z_mid + from_left + from_right).reshape(rows, cols, cout)
        if backward:
            margin_ref[band, 0] = z_right.reshape(rows, cols, cout)[:, 0, :]
            margin_ref[band, 1] = z_left.reshape(rows, cols, cout)[:, cols - 1, :]


def conv_pallas(pieces, first, width, sides, kernel, backward):
    source, before, after = pieces
    bands, rows, cols, _ = source.shape
    cout = kernel.shape[1] if backward else kernel.shape[2]
    if sides is None:
        sides = jnp.zeros((bands, 2, rows + 2, width), jnp.bfloat16)
    vmem = pl.BlockSpec(memory_space=pltpu.VMEM)
    out, margins = pl.pallas_call(
        functools.partial(conv_kernel, backward, first, width),
        in_specs=[vmem] * 5,
        out_specs=[vmem, vmem],
        out_shape=[
            jax.ShapeDtypeStruct((bands, rows, cols, cout), jnp.float32),
            jax.ShapeDtypeStruct((bands, 2, rows, cout), jnp.float32),
        ],
        compiler_params=pltpu.CompilerParams(vmem_limit_bytes=60 * 1024 * 1024),
    )(source, before, after, sides, kernel)
    return out, margins


def back_kernel(src_ref, before_ref, after_ref, k_ref, out_ref, margin_ref):
    band = pl.program_id(0)
    _, rows, cols, cout = out_ref.shape
    width = src_ref.shape[3]
    pixels = rows * cols
    col = lax.broadcasted_iota(jnp.int32, (rows, cols, cout), 1).reshape(pixels, cout)
    ext = jnp.concatenate([before_ref[0], src_ref[0], after_ref[0]], axis=0)
    lhs = jnp.concatenate([ext[dy : dy + rows].reshape(pixels, width) for dy in range(3)], axis=1)
    stacks = []
    for col_tap in range(3):
        taps = [k_ref[3 * (2 - dy + band * (2 * dy - 2)) + 2 - col_tap] for dy in range(3)]
        stacks.append(jnp.concatenate(taps, axis=1))
    joined = lax.dot_general(
        lhs, jnp.concatenate(stacks, axis=0), (((1,), (1,)), ((), ())), preferred_element_type=jnp.float32
    )
    z_left, z_mid, z_right = [joined[:, i * cout : (i + 1) * cout] for i in range(3)]
    from_left = jnp.where(col == 0, 0.0, pltpu.roll(z_left, 1, 0))
    from_right = jnp.where(col == cols - 1, 0.0, pltpu.roll(z_right, pixels - 1, 0))
    out_ref[0] = (z_mid + from_left + from_right).reshape(rows, cols, cout)
    margin_ref[0, 0] = z_right.reshape(rows, cols, cout)[:, 0, :]
    margin_ref[0, 1] = z_left.reshape(rows, cols, cout)[:, cols - 1, :]


def conv_back(pieces, first, width, kernel):
    source, before, after = pieces
    bands, rows, cols, _ = source.shape
    cout = kernel.shape[1]
    block = first // width
    return pl.pallas_call(
        back_kernel,
        grid=(bands,),
        in_specs=[
            pl.BlockSpec((1, rows, cols, width), lambda b: (b, 0, 0, block)),
            pl.BlockSpec((1, 1, cols, width), lambda b: (b, 0, 0, block)),
            pl.BlockSpec((1, 1, cols, width), lambda b: (b, 0, 0, block)),
            pl.BlockSpec(kernel.shape, lambda b: (0, 0, 0)),
        ],
        out_specs=[
            pl.BlockSpec((1, rows, cols, cout), lambda b: (b, 0, 0, 0)),
            pl.BlockSpec((1, 2, rows, cout), lambda b: (b, 0, 0, 0)),
        ],
        out_shape=[
            jax.ShapeDtypeStruct((bands, rows, cols, cout), jnp.float32),
            jax.ShapeDtypeStruct((bands, 2, rows, cout), jnp.float32),
        ],
        compiler_params=pltpu.CompilerParams(vmem_limit_bytes=60 * 1024 * 1024),
    )(source, before, after, kernel)


def conv_gather_kernel(count, block_ref, src_ref, before_ref, after_ref, k_ref,
                       out_ref, gathered_ref, landed, send_sems, recv_sems):
    step_at = pl.program_id(0)
    face = lax.axis_index("face")
    tile = lax.axis_index("tile")
    copies = []
    for step in range(1, count):
        peer = lax.rem(face + step, count)
        copies.append(
            pltpu.make_async_remote_copy(
                src_ref=block_ref,
                dst_ref=landed.at[step],
                send_sem=send_sems.at[step],
                recv_sem=recv_sems.at[step],
                device_id=(peer, tile),
                device_id_type=MESH_IDS,
            )
        )

    @pl.when(step_at == 0)
    def _():
        barrier = pltpu.get_barrier_semaphore()
        for step in range(1, count):
            peer = lax.rem(face + step, count)
            pl.semaphore_signal(barrier, inc=1, device_id=(peer, tile), device_id_type=MESH_IDS)
        pl.semaphore_wait(barrier, count - 1)
        for copy in copies:
            copy.start()
        gathered_ref[0] = block_ref[...]

    _, rows, cols, cout = out_ref.shape
    width = src_ref.shape[3]
    pixels = rows * cols
    col = lax.broadcasted_iota(jnp.int32, (rows, cols, cout), 1).reshape(pixels, cout)
    ext = jnp.concatenate([before_ref[0], src_ref[0], after_ref[0]], axis=0)
    lhs = jnp.concatenate([ext[dy : dy + rows].reshape(pixels, width) for dy in range(3)], axis=1)
    stacks = []
    for col_tap in range(3):
        taps = [k_ref[3 * (dy + step_at * (2 - 2 * dy)) + col_tap] for dy in range(3)]
        stacks.append(jnp.concatenate(taps, axis=0))
    joined = jnp.dot(lhs, jnp.concatenate(stacks, axis=1), preferred_element_type=jnp.float32)
    z_left, z_mid, z_right = [joined[:, i * cout : (i + 1) * cout] for i in range(3)]
    from_left = jnp.where(col == 0, 0.0, pltpu.roll(z_left, 1, 0))
    from_right = jnp.where(col == cols - 1, 0.0, pltpu.roll(z_right, pixels - 1, 0))
    out_ref[0] = (z_mid + from_left + from_right).reshape(rows, cols, cout)

    @pl.when(step_at == pl.num_programs(0) - 1)
    def _():
        for copy in copies:
            copy.wait()
        for step in range(1, count):
            gathered_ref[step] = landed[step]


def conv_gather(pieces, first, width, block, kernel, gather_id):
    source, before, after = pieces
    bands, rows, cols, _ = source.shape
    cout = kernel.shape[2]
    count = lax.axis_size("face")
    block_rows, lanes = block.shape
    lane_block = first // width
    return pl.pallas_call(
        functools.partial(conv_gather_kernel, count),
        grid=(bands,),
        in_specs=[
            pl.BlockSpec((block_rows, lanes), lambda b: (0, 0)),
            pl.BlockSpec((1, rows, cols, width), lambda b: (b, 0, 0, lane_block)),
            pl.BlockSpec((1, 1, cols, width), lambda b: (b, 0, 0, lane_block)),
            pl.BlockSpec((1, 1, cols, width), lambda b: (b, 0, 0, lane_block)),
            pl.BlockSpec(kernel.shape, lambda b: (0, 0, 0)),
        ],
        out_specs=[
            pl.BlockSpec((1, rows, cols, cout), lambda b: (b, 0, 0, 0)),
            pl.BlockSpec((count, block_rows, lanes), lambda b: (0, 0, 0)),
        ],
        out_shape=[
            jax.ShapeDtypeStruct((bands, rows, cols, cout), jnp.float32),
            jax.ShapeDtypeStruct((count, block_rows, lanes), block.dtype),
        ],
        scratch_shapes=[
            pltpu.VMEM((count, block_rows, lanes), block.dtype),
            pltpu.SemaphoreType.DMA((count,)),
            pltpu.SemaphoreType.DMA((count,)),
        ],
        compiler_params=pltpu.CompilerParams(
            collective_id=gather_id, has_side_effects=True, vmem_limit_bytes=60 * 1024 * 1024
        ),
    )(block, source, before, after, kernel)


def side_terms(sides, kernel):
    bands, _, ext_rows, width = sides.shape
    rows = ext_rows - 2
    terms = []
    for band in range(bands):
        per_side = []
        for side, col_tap in ((0, 0), (1, 2)):
            stacked = jnp.concatenate([sides[band, side, dy : dy + rows] for dy in range(3)], axis=1)
            weights = jnp.concatenate(
                [kernel[tap_index(band, dy, col_tap, False)] for dy in range(3)], axis=0
            )
            per_side.append(jnp.dot(stacked, weights, preferred_element_type=jnp.float32))
        terms.append(jnp.stack(per_side))
    return jnp.stack(terms)


def at_edges(field, left_add, right_add):
    cols = field.shape[2]
    col = lax.broadcasted_iota(jnp.int32, field.shape, 2)
    return field + jnp.where(col == 0, left_add[:, :, None], 0.0) + jnp.where(
        col == cols - 1, right_add[:, :, None], 0.0
    )


def extend_rows(source, last_tile):
    count = lax.axis_size("tile")
    band_rows = source.shape[1]
    head = source[:, 0:1]
    tail = source[:, band_rows - 1 : band_rows]
    before = lax.ppermute(tail, "tile", [(i, i + 1) for i in range(count - 1)])
    after = lax.ppermute(head, "tile", [(i + 1, i) for i in range(count - 1)])
    after = jnp.where(last_tile, tail[::-1], after)
    return source, before, after


def edge_cols(pieces, first, width):
    extended = jnp.concatenate([piece[..., first : first + width] for piece in (pieces[1], pieces[0], pieces[2])], axis=1)
    return jnp.stack([extended[:, :, 0], extended[:, :, -1]], axis=2)


def pick_partner(gathered, matching_row):
    picked_sides = []
    for side_number in range(2):
        partner = matching_row[side_number, 0]
        their_side = matching_row[side_number, 1]
        flipped = matching_row[side_number, 2]
        chosen = lax.dynamic_index_in_dim(gathered, partner, 0, keepdims=False)
        column = jnp.where(their_side == 0, chosen[:, :, 0], chosen[:, :, 1])
        column = jnp.where(flipped == 1, column[::-1], column)
        picked_sides.append(column)
    return picked_sides


def pack_parts(parts):
    flat = jnp.concatenate([part.astype(jnp.float32).reshape(-1) for part in parts])
    return flat.reshape(-1, 128)


def unpack_parts(landed, parts):
    face_count = lax.axis_size("face")
    face_at = lax.axis_index("face")
    landed = landed.reshape(face_count, -1)
    slot_of_face = lax.rem(face_at - lax.iota(jnp.int32, face_count) + face_count, face_count)
    gathered = jnp.take(landed, slot_of_face, axis=0)
    pieces = []
    offset = 0
    for part in parts:
        size = part.size
        piece = gathered[:, offset : offset + size].reshape((face_count,) + part.shape)
        pieces.append(piece)
        offset += size
    return pieces


def side_columns(gathered_edges, matching_row):
    left_side, right_side = pick_partner(gathered_edges, matching_row)
    return jnp.stack([left_side, right_side], axis=1).astype(jnp.bfloat16)


def add_ends(field, first_add, last_add, axis):
    length = field.shape[axis]
    head = lax.slice_in_dim(field, 0, 1, axis=axis) + jnp.expand_dims(first_add, axis)
    middle = lax.slice_in_dim(field, 1, length - 1, axis=axis)
    tail = lax.slice_in_dim(field, length - 1, length, axis=axis) + jnp.expand_dims(last_add, axis)
    return jnp.concatenate([head, middle, tail], axis=axis)


def return_sides(inside, gathered_margins, matching_row):
    left_back, right_back = pick_partner(gathered_margins, matching_row)
    return at_edges(inside, left_back, right_back)


def route_observations(obs_values, obs_dest, obs_pixel, device_count):
    obs_rows = obs_values.shape[0]
    obs_width = obs_values.shape[1]
    capacity = 2 * obs_rows // device_count
    target = obs_dest[:, 0]
    positions = lax.iota(jnp.int32, obs_rows)
    same_target = (target[:, None] == target[None, :]) & (positions[None, :] < positions[:, None])
    rank_within = jnp.sum(same_target.astype(jnp.int32), axis=1)
    slot_index = target * capacity + rank_within
    slot_ids = lax.iota(jnp.int32, device_count * capacity)
    hits = slot_ids[:, None] == slot_index[None, :]
    value_slots = jnp.dot(
        hits.astype(jnp.bfloat16), obs_values, preferred_element_type=jnp.float32
    ).astype(jnp.bfloat16)
    pixel_slots = jnp.sum(jnp.where(hits, obs_pixel[None, :], 0), axis=1)
    high = (pixel_slots // 16).astype(jnp.bfloat16).reshape(device_count, capacity)
    low = (pixel_slots % 16).astype(jnp.bfloat16).reshape(device_count, capacity)
    pixel_row = jnp.concatenate(
        [high, low, jnp.zeros((device_count, obs_width - 2 * capacity), jnp.bfloat16)], axis=1
    )
    payload = jnp.concatenate(
        [value_slots.reshape(device_count, capacity, obs_width), pixel_row[:, None]], axis=1
    )
    arrived = lax.all_to_all(payload, ("face", "tile"), split_axis=0, concat_axis=0, tiled=True)
    got_values = arrived[:, :capacity].reshape(-1, obs_width)
    got_high = arrived[:, capacity, 0:capacity].astype(jnp.int32)
    got_low = arrived[:, capacity, capacity : 2 * capacity].astype(jnp.int32)
    got_pixels = (got_high * 16 + got_low).reshape(-1)
    return got_values, got_pixels


def per_device(
    state,
    obs_values,
    obs_dest,
    obs_pixel,
    matching,
    kernel_one,
    bias_one,
    kernel_two,
    bias_two,
    cotangent,
):
    base_field = state[0, 0]
    cot_field = cotangent[0, 0]
    band_rows = base_field.shape[1]
    column_count = base_field.shape[2]
    channels = base_field.shape[3]
    tile_count = lax.axis_size("tile")
    face_count = lax.axis_size("face")
    tile_at = lax.axis_index("tile")
    face_at = lax.axis_index("face")
    device_count = tile_count * face_count
    obs_width = obs_values.shape[1]

    got_values, got_pixels = route_observations(obs_values, obs_dest, obs_pixel, device_count)
    pixel_count = 2 * band_rows * column_count
    pixel_ids = lax.iota(jnp.int32, pixel_count)
    onehot = (pixel_ids[:, None] == got_pixels[None, :]).astype(jnp.bfloat16)
    gridded = jnp.dot(onehot, got_values, preferred_element_type=jnp.float32)
    gridded = gridded.reshape(2, band_rows, column_count, obs_width)

    last_tile = tile_at == tile_count - 1
    matching_row = lax.dynamic_index_in_dim(matching, face_at, 0, keepdims=False)

    lifted = kernel_one.shape[2]
    fields, got_values = lax.optimization_barrier(
        (jnp.concatenate([base_field, cot_field], axis=3), got_values)
    )
    both = extend_rows(fields, last_tile)
    gridded, cot_before = lax.optimization_barrier((gridded, both[1]))
    both = (both[0], cot_before, both[2])
    cot_back, cot_margins = conv_back(both, channels, channels, kernel_two)
    parts = [edge_cols(both, 0, channels), jnp.swapaxes(cot_margins, 1, 2)]
    first_out, landed = conv_gather(both, 0, channels, pack_parts(parts), kernel_one, 0)
    base_edges, cot_gathered = unpack_parts(landed, parts)
    first_sides = side_terms(side_columns(base_edges, matching_row), kernel_one)

    pre_act = at_edges(first_out, first_sides[:, 0], first_sides[:, 1]) + bias_one + gridded
    inner = activation(pre_act).astype(jnp.bfloat16)
    grad_inner = return_sides(cot_back, cot_gathered, matching_row)
    grad_pre = jax.vjp(activation, pre_act)[1](grad_inner)[0].astype(jnp.bfloat16)

    pair = extend_rows(jnp.concatenate([inner, grad_pre], axis=3), last_tile)
    pre_back, pre_margins = conv_back(pair, lifted, lifted, kernel_one)
    parts = [edge_cols(pair, 0, lifted), jnp.swapaxes(pre_margins, 1, 2)]
    second_out, landed = conv_gather(pair, 0, lifted, pack_parts(parts), kernel_two, 1)
    inner_edges, pre_gathered = unpack_parts(landed, parts)
    second_sides = side_terms(side_columns(inner_edges, matching_row), kernel_two)

    second_out = at_edges(second_out, second_sides[:, 0], second_sides[:, 1])
    analysis = (base_field.astype(jnp.float32) + second_out + bias_two).astype(jnp.bfloat16)
    grad_base = cot_field.astype(jnp.float32) + return_sides(pre_back, pre_gathered, matching_row)
    return (analysis[None, None], grad_base[None, None])


def solution(mesh):
    return jax.shard_map(
        per_device,
        mesh=mesh,
        in_specs=(
            P("face", "tile", None, None, None, None),
            P(("face", "tile"), None),
            P(("face", "tile"), None),
            P(("face", "tile")),
            P(),
            P(),
            P(),
            P(),
            P(),
            P("face", "tile", None, None, None, None),
        ),
        out_specs=(
            P("face", "tile", None, None, None, None),
            P("face", "tile", None, None, None, None),
        ),
        check_vma=False,
    )
```

```python
import functools

import jax
import jax.numpy as jnp
from jax import lax
from jax.experimental import pallas as pl
from jax.experimental.pallas import tpu as pltpu
from jax.sharding import PartitionSpec as P

MESH_IDS = pl.DeviceIdType.MESH


def activation(values):
    return jax.nn.gelu(values, approximate=True)


def tap_index(band, row_tap, col_tap, backward):
    if backward:
        row = 2 - row_tap if band == 0 else row_tap
        return 3 * row + 2 - col_tap
    row = row_tap if band == 0 else 2 - row_tap
    return 3 * row + col_tap


def conv_kernel(backward, first, width, src_ref, before_ref, after_ref, side_ref, k_ref, out_ref, margin_ref):
    bands, rows, cols, cout = out_ref.shape
    pixels = rows * cols
    lanes = slice(first, first + width)
    col = lax.broadcasted_iota(jnp.int32, (rows, cols, cout), 1).reshape(pixels, cout)
    for band in range(bands):
        ext = jnp.concatenate(
            [before_ref[band, :, :, lanes], src_ref[band, :, :, lanes], after_ref[band, :, :, lanes]],
            axis=0,
        )
        lhs = jnp.concatenate(
            [ext[dy : dy + rows].reshape(pixels, width) for dy in range(3)], axis=1
        )
        stacks = []
        for col_tap in range(3):
            taps = [k_ref[tap_index(band, dy, col_tap, backward)] for dy in range(3)]
            if backward:
                stacks.append(jnp.concatenate(taps, axis=1))
            else:
                stacks.append(jnp.concatenate(taps, axis=0))

        def product(values, stack):
            if backward:
                return lax.dot_general(
                    values, stack, (((1,), (1,)), ((), ())), preferred_element_type=jnp.float32
                )
            return jnp.dot(values, stack, preferred_element_type=jnp.float32)

        z_left = product(lhs, stacks[0])
        z_mid = product(lhs, stacks[1])
        z_right = product(lhs, stacks[2])
        if backward or side_ref is None:
            left_full = jnp.zeros((pixels, cout), jnp.float32)
            right_full = left_full
        else:
            sides = side_ref[band]
            left = jnp.concatenate([sides[0, dy : dy + rows] for dy in range(3)], axis=1)
            right = jnp.concatenate([sides[1, dy : dy + rows] for dy in range(3)], axis=1)
            left_term = product(left, stacks[0])
            right_term = product(right, stacks[2])
            left_full = jnp.broadcast_to(left_term[:, None, :], (rows, cols, cout)).reshape(pixels, cout)
            right_full = jnp.broadcast_to(right_term[:, None, :], (rows, cols, cout)).reshape(pixels, cout)
        from_left = jnp.where(col == 0, left_full, pltpu.roll(z_left, 1, 0))
        from_right = jnp.where(col == cols - 1, right_full, pltpu.roll(z_right, pixels - 1, 0))
        out_ref[band] = (z_mid + from_left + from_right).reshape(rows, cols, cout)
        if backward:
            margin_ref[band, 0] = z_right.reshape(rows, cols, cout)[:, 0, :]
            margin_ref[band, 1] = z_left.reshape(rows, cols, cout)[:, cols - 1, :]


def conv_pallas(pieces, first, width, sides, kernel, backward):
    source, before, after = pieces
    bands, rows, cols, _ = source.shape
    cout = kernel.shape[1] if backward else kernel.shape[2]
    if sides is None:
        sides = jnp.zeros((bands, 2, rows + 2, width), jnp.bfloat16)
    vmem = pl.BlockSpec(memory_space=pltpu.VMEM)
    out, margins = pl.pallas_call(
        functools.partial(conv_kernel, backward, first, width),
        in_specs=[vmem] * 5,
        out_specs=[vmem, vmem],
        out_shape=[
            jax.ShapeDtypeStruct((bands, rows, cols, cout), jnp.float32),
            jax.ShapeDtypeStruct((bands, 2, rows, cout), jnp.float32),
        ],
        compiler_params=pltpu.CompilerParams(vmem_limit_bytes=60 * 1024 * 1024),
    )(source, before, after, sides, kernel)
    return out, margins


def back_kernel(src_ref, before_ref, after_ref, k_ref, *rest):
    residual_ref = rest[0] if len(rest) == 3 else None
    out_ref, margin_ref = rest[-2:]
    band = pl.program_id(0)
    _, rows, cols, cout = out_ref.shape
    width = src_ref.shape[3]
    pixels = rows * cols
    col = lax.broadcasted_iota(jnp.int32, (rows, cols, cout), 1).reshape(pixels, cout)
    ext = jnp.concatenate([before_ref[0], src_ref[0], after_ref[0]], axis=0)
    lhs = jnp.concatenate([ext[dy : dy + rows].reshape(pixels, width) for dy in range(3)], axis=1)
    stacks = []
    for col_tap in range(3):
        taps = [k_ref[3 * (2 - dy + band * (2 * dy - 2)) + 2 - col_tap] for dy in range(3)]
        stacks.append(jnp.concatenate(taps, axis=1))
    joined = lax.dot_general(
        lhs, jnp.concatenate(stacks, axis=0), (((1,), (1,)), ((), ())), preferred_element_type=jnp.float32
    )
    z_left, z_mid, z_right = [joined[:, i * cout : (i + 1) * cout] for i in range(3)]
    from_left = jnp.where(col == 0, 0.0, pltpu.roll(z_left, 1, 0))
    from_right = jnp.where(col == cols - 1, 0.0, pltpu.roll(z_right, pixels - 1, 0))
    total = (z_mid + from_left + from_right).reshape(rows, cols, cout)
    if residual_ref is not None:
        total = total + residual_ref[0].astype(jnp.float32)
    out_ref[0] = total
    margin_ref[0, 0] = z_right.reshape(rows, cols, cout)[:, 0, :]
    margin_ref[0, 1] = z_left.reshape(rows, cols, cout)[:, cols - 1, :]


def conv_back(pieces, first, width, kernel, residual=None):
    source, before, after = pieces
    bands, rows, cols, _ = source.shape
    cout = kernel.shape[1]
    block = first // width
    extra_specs = []
    extra_args = ()
    if residual is not None:
        extra_specs = [pl.BlockSpec((1, rows, cols, cout), lambda b: (b, 0, 0, 0))]
        extra_args = (residual,)
    return pl.pallas_call(
        back_kernel,
        grid=(bands,),
        in_specs=[
            pl.BlockSpec((1, rows, cols, width), lambda b: (b, 0, 0, block)),
            pl.BlockSpec((1, 1, cols, width), lambda b: (b, 0, 0, block)),
            pl.BlockSpec((1, 1, cols, width), lambda b: (b, 0, 0, block)),
            pl.BlockSpec(kernel.shape, lambda b: (0, 0, 0)),
        ]
        + extra_specs,
        out_specs=[
            pl.BlockSpec((1, rows, cols, cout), lambda b: (b, 0, 0, 0)),
            pl.BlockSpec((1, 2, rows, cout), lambda b: (b, 0, 0, 0)),
        ],
        out_shape=[
            jax.ShapeDtypeStruct((bands, rows, cols, cout), jnp.float32),
            jax.ShapeDtypeStruct((bands, 2, rows, cout), jnp.float32),
        ],
        compiler_params=pltpu.CompilerParams(vmem_limit_bytes=60 * 1024 * 1024),
    )(source, before, after, kernel, *extra_args)


def conv_gather_kernel(count, block_ref, src_ref, before_ref, after_ref, k_ref, *rest):
    if len(rest) == 7:
        residual_ref, bias_ref = rest[:2]
    else:
        residual_ref = None
    out_ref, gathered_ref, landed, send_sems, recv_sems = rest[-5:]
    step_at = pl.program_id(0)
    face = lax.axis_index("face")
    tile = lax.axis_index("tile")
    copies = []
    for step in range(1, count):
        peer = lax.rem(face + step, count)
        copies.append(
            pltpu.make_async_remote_copy(
                src_ref=block_ref,
                dst_ref=landed.at[step],
                send_sem=send_sems.at[step],
                recv_sem=recv_sems.at[step],
                device_id=(peer, tile),
                device_id_type=MESH_IDS,
            )
        )

    @pl.when(step_at == 0)
    def _():
        barrier = pltpu.get_barrier_semaphore()
        for step in range(1, count):
            peer = lax.rem(face + step, count)
            pl.semaphore_signal(barrier, inc=1, device_id=(peer, tile), device_id_type=MESH_IDS)
        pl.semaphore_wait(barrier, count - 1)
        for copy in copies:
            copy.start()
        gathered_ref[0] = block_ref[...]

    _, rows, cols, cout = out_ref.shape
    width = src_ref.shape[3]
    pixels = rows * cols
    col = lax.broadcasted_iota(jnp.int32, (rows, cols, cout), 1).reshape(pixels, cout)
    ext = jnp.concatenate([before_ref[0], src_ref[0], after_ref[0]], axis=0)
    lhs = jnp.concatenate([ext[dy : dy + rows].reshape(pixels, width) for dy in range(3)], axis=1)
    stacks = []
    for col_tap in range(3):
        taps = [k_ref[3 * (dy + step_at * (2 - 2 * dy)) + col_tap] for dy in range(3)]
        stacks.append(jnp.concatenate(taps, axis=0))
    joined = jnp.dot(lhs, jnp.concatenate(stacks, axis=1), preferred_element_type=jnp.float32)
    z_left, z_mid, z_right = [joined[:, i * cout : (i + 1) * cout] for i in range(3)]
    from_left = jnp.where(col == 0, 0.0, pltpu.roll(z_left, 1, 0))
    from_right = jnp.where(col == cols - 1, 0.0, pltpu.roll(z_right, pixels - 1, 0))
    total = (z_mid + from_left + from_right).reshape(rows, cols, cout)
    if residual_ref is not None:
        total = total + residual_ref[0].astype(jnp.float32) + bias_ref[...]
    out_ref[0] = total

    @pl.when(step_at == pl.num_programs(0) - 1)
    def _():
        for copy in copies:
            copy.wait()
        for step in range(1, count):
            gathered_ref[step] = landed[step]


def conv_gather(pieces, first, width, block, kernel, gather_id, residual=None, bias=None):
    source, before, after = pieces
    bands, rows, cols, _ = source.shape
    cout = kernel.shape[2]
    extra_specs = []
    extra_args = ()
    if residual is not None:
        extra_specs = [
            pl.BlockSpec((1, rows, cols, cout), lambda b: (b, 0, 0, 0)),
            pl.BlockSpec((1, cout), lambda b: (0, 0)),
        ]
        extra_args = (residual, bias.reshape(1, cout))
    count = lax.axis_size("face")
    block_rows, lanes = block.shape
    lane_block = first // width
    return pl.pallas_call(
        functools.partial(conv_gather_kernel, count),
        grid=(bands,),
        in_specs=[
            pl.BlockSpec((block_rows, lanes), lambda b: (0, 0)),
            pl.BlockSpec((1, rows, cols, width), lambda b: (b, 0, 0, lane_block)),
            pl.BlockSpec((1, 1, cols, width), lambda b: (b, 0, 0, lane_block)),
            pl.BlockSpec((1, 1, cols, width), lambda b: (b, 0, 0, lane_block)),
            pl.BlockSpec(kernel.shape, lambda b: (0, 0, 0)),
        ]
        + extra_specs,
        out_specs=[
            pl.BlockSpec((1, rows, cols, cout), lambda b: (b, 0, 0, 0)),
            pl.BlockSpec((count, block_rows, lanes), lambda b: (0, 0, 0)),
        ],
        out_shape=[
            jax.ShapeDtypeStruct((bands, rows, cols, cout), jnp.float32),
            jax.ShapeDtypeStruct((count, block_rows, lanes), block.dtype),
        ],
        scratch_shapes=[
            pltpu.VMEM((count, block_rows, lanes), block.dtype),
            pltpu.SemaphoreType.DMA((count,)),
            pltpu.SemaphoreType.DMA((count,)),
        ],
        compiler_params=pltpu.CompilerParams(
            collective_id=gather_id, has_side_effects=True, vmem_limit_bytes=60 * 1024 * 1024
        ),
    )(block, source, before, after, kernel, *extra_args)


def side_terms(sides, kernel):
    bands, _, ext_rows, width = sides.shape
    rows = ext_rows - 2
    terms = []
    for band in range(bands):
        per_side = []
        for side, col_tap in ((0, 0), (1, 2)):
            stacked = jnp.concatenate([sides[band, side, dy : dy + rows] for dy in range(3)], axis=1)
            weights = jnp.concatenate(
                [kernel[tap_index(band, dy, col_tap, False)] for dy in range(3)], axis=0
            )
            per_side.append(jnp.dot(stacked, weights, preferred_element_type=jnp.float32))
        terms.append(jnp.stack(per_side))
    return jnp.stack(terms)


def at_edges(field, left_add, right_add):
    cols = field.shape[2]
    col = lax.broadcasted_iota(jnp.int32, field.shape, 2)
    return field + jnp.where(col == 0, left_add[:, :, None], 0.0) + jnp.where(
        col == cols - 1, right_add[:, :, None], 0.0
    )


def extend_rows(source, last_tile):
    count = lax.axis_size("tile")
    band_rows = source.shape[1]
    head = source[:, 0:1]
    tail = source[:, band_rows - 1 : band_rows]
    before = lax.ppermute(tail, "tile", [(i, i + 1) for i in range(count - 1)])
    after = lax.ppermute(head, "tile", [(i + 1, i) for i in range(count - 1)])
    after = jnp.where(last_tile, tail[::-1], after)
    return source, before, after


def edge_cols(pieces, first, width):
    extended = jnp.concatenate([piece[..., first : first + width] for piece in (pieces[1], pieces[0], pieces[2])], axis=1)
    return jnp.stack([extended[:, :, 0], extended[:, :, -1]], axis=2)


def pick_partner(gathered, matching_row):
    picked_sides = []
    for side_number in range(2):
        partner = matching_row[side_number, 0]
        their_side = matching_row[side_number, 1]
        flipped = matching_row[side_number, 2]
        chosen = lax.dynamic_index_in_dim(gathered, partner, 0, keepdims=False)
        column = jnp.where(their_side == 0, chosen[:, :, 0], chosen[:, :, 1])
        column = jnp.where(flipped == 1, column[::-1], column)
        picked_sides.append(column)
    return picked_sides


def pack_parts(parts):
    flat = jnp.concatenate([part.astype(jnp.float32).reshape(-1) for part in parts])
    return flat.reshape(-1, 128)


def unpack_parts(landed, parts):
    face_count = lax.axis_size("face")
    face_at = lax.axis_index("face")
    landed = landed.reshape(face_count, -1)
    slot_of_face = lax.rem(face_at - lax.iota(jnp.int32, face_count) + face_count, face_count)
    gathered = jnp.take(landed, slot_of_face, axis=0)
    pieces = []
    offset = 0
    for part in parts:
        size = part.size
        piece = gathered[:, offset : offset + size].reshape((face_count,) + part.shape)
        pieces.append(piece)
        offset += size
    return pieces


def side_columns(gathered_edges, matching_row):
    left_side, right_side = pick_partner(gathered_edges, matching_row)
    return jnp.stack([left_side, right_side], axis=1).astype(jnp.bfloat16)


def add_ends(field, first_add, last_add, axis):
    length = field.shape[axis]
    head = lax.slice_in_dim(field, 0, 1, axis=axis) + jnp.expand_dims(first_add, axis)
    middle = lax.slice_in_dim(field, 1, length - 1, axis=axis)
    tail = lax.slice_in_dim(field, length - 1, length, axis=axis) + jnp.expand_dims(last_add, axis)
    return jnp.concatenate([head, middle, tail], axis=axis)


def return_sides(inside, gathered_margins, matching_row):
    left_back, right_back = pick_partner(gathered_margins, matching_row)
    return at_edges(inside, left_back, right_back)


def route_observations(obs_values, obs_dest, obs_pixel, device_count):
    obs_rows = obs_values.shape[0]
    obs_width = obs_values.shape[1]
    capacity = 2 * obs_rows // device_count
    target = obs_dest[:, 0]
    positions = lax.iota(jnp.int32, obs_rows)
    same_target = (target[:, None] == target[None, :]) & (positions[None, :] < positions[:, None])
    rank_within = jnp.sum(same_target.astype(jnp.int32), axis=1)
    slot_index = target * capacity + rank_within
    slot_ids = lax.iota(jnp.int32, device_count * capacity)
    hits = slot_ids[:, None] == slot_index[None, :]
    value_slots = jnp.dot(
        hits.astype(jnp.bfloat16), obs_values, preferred_element_type=jnp.float32
    ).astype(jnp.bfloat16)
    pixel_slots = jnp.sum(jnp.where(hits, obs_pixel[None, :], 0), axis=1)
    high = (pixel_slots // 16).astype(jnp.bfloat16).reshape(device_count, capacity)
    low = (pixel_slots % 16).astype(jnp.bfloat16).reshape(device_count, capacity)
    pixel_row = jnp.concatenate(
        [high, low, jnp.zeros((device_count, obs_width - 2 * capacity), jnp.bfloat16)], axis=1
    )
    payload = jnp.concatenate(
        [value_slots.reshape(device_count, capacity, obs_width), pixel_row[:, None]], axis=1
    )
    arrived = lax.all_to_all(payload, ("face", "tile"), split_axis=0, concat_axis=0, tiled=True)
    got_values = arrived[:, :capacity].reshape(-1, obs_width)
    got_high = arrived[:, capacity, 0:capacity].astype(jnp.int32)
    got_low = arrived[:, capacity, capacity : 2 * capacity].astype(jnp.int32)
    got_pixels = (got_high * 16 + got_low).reshape(-1)
    return got_values, got_pixels


def per_device(
    state,
    obs_values,
    obs_dest,
    obs_pixel,
    matching,
    kernel_one,
    bias_one,
    kernel_two,
    bias_two,
    cotangent,
):
    base_field = state[0, 0]
    cot_field = cotangent[0, 0]
    band_rows = base_field.shape[1]
    column_count = base_field.shape[2]
    channels = base_field.shape[3]
    tile_count = lax.axis_size("tile")
    face_count = lax.axis_size("face")
    tile_at = lax.axis_index("tile")
    face_at = lax.axis_index("face")
    device_count = tile_count * face_count
    obs_width = obs_values.shape[1]

    got_values, got_pixels = route_observations(obs_values, obs_dest, obs_pixel, device_count)
    pixel_count = 2 * band_rows * column_count
    pixel_ids = lax.iota(jnp.int32, pixel_count)
    onehot = (pixel_ids[:, None] == got_pixels[None, :]).astype(jnp.bfloat16)
    gridded = jnp.dot(onehot, got_values, preferred_element_type=jnp.float32)
    gridded = gridded.reshape(2, band_rows, column_count, obs_width)

    last_tile = tile_at == tile_count - 1
    matching_row = lax.dynamic_index_in_dim(matching, face_at, 0, keepdims=False)

    lifted = kernel_one.shape[2]
    fields, got_values = lax.optimization_barrier(
        (jnp.concatenate([base_field, cot_field], axis=3), got_values)
    )
    both = extend_rows(fields, last_tile)
    cot_back, cot_margins = conv_back(both, channels, channels, kernel_two)
    parts = [edge_cols(both, 0, channels), jnp.swapaxes(cot_margins, 1, 2)]
    first_out, landed = conv_gather(both, 0, channels, pack_parts(parts), kernel_one, 0)
    base_edges, cot_gathered = unpack_parts(landed, parts)
    first_sides = side_terms(side_columns(base_edges, matching_row), kernel_one)

    pre_act = at_edges(first_out, first_sides[:, 0], first_sides[:, 1]) + bias_one + gridded
    inner = activation(pre_act).astype(jnp.bfloat16)
    grad_inner = return_sides(cot_back, cot_gathered, matching_row)
    grad_pre = jax.vjp(activation, pre_act)[1](grad_inner)[0].astype(jnp.bfloat16)

    pair = extend_rows(jnp.concatenate([inner, grad_pre], axis=3), last_tile)
    pre_back, pre_margins = conv_back(pair, lifted, lifted, kernel_one, cot_field)
    parts = [edge_cols(pair, 0, lifted), jnp.swapaxes(pre_margins, 1, 2)]
    second_out, landed = conv_gather(
        pair, 0, lifted, pack_parts(parts), kernel_two, 1, base_field, bias_two
    )
    inner_edges, pre_gathered = unpack_parts(landed, parts)
    second_sides = side_terms(side_columns(inner_edges, matching_row), kernel_two)

    second_out = at_edges(second_out, second_sides[:, 0], second_sides[:, 1])
    analysis = second_out.astype(jnp.bfloat16)
    grad_base = return_sides(pre_back, pre_gathered, matching_row)
    return (analysis[None, None], grad_base[None, None])


def solution(mesh):
    return jax.shard_map(
        per_device,
        mesh=mesh,
        in_specs=(
            P("face", "tile", None, None, None, None),
            P(("face", "tile"), None),
            P(("face", "tile"), None),
            P(("face", "tile")),
            P(),
            P(),
            P(),
            P(),
            P(),
            P("face", "tile", None, None, None, None),
        ),
        out_specs=(
            P("face", "tile", None, None, None, None),
            P("face", "tile", None, None, None, None),
        ),
        check_vma=False,
    )
```

```python
import functools

import jax
import jax.numpy as jnp
from jax import lax
from jax.experimental import pallas as pl
from jax.experimental.pallas import tpu as pltpu
from jax.sharding import PartitionSpec as P

MESH_IDS = pl.DeviceIdType.MESH


def activation(values):
    return jax.nn.gelu(values, approximate=True)


def tap_index(band, row_tap, col_tap, backward):
    if backward:
        row = 2 - row_tap if band == 0 else row_tap
        return 3 * row + 2 - col_tap
    row = row_tap if band == 0 else 2 - row_tap
    return 3 * row + col_tap


def conv_kernel(backward, first, width, src_ref, before_ref, after_ref, side_ref, k_ref, out_ref, margin_ref):
    bands, rows, cols, cout = out_ref.shape
    pixels = rows * cols
    lanes = slice(first, first + width)
    col = lax.broadcasted_iota(jnp.int32, (rows, cols, cout), 1).reshape(pixels, cout)
    for band in range(bands):
        ext = jnp.concatenate(
            [before_ref[band, :, :, lanes], src_ref[band, :, :, lanes], after_ref[band, :, :, lanes]],
            axis=0,
        )
        lhs = jnp.concatenate(
            [ext[dy : dy + rows].reshape(pixels, width) for dy in range(3)], axis=1
        )
        stacks = []
        for col_tap in range(3):
            taps = [k_ref[tap_index(band, dy, col_tap, backward)] for dy in range(3)]
            if backward:
                stacks.append(jnp.concatenate(taps, axis=1))
            else:
                stacks.append(jnp.concatenate(taps, axis=0))

        def product(values, stack):
            if backward:
                return lax.dot_general(
                    values, stack, (((1,), (1,)), ((), ())), preferred_element_type=jnp.float32
                )
            return jnp.dot(values, stack, preferred_element_type=jnp.float32)

        z_left = product(lhs, stacks[0])
        z_mid = product(lhs, stacks[1])
        z_right = product(lhs, stacks[2])
        if backward or side_ref is None:
            left_full = jnp.zeros((pixels, cout), jnp.float32)
            right_full = left_full
        else:
            sides = side_ref[band]
            left = jnp.concatenate([sides[0, dy : dy + rows] for dy in range(3)], axis=1)
            right = jnp.concatenate([sides[1, dy : dy + rows] for dy in range(3)], axis=1)
            left_term = product(left, stacks[0])
            right_term = product(right, stacks[2])
            left_full = jnp.broadcast_to(left_term[:, None, :], (rows, cols, cout)).reshape(pixels, cout)
            right_full = jnp.broadcast_to(right_term[:, None, :], (rows, cols, cout)).reshape(pixels, cout)
        from_left = jnp.where(col == 0, left_full, pltpu.roll(z_left, 1, 0))
        from_right = jnp.where(col == cols - 1, right_full, pltpu.roll(z_right, pixels - 1, 0))
        out_ref[band] = (z_mid + from_left + from_right).reshape(rows, cols, cout)
        if backward:
            margin_ref[band, 0] = z_right.reshape(rows, cols, cout)[:, 0, :]
            margin_ref[band, 1] = z_left.reshape(rows, cols, cout)[:, cols - 1, :]


def conv_pallas(pieces, first, width, sides, kernel, backward):
    source, before, after = pieces
    bands, rows, cols, _ = source.shape
    cout = kernel.shape[1] if backward else kernel.shape[2]
    if sides is None:
        sides = jnp.zeros((bands, 2, rows + 2, width), jnp.bfloat16)
    vmem = pl.BlockSpec(memory_space=pltpu.VMEM)
    out, margins = pl.pallas_call(
        functools.partial(conv_kernel, backward, first, width),
        in_specs=[vmem] * 5,
        out_specs=[vmem, vmem],
        out_shape=[
            jax.ShapeDtypeStruct((bands, rows, cols, cout), jnp.float32),
            jax.ShapeDtypeStruct((bands, 2, rows, cout), jnp.float32),
        ],
        compiler_params=pltpu.CompilerParams(vmem_limit_bytes=60 * 1024 * 1024),
    )(source, before, after, sides, kernel)
    return out, margins


def back_kernel(src_ref, before_ref, after_ref, k_ref, *rest):
    residual_ref = rest[0] if len(rest) == 3 else None
    out_ref, margin_ref = rest[-2:]
    band = pl.program_id(0)
    _, rows, cols, cout = out_ref.shape
    width = src_ref.shape[3]
    pixels = rows * cols
    col = lax.broadcasted_iota(jnp.int32, (rows, cols, cout), 1).reshape(pixels, cout)
    ext = jnp.concatenate([before_ref[0], src_ref[0], after_ref[0]], axis=0)
    lhs = jnp.concatenate([ext[dy : dy + rows].reshape(pixels, width) for dy in range(3)], axis=1)
    stacks = []
    for col_tap in range(3):
        taps = [k_ref[3 * (2 - dy + band * (2 * dy - 2)) + 2 - col_tap] for dy in range(3)]
        stacks.append(jnp.concatenate(taps, axis=1))
    joined = lax.dot_general(
        lhs, jnp.concatenate(stacks, axis=0), (((1,), (1,)), ((), ())), preferred_element_type=jnp.float32
    )
    z_left, z_mid, z_right = [joined[:, i * cout : (i + 1) * cout] for i in range(3)]
    from_left = jnp.where(col == 0, 0.0, pltpu.roll(z_left, 1, 0))
    from_right = jnp.where(col == cols - 1, 0.0, pltpu.roll(z_right, pixels - 1, 0))
    total = (z_mid + from_left + from_right).reshape(rows, cols, cout)
    if residual_ref is not None:
        total = total + residual_ref[0].astype(jnp.float32)
    out_ref[0] = total
    margin_ref[0, 0] = z_right.reshape(rows, cols, cout)[:, 0, :]
    margin_ref[0, 1] = z_left.reshape(rows, cols, cout)[:, cols - 1, :]


def conv_back(pieces, first, width, kernel, residual=None):
    source, before, after = pieces
    bands, rows, cols, _ = source.shape
    cout = kernel.shape[1]
    block = first // width
    extra_specs = []
    extra_args = ()
    if residual is not None:
        extra_specs = [pl.BlockSpec((1, rows, cols, cout), lambda b: (b, 0, 0, 0))]
        extra_args = (residual,)
    return pl.pallas_call(
        back_kernel,
        grid=(bands,),
        in_specs=[
            pl.BlockSpec((1, rows, cols, width), lambda b: (b, 0, 0, block)),
            pl.BlockSpec((1, 1, cols, width), lambda b: (b, 0, 0, block)),
            pl.BlockSpec((1, 1, cols, width), lambda b: (b, 0, 0, block)),
            pl.BlockSpec(kernel.shape, lambda b: (0, 0, 0)),
        ]
        + extra_specs,
        out_specs=[
            pl.BlockSpec((1, rows, cols, cout), lambda b: (b, 0, 0, 0)),
            pl.BlockSpec((1, 2, rows, cout), lambda b: (b, 0, 0, 0)),
        ],
        out_shape=[
            jax.ShapeDtypeStruct((bands, rows, cols, cout), jnp.float32),
            jax.ShapeDtypeStruct((bands, 2, rows, cout), jnp.float32),
        ],
        compiler_params=pltpu.CompilerParams(vmem_limit_bytes=60 * 1024 * 1024),
    )(source, before, after, kernel, *extra_args)


def conv_gather_kernel(count, block_ref, src_ref, before_ref, after_ref, k_ref, *rest):
    if len(rest) == 7:
        residual_ref, bias_ref = rest[:2]
    else:
        residual_ref = None
    out_ref, gathered_ref, landed, send_sems, recv_sems = rest[-5:]
    step_at = pl.program_id(0)
    face = lax.axis_index("face")
    tile = lax.axis_index("tile")
    copies = []
    for step in range(1, count):
        peer = lax.rem(face + step, count)
        copies.append(
            pltpu.make_async_remote_copy(
                src_ref=block_ref,
                dst_ref=landed.at[step],
                send_sem=send_sems.at[step],
                recv_sem=recv_sems.at[step],
                device_id=(peer, tile),
                device_id_type=MESH_IDS,
            )
        )

    @pl.when(step_at == 0)
    def _():
        barrier = pltpu.get_barrier_semaphore()
        for step in range(1, count):
            peer = lax.rem(face + step, count)
            pl.semaphore_signal(barrier, inc=1, device_id=(peer, tile), device_id_type=MESH_IDS)
        pl.semaphore_wait(barrier, count - 1)
        for copy in copies:
            copy.start()
        gathered_ref[0] = block_ref[...]

    _, rows, cols, cout = out_ref.shape
    width = src_ref.shape[3]
    pixels = rows * cols
    col = lax.broadcasted_iota(jnp.int32, (rows, cols, cout), 1).reshape(pixels, cout)
    ext = jnp.concatenate([before_ref[0], src_ref[0], after_ref[0]], axis=0)
    lhs = jnp.concatenate([ext[dy : dy + rows].reshape(pixels, width) for dy in range(3)], axis=1)
    stacks = []
    for col_tap in range(3):
        taps = [k_ref[3 * (dy + step_at * (2 - 2 * dy)) + col_tap] for dy in range(3)]
        stacks.append(jnp.concatenate(taps, axis=0))
    joined = jnp.dot(lhs, jnp.concatenate(stacks, axis=1), preferred_element_type=jnp.float32)
    z_left, z_mid, z_right = [joined[:, i * cout : (i + 1) * cout] for i in range(3)]
    from_left = jnp.where(col == 0, 0.0, pltpu.roll(z_left, 1, 0))
    from_right = jnp.where(col == cols - 1, 0.0, pltpu.roll(z_right, pixels - 1, 0))
    total = (z_mid + from_left + from_right).reshape(rows, cols, cout)
    if residual_ref is not None:
        total = total + residual_ref[0].astype(jnp.float32) + bias_ref[...]
    out_ref[0] = total

    @pl.when(step_at == pl.num_programs(0) - 1)
    def _():
        for copy in copies:
            copy.wait()
        for step in range(1, count):
            gathered_ref[step] = landed[step]


def conv_gather(pieces, first, width, block, kernel, gather_id, residual=None, bias=None):
    source, before, after = pieces
    bands, rows, cols, _ = source.shape
    cout = kernel.shape[2]
    extra_specs = []
    extra_args = ()
    if residual is not None:
        extra_specs = [
            pl.BlockSpec((1, rows, cols, cout), lambda b: (b, 0, 0, 0)),
            pl.BlockSpec((1, cout), lambda b: (0, 0)),
        ]
        extra_args = (residual, bias.reshape(1, cout))
    count = lax.axis_size("face")
    block_rows, lanes = block.shape
    lane_block = first // width
    return pl.pallas_call(
        functools.partial(conv_gather_kernel, count),
        grid=(bands,),
        in_specs=[
            pl.BlockSpec((block_rows, lanes), lambda b: (0, 0)),
            pl.BlockSpec((1, rows, cols, width), lambda b: (b, 0, 0, lane_block)),
            pl.BlockSpec((1, 1, cols, width), lambda b: (b, 0, 0, lane_block)),
            pl.BlockSpec((1, 1, cols, width), lambda b: (b, 0, 0, lane_block)),
            pl.BlockSpec(kernel.shape, lambda b: (0, 0, 0)),
        ]
        + extra_specs,
        out_specs=[
            pl.BlockSpec((1, rows, cols, cout), lambda b: (b, 0, 0, 0)),
            pl.BlockSpec((count, block_rows, lanes), lambda b: (0, 0, 0)),
        ],
        out_shape=[
            jax.ShapeDtypeStruct((bands, rows, cols, cout), jnp.float32),
            jax.ShapeDtypeStruct((count, block_rows, lanes), block.dtype),
        ],
        scratch_shapes=[
            pltpu.VMEM((count, block_rows, lanes), block.dtype),
            pltpu.SemaphoreType.DMA((count,)),
            pltpu.SemaphoreType.DMA((count,)),
        ],
        compiler_params=pltpu.CompilerParams(
            collective_id=gather_id, has_side_effects=True, vmem_limit_bytes=60 * 1024 * 1024
        ),
    )(block, source, before, after, kernel, *extra_args)


def side_terms(sides, kernel):
    bands, _, ext_rows, width = sides.shape
    rows = ext_rows - 2
    terms = []
    for band in range(bands):
        per_side = []
        for side, col_tap in ((0, 0), (1, 2)):
            stacked = jnp.concatenate([sides[band, side, dy : dy + rows] for dy in range(3)], axis=1)
            weights = jnp.concatenate(
                [kernel[tap_index(band, dy, col_tap, False)] for dy in range(3)], axis=0
            )
            per_side.append(jnp.dot(stacked, weights, preferred_element_type=jnp.float32))
        terms.append(jnp.stack(per_side))
    return jnp.stack(terms)


def at_edges(field, left_add, right_add):
    cols = field.shape[2]
    col = lax.broadcasted_iota(jnp.int32, field.shape, 2)
    return field + jnp.where(col == 0, left_add[:, :, None], 0.0) + jnp.where(
        col == cols - 1, right_add[:, :, None], 0.0
    )


def extend_rows(source, last_tile):
    count = lax.axis_size("tile")
    band_rows = source.shape[1]
    head = source[:, 0:1]
    tail = source[:, band_rows - 1 : band_rows]
    before = lax.ppermute(tail, "tile", [(i, i + 1) for i in range(count - 1)])
    after = lax.ppermute(head, "tile", [(i + 1, i) for i in range(count - 1)])
    after = jnp.where(last_tile, tail[::-1], after)
    return source, before, after


def edge_cols(pieces, first, width):
    extended = jnp.concatenate([piece[..., first : first + width] for piece in (pieces[1], pieces[0], pieces[2])], axis=1)
    return jnp.stack([extended[:, :, 0], extended[:, :, -1]], axis=2)


def pick_partner(gathered, matching_row):
    picked_sides = []
    for side_number in range(2):
        partner = matching_row[side_number, 0]
        their_side = matching_row[side_number, 1]
        flipped = matching_row[side_number, 2]
        face_count = lax.axis_size("face")
        slot = lax.rem(lax.axis_index("face") - partner + face_count, face_count)
        chosen = lax.dynamic_index_in_dim(gathered, slot, 0, keepdims=False)
        column = jnp.where(their_side == 0, chosen[:, :, 0], chosen[:, :, 1])
        column = jnp.where(flipped == 1, column[::-1], column)
        picked_sides.append(column)
    return picked_sides


def pack_parts(parts):
    flat = jnp.concatenate([part.astype(jnp.float32).reshape(-1) for part in parts])
    return flat.reshape(-1, 128)


def unpack_parts(landed, parts):
    face_count = lax.axis_size("face")
    face_at = lax.axis_index("face")
    gathered = landed.reshape(face_count, -1)
    pieces = []
    offset = 0
    for part in parts:
        size = part.size
        piece = gathered[:, offset : offset + size].reshape((face_count,) + part.shape)
        pieces.append(piece)
        offset += size
    return pieces


def side_columns(gathered_edges, matching_row):
    left_side, right_side = pick_partner(gathered_edges, matching_row)
    return jnp.stack([left_side, right_side], axis=1).astype(jnp.bfloat16)


def add_ends(field, first_add, last_add, axis):
    length = field.shape[axis]
    head = lax.slice_in_dim(field, 0, 1, axis=axis) + jnp.expand_dims(first_add, axis)
    middle = lax.slice_in_dim(field, 1, length - 1, axis=axis)
    tail = lax.slice_in_dim(field, length - 1, length, axis=axis) + jnp.expand_dims(last_add, axis)
    return jnp.concatenate([head, middle, tail], axis=axis)


def return_sides(inside, gathered_margins, matching_row):
    left_back, right_back = pick_partner(gathered_margins, matching_row)
    return at_edges(inside, left_back, right_back)


def route_observations(obs_values, obs_dest, obs_pixel, device_count):
    obs_rows = obs_values.shape[0]
    obs_width = obs_values.shape[1]
    capacity = 2 * obs_rows // device_count
    target = obs_dest[:, 0]
    positions = lax.iota(jnp.int32, obs_rows)
    same_target = (target[:, None] == target[None, :]) & (positions[None, :] < positions[:, None])
    rank_within = jnp.sum(same_target.astype(jnp.int32), axis=1)
    slot_index = target * capacity + rank_within
    slot_ids = lax.iota(jnp.int32, device_count * capacity)
    hits = slot_ids[:, None] == slot_index[None, :]
    value_slots = jnp.dot(
        hits.astype(jnp.bfloat16), obs_values, preferred_element_type=jnp.float32
    ).astype(jnp.bfloat16)
    pixel_slots = jnp.sum(jnp.where(hits, obs_pixel[None, :], 0), axis=1)
    high = (pixel_slots // 16).astype(jnp.bfloat16).reshape(device_count, capacity)
    low = (pixel_slots % 16).astype(jnp.bfloat16).reshape(device_count, capacity)
    pixel_row = jnp.concatenate(
        [high, low, jnp.zeros((device_count, obs_width - 2 * capacity), jnp.bfloat16)], axis=1
    )
    payload = jnp.concatenate(
        [value_slots.reshape(device_count, capacity, obs_width), pixel_row[:, None]], axis=1
    )
    arrived = lax.all_to_all(payload, ("face", "tile"), split_axis=0, concat_axis=0, tiled=True)
    got_values = arrived[:, :capacity].reshape(-1, obs_width)
    got_high = arrived[:, capacity, 0:capacity].astype(jnp.int32)
    got_low = arrived[:, capacity, capacity : 2 * capacity].astype(jnp.int32)
    got_pixels = (got_high * 16 + got_low).reshape(-1)
    return got_values, got_pixels


def per_device(
    state,
    obs_values,
    obs_dest,
    obs_pixel,
    matching,
    kernel_one,
    bias_one,
    kernel_two,
    bias_two,
    cotangent,
):
    base_field = state[0, 0]
    cot_field = cotangent[0, 0]
    band_rows = base_field.shape[1]
    column_count = base_field.shape[2]
    channels = base_field.shape[3]
    tile_count = lax.axis_size("tile")
    face_count = lax.axis_size("face")
    tile_at = lax.axis_index("tile")
    face_at = lax.axis_index("face")
    device_count = tile_count * face_count
    obs_width = obs_values.shape[1]

    got_values, got_pixels = route_observations(obs_values, obs_dest, obs_pixel, device_count)
    pixel_count = 2 * band_rows * column_count
    pixel_ids = lax.iota(jnp.int32, pixel_count)
    onehot = (pixel_ids[:, None] == got_pixels[None, :]).astype(jnp.bfloat16)
    gridded = jnp.dot(onehot, got_values, preferred_element_type=jnp.float32)
    gridded = gridded.reshape(2, band_rows, column_count, obs_width)

    last_tile = tile_at == tile_count - 1
    matching_row = lax.dynamic_index_in_dim(matching, face_at, 0, keepdims=False)

    lifted = kernel_one.shape[2]
    fields, got_values = lax.optimization_barrier(
        (jnp.concatenate([base_field, cot_field], axis=3), got_values)
    )
    both = extend_rows(fields, last_tile)
    cot_back, cot_margins = conv_back(both, channels, channels, kernel_two)
    parts = [edge_cols(both, 0, channels), jnp.swapaxes(cot_margins, 1, 2)]
    first_out, landed = conv_gather(both, 0, channels, pack_parts(parts), kernel_one, 0)
    base_edges, cot_gathered = unpack_parts(landed, parts)
    first_sides = side_terms(side_columns(base_edges, matching_row), kernel_one)

    pre_act = at_edges(first_out, first_sides[:, 0], first_sides[:, 1]) + bias_one + gridded
    inner = activation(pre_act).astype(jnp.bfloat16)
    grad_inner = return_sides(cot_back, cot_gathered, matching_row)
    grad_pre = jax.vjp(activation, pre_act)[1](grad_inner)[0].astype(jnp.bfloat16)

    pair = extend_rows(jnp.concatenate([inner, grad_pre], axis=3), last_tile)
    pre_back, pre_margins = conv_back(pair, lifted, lifted, kernel_one, cot_field)
    parts = [edge_cols(pair, 0, lifted), jnp.swapaxes(pre_margins, 1, 2)]
    second_out, landed = conv_gather(
        pair, 0, lifted, pack_parts(parts), kernel_two, 1, base_field, bias_two
    )
    inner_edges, pre_gathered = unpack_parts(landed, parts)
    second_sides = side_terms(side_columns(inner_edges, matching_row), kernel_two)

    second_out = at_edges(second_out, second_sides[:, 0], second_sides[:, 1])
    analysis = second_out.astype(jnp.bfloat16)
    grad_base = return_sides(pre_back, pre_gathered, matching_row)
    return (analysis[None, None], grad_base[None, None])


def solution(mesh):
    return jax.shard_map(
        per_device,
        mesh=mesh,
        in_specs=(
            P("face", "tile", None, None, None, None),
            P(("face", "tile"), None),
            P(("face", "tile"), None),
            P(("face", "tile")),
            P(),
            P(),
            P(),
            P(),
            P(),
            P("face", "tile", None, None, None, None),
        ),
        out_specs=(
            P("face", "tile", None, None, None, None),
            P("face", "tile", None, None, None, None),
        ),
        check_vma=False,
    )
```

```python
import functools

import jax
import jax.numpy as jnp
from jax import lax
from jax.experimental import pallas as pl
from jax.experimental.pallas import tpu as pltpu
from jax.sharding import PartitionSpec as P

MESH_IDS = pl.DeviceIdType.MESH


def activation(values):
    return jax.nn.gelu(values, approximate=True)


def tap_index(band, row_tap, col_tap, backward):
    if backward:
        row = 2 - row_tap if band == 0 else row_tap
        return 3 * row + 2 - col_tap
    row = row_tap if band == 0 else 2 - row_tap
    return 3 * row + col_tap


def conv_kernel(backward, first, width, src_ref, before_ref, after_ref, side_ref, k_ref, out_ref, margin_ref):
    bands, rows, cols, cout = out_ref.shape
    pixels = rows * cols
    lanes = slice(first, first + width)
    col = lax.broadcasted_iota(jnp.int32, (rows, cols, cout), 1).reshape(pixels, cout)
    for band in range(bands):
        ext = jnp.concatenate(
            [before_ref[band, :, :, lanes], src_ref[band, :, :, lanes], after_ref[band, :, :, lanes]],
            axis=0,
        )
        lhs = jnp.concatenate(
            [ext[dy : dy + rows].reshape(pixels, width) for dy in range(3)], axis=1
        )
        stacks = []
        for col_tap in range(3):
            taps = [k_ref[tap_index(band, dy, col_tap, backward)] for dy in range(3)]
            if backward:
                stacks.append(jnp.concatenate(taps, axis=1))
            else:
                stacks.append(jnp.concatenate(taps, axis=0))

        def product(values, stack):
            if backward:
                return lax.dot_general(
                    values, stack, (((1,), (1,)), ((), ())), preferred_element_type=jnp.float32
                )
            return jnp.dot(values, stack, preferred_element_type=jnp.float32)

        z_left = product(lhs, stacks[0])
        z_mid = product(lhs, stacks[1])
        z_right = product(lhs, stacks[2])
        if backward or side_ref is None:
            left_full = jnp.zeros((pixels, cout), jnp.float32)
            right_full = left_full
        else:
            sides = side_ref[band]
            left = jnp.concatenate([sides[0, dy : dy + rows] for dy in range(3)], axis=1)
            right = jnp.concatenate([sides[1, dy : dy + rows] for dy in range(3)], axis=1)
            left_term = product(left, stacks[0])
            right_term = product(right, stacks[2])
            left_full = jnp.broadcast_to(left_term[:, None, :], (rows, cols, cout)).reshape(pixels, cout)
            right_full = jnp.broadcast_to(right_term[:, None, :], (rows, cols, cout)).reshape(pixels, cout)
        from_left = jnp.where(col == 0, left_full, pltpu.roll(z_left, 1, 0))
        from_right = jnp.where(col == cols - 1, right_full, pltpu.roll(z_right, pixels - 1, 0))
        out_ref[band] = (z_mid + from_left + from_right).reshape(rows, cols, cout)
        if backward:
            margin_ref[band, 0] = z_right.reshape(rows, cols, cout)[:, 0, :]
            margin_ref[band, 1] = z_left.reshape(rows, cols, cout)[:, cols - 1, :]


def conv_pallas(pieces, first, width, sides, kernel, backward):
    source, before, after = pieces
    bands, rows, cols, _ = source.shape
    cout = kernel.shape[1] if backward else kernel.shape[2]
    if sides is None:
        sides = jnp.zeros((bands, 2, rows + 2, width), jnp.bfloat16)
    vmem = pl.BlockSpec(memory_space=pltpu.VMEM)
    out, margins = pl.pallas_call(
        functools.partial(conv_kernel, backward, first, width),
        in_specs=[vmem] * 5,
        out_specs=[vmem, vmem],
        out_shape=[
            jax.ShapeDtypeStruct((bands, rows, cols, cout), jnp.float32),
            jax.ShapeDtypeStruct((bands, 2, rows, cout), jnp.float32),
        ],
        compiler_params=pltpu.CompilerParams(vmem_limit_bytes=60 * 1024 * 1024),
    )(source, before, after, sides, kernel)
    return out, margins


def back_kernel(src_ref, before_ref, after_ref, k_ref, *rest):
    residual_ref = rest[0] if len(rest) == 3 else None
    out_ref, margin_ref = rest[-2:]
    band = pl.program_id(0)
    _, rows, cols, cout = out_ref.shape
    width = src_ref.shape[3]
    pixels = rows * cols
    col = lax.broadcasted_iota(jnp.int32, (rows, cols, cout), 1).reshape(pixels, cout)
    ext = jnp.concatenate([before_ref[0], src_ref[0], after_ref[0]], axis=0)
    lhs = jnp.concatenate([ext[dy : dy + rows].reshape(pixels, width) for dy in range(3)], axis=1)
    stacks = []
    for col_tap in range(3):
        taps = [k_ref[3 * (2 - dy + band * (2 * dy - 2)) + 2 - col_tap] for dy in range(3)]
        stacks.append(jnp.concatenate(taps, axis=1))
    joined = lax.dot_general(
        lhs, jnp.concatenate(stacks, axis=0), (((1,), (1,)), ((), ())), preferred_element_type=jnp.float32
    )
    z_left, z_mid, z_right = [joined[:, i * cout : (i + 1) * cout] for i in range(3)]
    from_left = jnp.where(col == 0, 0.0, pltpu.roll(z_left, 1, 0))
    from_right = jnp.where(col == cols - 1, 0.0, pltpu.roll(z_right, pixels - 1, 0))
    total = (z_mid + from_left + from_right).reshape(rows, cols, cout)
    if residual_ref is not None:
        total = total + residual_ref[0].astype(jnp.float32)
    out_ref[0] = total
    margin_ref[0, 0] = z_right.reshape(rows, cols, cout)[:, 0, :]
    margin_ref[0, 1] = z_left.reshape(rows, cols, cout)[:, cols - 1, :]


def conv_back(pieces, first, width, kernel, residual=None):
    source, before, after = pieces
    bands, rows, cols, _ = source.shape
    cout = kernel.shape[1]
    block = first // width
    extra_specs = []
    extra_args = ()
    if residual is not None:
        extra_specs = [pl.BlockSpec((1, rows, cols, cout), lambda b: (b, 0, 0, 0))]
        extra_args = (residual,)
    return pl.pallas_call(
        back_kernel,
        grid=(bands,),
        in_specs=[
            pl.BlockSpec((1, rows, cols, width), lambda b: (b, 0, 0, block)),
            pl.BlockSpec((1, 1, cols, width), lambda b: (b, 0, 0, block)),
            pl.BlockSpec((1, 1, cols, width), lambda b: (b, 0, 0, block)),
            pl.BlockSpec(kernel.shape, lambda b: (0, 0, 0)),
        ]
        + extra_specs,
        out_specs=[
            pl.BlockSpec((1, rows, cols, cout), lambda b: (b, 0, 0, 0)),
            pl.BlockSpec((1, 2, rows, cout), lambda b: (b, 0, 0, 0)),
        ],
        out_shape=[
            jax.ShapeDtypeStruct((bands, rows, cols, cout), jnp.float32),
            jax.ShapeDtypeStruct((bands, 2, rows, cout), jnp.float32),
        ],
        compiler_params=pltpu.CompilerParams(vmem_limit_bytes=60 * 1024 * 1024),
    )(source, before, after, kernel, *extra_args)


def conv_gather_kernel(count, block_ref, src_ref, before_ref, after_ref, k_ref, *rest):
    if len(rest) == 7:
        residual_ref, bias_ref = rest[:2]
    else:
        residual_ref = None
    out_ref, gathered_ref, landed, send_sems, recv_sems = rest[-5:]
    step_at = pl.program_id(0)
    face = lax.axis_index("face")
    tile = lax.axis_index("tile")
    copies = []
    for step in range(1, count):
        peer = lax.rem(face + step, count)
        copies.append(
            pltpu.make_async_remote_copy(
                src_ref=block_ref,
                dst_ref=landed.at[step],
                send_sem=send_sems.at[step],
                recv_sem=recv_sems.at[step],
                device_id=(peer, tile),
                device_id_type=MESH_IDS,
            )
        )

    @pl.when(step_at == 0)
    def _():
        barrier = pltpu.get_barrier_semaphore()
        for step in range(1, count):
            peer = lax.rem(face + step, count)
            pl.semaphore_signal(barrier, inc=1, device_id=(peer, tile), device_id_type=MESH_IDS)
        pl.semaphore_wait(barrier, count - 1)
        for copy in copies:
            copy.start()
        gathered_ref[0] = block_ref[...]

    _, rows, cols, cout = out_ref.shape
    width = src_ref.shape[3]
    pixels = rows * cols
    col = lax.broadcasted_iota(jnp.int32, (rows, cols, cout), 1).reshape(pixels, cout)
    ext = jnp.concatenate([before_ref[0], src_ref[0], after_ref[0]], axis=0)
    lhs = jnp.concatenate([ext[dy : dy + rows].reshape(pixels, width) for dy in range(3)], axis=1)
    stacks = []
    for col_tap in range(3):
        taps = [k_ref[3 * (dy + step_at * (2 - 2 * dy)) + col_tap] for dy in range(3)]
        stacks.append(jnp.concatenate(taps, axis=0))
    joined = jnp.dot(lhs, jnp.concatenate(stacks, axis=1), preferred_element_type=jnp.float32)
    z_left, z_mid, z_right = [joined[:, i * cout : (i + 1) * cout] for i in range(3)]
    from_left = jnp.where(col == 0, 0.0, pltpu.roll(z_left, 1, 0))
    from_right = jnp.where(col == cols - 1, 0.0, pltpu.roll(z_right, pixels - 1, 0))
    total = (z_mid + from_left + from_right).reshape(rows, cols, cout)
    if residual_ref is not None:
        total = total + residual_ref[0].astype(jnp.float32) + bias_ref[...]
    out_ref[0] = total

    @pl.when(step_at == pl.num_programs(0) - 1)
    def _():
        for copy in copies:
            copy.wait()
        for step in range(1, count):
            gathered_ref[step] = landed[step]


def conv_gather(pieces, first, width, block, kernel, gather_id, residual=None, bias=None):
    source, before, after = pieces
    bands, rows, cols, _ = source.shape
    cout = kernel.shape[2]
    extra_specs = []
    extra_args = ()
    if residual is not None:
        extra_specs = [
            pl.BlockSpec((1, rows, cols, cout), lambda b: (b, 0, 0, 0)),
            pl.BlockSpec((1, cout), lambda b: (0, 0)),
        ]
        extra_args = (residual, bias.reshape(1, cout))
    count = lax.axis_size("face")
    block_rows, lanes = block.shape
    lane_block = first // width
    return pl.pallas_call(
        functools.partial(conv_gather_kernel, count),
        grid=(bands,),
        in_specs=[
            pl.BlockSpec((block_rows, lanes), lambda b: (0, 0)),
            pl.BlockSpec((1, rows, cols, width), lambda b: (b, 0, 0, lane_block)),
            pl.BlockSpec((1, 1, cols, width), lambda b: (b, 0, 0, lane_block)),
            pl.BlockSpec((1, 1, cols, width), lambda b: (b, 0, 0, lane_block)),
            pl.BlockSpec(kernel.shape, lambda b: (0, 0, 0)),
        ]
        + extra_specs,
        out_specs=[
            pl.BlockSpec((1, rows, cols, cout), lambda b: (b, 0, 0, 0)),
            pl.BlockSpec((count, block_rows, lanes), lambda b: (0, 0, 0)),
        ],
        out_shape=[
            jax.ShapeDtypeStruct((bands, rows, cols, cout), jnp.float32),
            jax.ShapeDtypeStruct((count, block_rows, lanes), block.dtype),
        ],
        scratch_shapes=[
            pltpu.VMEM((count, block_rows, lanes), block.dtype),
            pltpu.SemaphoreType.DMA((count,)),
            pltpu.SemaphoreType.DMA((count,)),
        ],
        compiler_params=pltpu.CompilerParams(
            collective_id=gather_id, has_side_effects=True, vmem_limit_bytes=60 * 1024 * 1024
        ),
    )(block, source, before, after, kernel, *extra_args)


def side_terms(sides, kernel):
    bands, _, ext_rows, width = sides.shape
    rows = ext_rows - 2
    terms = []
    for band in range(bands):
        per_side = []
        for side, col_tap in ((0, 0), (1, 2)):
            stacked = jnp.concatenate([sides[band, side, dy : dy + rows] for dy in range(3)], axis=1)
            weights = jnp.concatenate(
                [kernel[tap_index(band, dy, col_tap, False)] for dy in range(3)], axis=0
            )
            per_side.append(jnp.dot(stacked, weights, preferred_element_type=jnp.float32))
        terms.append(jnp.stack(per_side))
    return jnp.stack(terms)


def at_edges(field, left_add, right_add):
    cols = field.shape[2]
    col = lax.broadcasted_iota(jnp.int32, field.shape, 2)
    return field + jnp.where(col == 0, left_add[:, :, None], 0.0) + jnp.where(
        col == cols - 1, right_add[:, :, None], 0.0
    )


def extend_rows(source, last_tile):
    count = lax.axis_size("tile")
    band_rows = source.shape[1]
    head = source[:, 0:1]
    tail = source[:, band_rows - 1 : band_rows]
    before = lax.ppermute(tail, "tile", [(i, i + 1) for i in range(count - 1)])
    after = lax.ppermute(head, "tile", [(i + 1, i) for i in range(count - 1)])
    after = jnp.where(last_tile, tail[::-1], after)
    return source, before, after


def edge_cols(pieces, first, width):
    extended = jnp.concatenate([piece[..., first : first + width] for piece in (pieces[1], pieces[0], pieces[2])], axis=1)
    return jnp.stack([extended[:, :, 0], extended[:, :, -1]], axis=2)


def pick_partner(gathered, matching_row):
    picked_sides = []
    for side_number in range(2):
        partner = matching_row[side_number, 0]
        their_side = matching_row[side_number, 1]
        flipped = matching_row[side_number, 2]
        face_count = lax.axis_size("face")
        slot = lax.rem(lax.axis_index("face") - partner + face_count, face_count)
        landed, offset, shape = gathered
        size = 1
        for dim in shape:
            size *= dim
        row = lax.dynamic_index_in_dim(landed, slot, 0, keepdims=False).reshape(-1)
        chosen = row[offset : offset + size].reshape(shape)
        column = jnp.where(their_side == 0, chosen[:, :, 0], chosen[:, :, 1])
        column = jnp.where(flipped == 1, column[::-1], column)
        picked_sides.append(column)
    return picked_sides


def pack_parts(parts):
    flat = jnp.concatenate([part.astype(jnp.float32).reshape(-1) for part in parts])
    return flat.reshape(-1, 128)


def unpack_parts(landed, parts):
    pieces = []
    offset = 0
    for part in parts:
        pieces.append((landed, offset, part.shape))
        offset += part.size
    return pieces


def side_columns(gathered_edges, matching_row):
    left_side, right_side = pick_partner(gathered_edges, matching_row)
    return jnp.stack([left_side, right_side], axis=1).astype(jnp.bfloat16)


def add_ends(field, first_add, last_add, axis):
    length = field.shape[axis]
    head = lax.slice_in_dim(field, 0, 1, axis=axis) + jnp.expand_dims(first_add, axis)
    middle = lax.slice_in_dim(field, 1, length - 1, axis=axis)
    tail = lax.slice_in_dim(field, length - 1, length, axis=axis) + jnp.expand_dims(last_add, axis)
    return jnp.concatenate([head, middle, tail], axis=axis)


def return_sides(inside, gathered_margins, matching_row):
    left_back, right_back = pick_partner(gathered_margins, matching_row)
    return at_edges(inside, left_back, right_back)


def route_observations(obs_values, obs_dest, obs_pixel, device_count):
    obs_rows = obs_values.shape[0]
    obs_width = obs_values.shape[1]
    capacity = 2 * obs_rows // device_count
    target = obs_dest[:, 0]
    positions = lax.iota(jnp.int32, obs_rows)
    same_target = (target[:, None] == target[None, :]) & (positions[None, :] < positions[:, None])
    rank_within = jnp.sum(same_target.astype(jnp.int32), axis=1)
    slot_index = target * capacity + rank_within
    slot_ids = lax.iota(jnp.int32, device_count * capacity)
    hits = slot_ids[:, None] == slot_index[None, :]
    value_slots = jnp.dot(
        hits.astype(jnp.bfloat16), obs_values, preferred_element_type=jnp.float32
    ).astype(jnp.bfloat16)
    pixel_slots = jnp.sum(jnp.where(hits, obs_pixel[None, :], 0), axis=1)
    high = (pixel_slots // 16).astype(jnp.bfloat16).reshape(device_count, capacity)
    low = (pixel_slots % 16).astype(jnp.bfloat16).reshape(device_count, capacity)
    pixel_row = jnp.concatenate(
        [high, low, jnp.zeros((device_count, obs_width - 2 * capacity), jnp.bfloat16)], axis=1
    )
    payload = jnp.concatenate(
        [value_slots.reshape(device_count, capacity, obs_width), pixel_row[:, None]], axis=1
    )
    arrived = lax.all_to_all(payload, ("face", "tile"), split_axis=0, concat_axis=0, tiled=True)
    got_values = arrived[:, :capacity].reshape(-1, obs_width)
    got_high = arrived[:, capacity, 0:capacity].astype(jnp.int32)
    got_low = arrived[:, capacity, capacity : 2 * capacity].astype(jnp.int32)
    got_pixels = (got_high * 16 + got_low).reshape(-1)
    return got_values, got_pixels


def per_device(
    state,
    obs_values,
    obs_dest,
    obs_pixel,
    matching,
    kernel_one,
    bias_one,
    kernel_two,
    bias_two,
    cotangent,
):
    base_field = state[0, 0]
    cot_field = cotangent[0, 0]
    band_rows = base_field.shape[1]
    column_count = base_field.shape[2]
    channels = base_field.shape[3]
    tile_count = lax.axis_size("tile")
    face_count = lax.axis_size("face")
    tile_at = lax.axis_index("tile")
    face_at = lax.axis_index("face")
    device_count = tile_count * face_count
    obs_width = obs_values.shape[1]

    got_values, got_pixels = route_observations(obs_values, obs_dest, obs_pixel, device_count)
    pixel_count = 2 * band_rows * column_count
    pixel_ids = lax.iota(jnp.int32, pixel_count)
    onehot = (pixel_ids[:, None] == got_pixels[None, :]).astype(jnp.bfloat16)
    gridded = jnp.dot(onehot, got_values, preferred_element_type=jnp.float32)
    gridded = gridded.reshape(2, band_rows, column_count, obs_width)

    last_tile = tile_at == tile_count - 1
    matching_row = lax.dynamic_index_in_dim(matching, face_at, 0, keepdims=False)

    lifted = kernel_one.shape[2]
    fields, got_values = lax.optimization_barrier(
        (jnp.concatenate([base_field, cot_field], axis=3), got_values)
    )
    both = extend_rows(fields, last_tile)
    cot_back, cot_margins = conv_back(both, channels, channels, kernel_two)
    parts = [edge_cols(both, 0, channels), jnp.swapaxes(cot_margins, 1, 2)]
    first_out, landed = conv_gather(both, 0, channels, pack_parts(parts), kernel_one, 0)
    base_edges, cot_gathered = unpack_parts(landed, parts)
    first_sides = side_terms(side_columns(base_edges, matching_row), kernel_one)

    pre_act = at_edges(first_out, first_sides[:, 0], first_sides[:, 1]) + bias_one + gridded
    inner = activation(pre_act).astype(jnp.bfloat16)
    grad_inner = return_sides(cot_back, cot_gathered, matching_row)
    grad_pre = jax.vjp(activation, pre_act)[1](grad_inner)[0].astype(jnp.bfloat16)

    pair = extend_rows(jnp.concatenate([inner, grad_pre], axis=3), last_tile)
    pre_back, pre_margins = conv_back(pair, lifted, lifted, kernel_one, cot_field)
    parts = [edge_cols(pair, 0, lifted), jnp.swapaxes(pre_margins, 1, 2)]
    second_out, landed = conv_gather(
        pair, 0, lifted, pack_parts(parts), kernel_two, 1, base_field, bias_two
    )
    inner_edges, pre_gathered = unpack_parts(landed, parts)
    second_sides = side_terms(side_columns(inner_edges, matching_row), kernel_two)

    second_out = at_edges(second_out, second_sides[:, 0], second_sides[:, 1])
    analysis = second_out.astype(jnp.bfloat16)
    grad_base = return_sides(pre_back, pre_gathered, matching_row)
    return (analysis[None, None], grad_base[None, None])


def solution(mesh):
    return jax.shard_map(
        per_device,
        mesh=mesh,
        in_specs=(
            P("face", "tile", None, None, None, None),
            P(("face", "tile"), None),
            P(("face", "tile"), None),
            P(("face", "tile")),
            P(),
            P(),
            P(),
            P(),
            P(),
            P("face", "tile", None, None, None, None),
        ),
        out_specs=(
            P("face", "tile", None, None, None, None),
            P("face", "tile", None, None, None, None),
        ),
        check_vma=False,
    )
```

```python
import functools

import jax
import jax.numpy as jnp
from jax import lax
from jax.experimental import pallas as pl
from jax.experimental.pallas import tpu as pltpu
from jax.sharding import PartitionSpec as P

MESH_IDS = pl.DeviceIdType.MESH


def activation(values):
    return jax.nn.gelu(values, approximate=True)


def tap_index(band, row_tap, col_tap, backward):
    if backward:
        row = 2 - row_tap if band == 0 else row_tap
        return 3 * row + 2 - col_tap
    row = row_tap if band == 0 else 2 - row_tap
    return 3 * row + col_tap


def conv_kernel(backward, first, width, src_ref, before_ref, after_ref, side_ref, k_ref, out_ref, margin_ref):
    bands, rows, cols, cout = out_ref.shape
    pixels = rows * cols
    lanes = slice(first, first + width)
    col = lax.broadcasted_iota(jnp.int32, (rows, cols, cout), 1).reshape(pixels, cout)
    for band in range(bands):
        ext = jnp.concatenate(
            [before_ref[band, :, :, lanes], src_ref[band, :, :, lanes], after_ref[band, :, :, lanes]],
            axis=0,
        )
        lhs = jnp.concatenate(
            [ext[dy : dy + rows].reshape(pixels, width) for dy in range(3)], axis=1
        )
        stacks = []
        for col_tap in range(3):
            taps = [k_ref[tap_index(band, dy, col_tap, backward)] for dy in range(3)]
            if backward:
                stacks.append(jnp.concatenate(taps, axis=1))
            else:
                stacks.append(jnp.concatenate(taps, axis=0))

        def product(values, stack):
            if backward:
                return lax.dot_general(
                    values, stack, (((1,), (1,)), ((), ())), preferred_element_type=jnp.float32
                )
            return jnp.dot(values, stack, preferred_element_type=jnp.float32)

        z_left = product(lhs, stacks[0])
        z_mid = product(lhs, stacks[1])
        z_right = product(lhs, stacks[2])
        if backward or side_ref is None:
            left_full = jnp.zeros((pixels, cout), jnp.float32)
            right_full = left_full
        else:
            sides = side_ref[band]
            left = jnp.concatenate([sides[0, dy : dy + rows] for dy in range(3)], axis=1)
            right = jnp.concatenate([sides[1, dy : dy + rows] for dy in range(3)], axis=1)
            left_term = product(left, stacks[0])
            right_term = product(right, stacks[2])
            left_full = jnp.broadcast_to(left_term[:, None, :], (rows, cols, cout)).reshape(pixels, cout)
            right_full = jnp.broadcast_to(right_term[:, None, :], (rows, cols, cout)).reshape(pixels, cout)
        from_left = jnp.where(col == 0, left_full, pltpu.roll(z_left, 1, 0))
        from_right = jnp.where(col == cols - 1, right_full, pltpu.roll(z_right, pixels - 1, 0))
        out_ref[band] = (z_mid + from_left + from_right).reshape(rows, cols, cout)
        if backward:
            margin_ref[band, 0] = z_right.reshape(rows, cols, cout)[:, 0, :]
            margin_ref[band, 1] = z_left.reshape(rows, cols, cout)[:, cols - 1, :]


def conv_pallas(pieces, first, width, sides, kernel, backward):
    source, before, after = pieces
    bands, rows, cols, _ = source.shape
    cout = kernel.shape[1] if backward else kernel.shape[2]
    if sides is None:
        sides = jnp.zeros((bands, 2, rows + 2, width), jnp.bfloat16)
    vmem = pl.BlockSpec(memory_space=pltpu.VMEM)
    out, margins = pl.pallas_call(
        functools.partial(conv_kernel, backward, first, width),
        in_specs=[vmem] * 5,
        out_specs=[vmem, vmem],
        out_shape=[
            jax.ShapeDtypeStruct((bands, rows, cols, cout), jnp.float32),
            jax.ShapeDtypeStruct((bands, 2, rows, cout), jnp.float32),
        ],
        compiler_params=pltpu.CompilerParams(vmem_limit_bytes=60 * 1024 * 1024),
    )(source, before, after, sides, kernel)
    return out, margins


def back_kernel(src_ref, before_ref, after_ref, k_ref, *rest):
    residual_ref = rest[0] if len(rest) == 3 else None
    out_ref, margin_ref = rest[-2:]
    band = pl.program_id(0)
    _, rows, cols, cout = out_ref.shape
    width = src_ref.shape[3]
    pixels = rows * cols
    col = lax.broadcasted_iota(jnp.int32, (rows, cols, cout), 1).reshape(pixels, cout)
    ext = jnp.concatenate([before_ref[0], src_ref[0], after_ref[0]], axis=0)
    lhs = jnp.concatenate([ext[dy : dy + rows].reshape(pixels, width) for dy in range(3)], axis=1)
    stacks = []
    for col_tap in range(3):
        taps = [k_ref[3 * (2 - dy + band * (2 * dy - 2)) + 2 - col_tap] for dy in range(3)]
        stacks.append(jnp.concatenate(taps, axis=1))
    joined = lax.dot_general(
        lhs, jnp.concatenate(stacks, axis=0), (((1,), (1,)), ((), ())), preferred_element_type=jnp.float32
    )
    z_left, z_mid, z_right = [joined[:, i * cout : (i + 1) * cout] for i in range(3)]
    from_left = jnp.where(col == 0, 0.0, pltpu.roll(z_left, 1, 0))
    from_right = jnp.where(col == cols - 1, 0.0, pltpu.roll(z_right, pixels - 1, 0))
    total = (z_mid + from_left + from_right).reshape(rows, cols, cout)
    if residual_ref is not None:
        total = total + residual_ref[0].astype(jnp.float32)
    out_ref[0] = total
    margin_ref[0, 0] = z_right.reshape(rows, cols, cout)[:, 0, :]
    margin_ref[0, 1] = z_left.reshape(rows, cols, cout)[:, cols - 1, :]


def conv_back(pieces, first, width, kernel, residual=None):
    source, before, after = pieces
    bands, rows, cols, _ = source.shape
    cout = kernel.shape[1]
    block = first // width
    extra_specs = []
    extra_args = ()
    if residual is not None:
        extra_specs = [pl.BlockSpec((1, rows, cols, cout), lambda b: (b, 0, 0, 0))]
        extra_args = (residual,)
    return pl.pallas_call(
        back_kernel,
        grid=(bands,),
        in_specs=[
            pl.BlockSpec((1, rows, cols, width), lambda b: (b, 0, 0, block)),
            pl.BlockSpec((1, 1, cols, width), lambda b: (b, 0, 0, block)),
            pl.BlockSpec((1, 1, cols, width), lambda b: (b, 0, 0, block)),
            pl.BlockSpec(kernel.shape, lambda b: (0, 0, 0)),
        ]
        + extra_specs,
        out_specs=[
            pl.BlockSpec((1, rows, cols, cout), lambda b: (b, 0, 0, 0)),
            pl.BlockSpec((1, 2, rows, cout), lambda b: (b, 0, 0, 0)),
        ],
        out_shape=[
            jax.ShapeDtypeStruct((bands, rows, cols, cout), jnp.float32),
            jax.ShapeDtypeStruct((bands, 2, rows, cout), jnp.float32),
        ],
        compiler_params=pltpu.CompilerParams(vmem_limit_bytes=60 * 1024 * 1024),
    )(source, before, after, kernel, *extra_args)


def conv_gather_kernel(count, block_ref, src_ref, before_ref, after_ref, k_ref, *rest):
    if len(rest) == 7:
        residual_ref, bias_ref = rest[:2]
    else:
        residual_ref = None
    out_ref, gathered_ref, landed, send_sems, recv_sems = rest[-5:]
    step_at = pl.program_id(0)
    face = lax.axis_index("face")
    tile = lax.axis_index("tile")
    copies = []
    for step in range(1, count):
        peer = lax.rem(face + step, count)
        copies.append(
            pltpu.make_async_remote_copy(
                src_ref=block_ref,
                dst_ref=landed.at[step],
                send_sem=send_sems.at[step],
                recv_sem=recv_sems.at[step],
                device_id=(peer, tile),
                device_id_type=MESH_IDS,
            )
        )

    @pl.when(step_at == 0)
    def _():
        barrier = pltpu.get_barrier_semaphore()
        for step in range(1, count):
            peer = lax.rem(face + step, count)
            pl.semaphore_signal(barrier, inc=1, device_id=(peer, tile), device_id_type=MESH_IDS)
        pl.semaphore_wait(barrier, count - 1)
        for copy in copies:
            copy.start()
        gathered_ref[0] = block_ref[...]

    _, rows, cols, cout = out_ref.shape
    width = src_ref.shape[3]
    pixels = rows * cols
    col = lax.broadcasted_iota(jnp.int32, (rows, cols, cout), 1).reshape(pixels, cout)
    ext = jnp.concatenate([before_ref[0], src_ref[0], after_ref[0]], axis=0)
    lhs = jnp.concatenate([ext[dy : dy + rows].reshape(pixels, width) for dy in range(3)], axis=1)
    stacks = []
    for col_tap in range(3):
        taps = [k_ref[3 * (dy + step_at * (2 - 2 * dy)) + col_tap] for dy in range(3)]
        stacks.append(jnp.concatenate(taps, axis=0))
    joined = jnp.dot(lhs, jnp.concatenate(stacks, axis=1), preferred_element_type=jnp.float32)
    z_left, z_mid, z_right = [joined[:, i * cout : (i + 1) * cout] for i in range(3)]
    from_left = jnp.where(col == 0, 0.0, pltpu.roll(z_left, 1, 0))
    from_right = jnp.where(col == cols - 1, 0.0, pltpu.roll(z_right, pixels - 1, 0))
    total = (z_mid + from_left + from_right).reshape(rows, cols, cout)
    if residual_ref is not None:
        total = total + residual_ref[0].astype(jnp.float32) + bias_ref[...]
    out_ref[0] = total

    @pl.when(step_at == pl.num_programs(0) - 1)
    def _():
        for copy in copies:
            copy.wait()
        for step in range(1, count):
            gathered_ref[step] = landed[step]


def conv_gather(pieces, first, width, block, kernel, gather_id, residual=None, bias=None):
    source, before, after = pieces
    bands, rows, cols, _ = source.shape
    cout = kernel.shape[2]
    extra_specs = []
    extra_args = ()
    if residual is not None:
        extra_specs = [
            pl.BlockSpec((1, rows, cols, cout), lambda b: (b, 0, 0, 0)),
            pl.BlockSpec((1, cout), lambda b: (0, 0)),
        ]
        extra_args = (residual, bias.reshape(1, cout))
    count = lax.axis_size("face")
    block_rows, lanes = block.shape
    lane_block = first // width
    return pl.pallas_call(
        functools.partial(conv_gather_kernel, count),
        grid=(bands,),
        in_specs=[
            pl.BlockSpec((block_rows, lanes), lambda b: (0, 0)),
            pl.BlockSpec((1, rows, cols, width), lambda b: (b, 0, 0, lane_block)),
            pl.BlockSpec((1, 1, cols, width), lambda b: (b, 0, 0, lane_block)),
            pl.BlockSpec((1, 1, cols, width), lambda b: (b, 0, 0, lane_block)),
            pl.BlockSpec(kernel.shape, lambda b: (0, 0, 0)),
        ]
        + extra_specs,
        out_specs=[
            pl.BlockSpec((1, rows, cols, cout), lambda b: (b, 0, 0, 0)),
            pl.BlockSpec((count, block_rows, lanes), lambda b: (0, 0, 0)),
        ],
        out_shape=[
            jax.ShapeDtypeStruct((bands, rows, cols, cout), jnp.float32),
            jax.ShapeDtypeStruct((count, block_rows, lanes), block.dtype),
        ],
        scratch_shapes=[
            pltpu.VMEM((count, block_rows, lanes), block.dtype),
            pltpu.SemaphoreType.DMA((count,)),
            pltpu.SemaphoreType.DMA((count,)),
        ],
        compiler_params=pltpu.CompilerParams(
            collective_id=gather_id, has_side_effects=True, vmem_limit_bytes=60 * 1024 * 1024
        ),
    )(block, source, before, after, kernel, *extra_args)


def side_terms(sides, kernel):
    bands, _, ext_rows, width = sides.shape
    rows = ext_rows - 2
    terms = []
    for band in range(bands):
        per_side = []
        for side, col_tap in ((0, 0), (1, 2)):
            stacked = jnp.concatenate([sides[band, side, dy : dy + rows] for dy in range(3)], axis=1)
            weights = jnp.concatenate(
                [kernel[tap_index(band, dy, col_tap, False)] for dy in range(3)], axis=0
            )
            per_side.append(jnp.dot(stacked, weights, preferred_element_type=jnp.float32))
        terms.append(jnp.stack(per_side))
    return jnp.stack(terms)


def at_edges(field, left_add, right_add):
    cols = field.shape[2]
    col = lax.broadcasted_iota(jnp.int32, field.shape, 2)
    return field + jnp.where(col == 0, left_add[:, :, None], 0.0) + jnp.where(
        col == cols - 1, right_add[:, :, None], 0.0
    )


def extend_rows(source, last_tile):
    count = lax.axis_size("tile")
    band_rows = source.shape[1]
    head = source[:, 0:1]
    tail = source[:, band_rows - 1 : band_rows]
    before = lax.ppermute(tail, "tile", [(i, i + 1) for i in range(count - 1)])
    after = lax.ppermute(head, "tile", [(i + 1, i) for i in range(count - 1)])
    after = jnp.where(last_tile, tail[::-1], after)
    return source, before, after


def edge_cols(pieces, first, width):
    extended = jnp.concatenate([piece[..., first : first + width] for piece in (pieces[1], pieces[0], pieces[2])], axis=1)
    return jnp.stack([extended[:, :, 0], extended[:, :, -1]], axis=2)


def pick_partner(gathered, matching_row):
    picked_sides = []
    for side_number in range(2):
        partner = matching_row[side_number, 0]
        their_side = matching_row[side_number, 1]
        flipped = matching_row[side_number, 2]
        face_count = lax.axis_size("face")
        slot = lax.rem(lax.axis_index("face") - partner + face_count, face_count)
        chosen = lax.dynamic_index_in_dim(gathered, slot, 0, keepdims=False)
        column = jnp.where(their_side == 0, chosen[:, :, 0], chosen[:, :, 1])
        column = jnp.where(flipped == 1, column[::-1], column)
        picked_sides.append(column)
    return picked_sides


def pack_parts(parts):
    flat = jnp.concatenate([part.astype(jnp.float32).reshape(-1) for part in parts])
    return flat.reshape(-1, 128)


def unpack_parts(landed, parts):
    face_count = lax.axis_size("face")
    face_at = lax.axis_index("face")
    gathered = landed.reshape(face_count, -1)
    pieces = []
    offset = 0
    for part in parts:
        size = part.size
        piece = gathered[:, offset : offset + size].reshape((face_count,) + part.shape)
        pieces.append(piece)
        offset += size
    return pieces


def side_columns(gathered_edges, matching_row):
    left_side, right_side = pick_partner(gathered_edges, matching_row)
    return jnp.stack([left_side, right_side], axis=1).astype(jnp.bfloat16)


def add_ends(field, first_add, last_add, axis):
    length = field.shape[axis]
    head = lax.slice_in_dim(field, 0, 1, axis=axis) + jnp.expand_dims(first_add, axis)
    middle = lax.slice_in_dim(field, 1, length - 1, axis=axis)
    tail = lax.slice_in_dim(field, length - 1, length, axis=axis) + jnp.expand_dims(last_add, axis)
    return jnp.concatenate([head, middle, tail], axis=axis)


def return_sides(inside, gathered_margins, matching_row):
    left_back, right_back = pick_partner(gathered_margins, matching_row)
    return at_edges(inside, left_back, right_back)


def route_observations(obs_values, obs_dest, obs_pixel, device_count):
    obs_rows = obs_values.shape[0]
    obs_width = obs_values.shape[1]
    capacity = 2 * obs_rows // device_count
    target = obs_dest[:, 0]
    positions = lax.iota(jnp.int32, obs_rows)
    same_target = (target[:, None] == target[None, :]) & (positions[None, :] < positions[:, None])
    rank_within = jnp.sum(same_target.astype(jnp.int32), axis=1)
    slot_index = target * capacity + rank_within
    slot_ids = lax.iota(jnp.int32, device_count * capacity)
    hits = slot_ids[:, None] == slot_index[None, :]
    codes = jnp.stack([obs_pixel // 16, obs_pixel % 16], axis=1).astype(jnp.bfloat16)
    widened = jnp.concatenate(
        [obs_values, codes, jnp.zeros((obs_rows, 126), jnp.bfloat16)], axis=1
    )
    slots = jnp.dot(
        hits.astype(jnp.bfloat16), widened, preferred_element_type=jnp.float32
    ).astype(jnp.bfloat16)
    value_slots = slots[:, :obs_width]
    high = slots[:, obs_width].reshape(device_count, capacity)
    low = slots[:, obs_width + 1].reshape(device_count, capacity)
    pixel_row = jnp.concatenate(
        [high, low, jnp.zeros((device_count, obs_width - 2 * capacity), jnp.bfloat16)], axis=1
    )
    payload = jnp.concatenate(
        [value_slots.reshape(device_count, capacity, obs_width), pixel_row[:, None]], axis=1
    )
    arrived = lax.all_to_all(payload, ("face", "tile"), split_axis=0, concat_axis=0, tiled=True)
    got_values = arrived[:, :capacity].reshape(-1, obs_width)
    got_high = arrived[:, capacity, 0:capacity].astype(jnp.int32)
    got_low = arrived[:, capacity, capacity : 2 * capacity].astype(jnp.int32)
    got_pixels = (got_high * 16 + got_low).reshape(-1)
    return got_values, got_pixels


def per_device(
    state,
    obs_values,
    obs_dest,
    obs_pixel,
    matching,
    kernel_one,
    bias_one,
    kernel_two,
    bias_two,
    cotangent,
):
    base_field = state[0, 0]
    cot_field = cotangent[0, 0]
    band_rows = base_field.shape[1]
    column_count = base_field.shape[2]
    channels = base_field.shape[3]
    tile_count = lax.axis_size("tile")
    face_count = lax.axis_size("face")
    tile_at = lax.axis_index("tile")
    face_at = lax.axis_index("face")
    device_count = tile_count * face_count
    obs_width = obs_values.shape[1]

    got_values, got_pixels = route_observations(obs_values, obs_dest, obs_pixel, device_count)
    pixel_count = 2 * band_rows * column_count
    pixel_ids = lax.iota(jnp.int32, pixel_count)
    onehot = (pixel_ids[:, None] == got_pixels[None, :]).astype(jnp.bfloat16)
    gridded = jnp.dot(onehot, got_values, preferred_element_type=jnp.float32)
    gridded = gridded.reshape(2, band_rows, column_count, obs_width)

    last_tile = tile_at == tile_count - 1
    matching_row = lax.dynamic_index_in_dim(matching, face_at, 0, keepdims=False)

    lifted = kernel_one.shape[2]
    fields, got_values = lax.optimization_barrier(
        (jnp.concatenate([base_field, cot_field], axis=3), got_values)
    )
    both = extend_rows(fields, last_tile)
    cot_back, cot_margins = conv_back(both, channels, channels, kernel_two)
    parts = [edge_cols(both, 0, channels), jnp.swapaxes(cot_margins, 1, 2)]
    first_out, landed = conv_gather(both, 0, channels, pack_parts(parts), kernel_one, 0)
    base_edges, cot_gathered = unpack_parts(landed, parts)
    first_sides = side_terms(side_columns(base_edges, matching_row), kernel_one)

    pre_act = at_edges(first_out, first_sides[:, 0], first_sides[:, 1]) + bias_one + gridded
    inner = activation(pre_act).astype(jnp.bfloat16)
    grad_inner = return_sides(cot_back, cot_gathered, matching_row)
    grad_pre = jax.vjp(activation, pre_act)[1](grad_inner)[0].astype(jnp.bfloat16)

    pair = extend_rows(jnp.concatenate([inner, grad_pre], axis=3), last_tile)
    pre_back, pre_margins = conv_back(pair, lifted, lifted, kernel_one, cot_field)
    parts = [edge_cols(pair, 0, lifted), jnp.swapaxes(pre_margins, 1, 2)]
    second_out, landed = conv_gather(
        pair, 0, lifted, pack_parts(parts), kernel_two, 1, base_field, bias_two
    )
    inner_edges, pre_gathered = unpack_parts(landed, parts)
    second_sides = side_terms(side_columns(inner_edges, matching_row), kernel_two)

    second_out = at_edges(second_out, second_sides[:, 0], second_sides[:, 1])
    analysis = second_out.astype(jnp.bfloat16)
    grad_base = return_sides(pre_back, pre_gathered, matching_row)
    return (analysis[None, None], grad_base[None, None])


def solution(mesh):
    return jax.shard_map(
        per_device,
        mesh=mesh,
        in_specs=(
            P("face", "tile", None, None, None, None),
            P(("face", "tile"), None),
            P(("face", "tile"), None),
            P(("face", "tile")),
            P(),
            P(),
            P(),
            P(),
            P(),
            P("face", "tile", None, None, None, None),
        ),
        out_specs=(
            P("face", "tile", None, None, None, None),
            P("face", "tile", None, None, None, None),
        ),
        check_vma=False,
    )
```

```python
import functools

import jax
import jax.numpy as jnp
from jax import lax
from jax.experimental import pallas as pl
from jax.experimental.pallas import tpu as pltpu
from jax.sharding import PartitionSpec as P

MESH_IDS = pl.DeviceIdType.MESH


def activation(values):
    return jax.nn.gelu(values, approximate=True)


def tap_index(band, row_tap, col_tap, backward):
    if backward:
        row = 2 - row_tap if band == 0 else row_tap
        return 3 * row + 2 - col_tap
    row = row_tap if band == 0 else 2 - row_tap
    return 3 * row + col_tap


def conv_kernel(backward, first, width, src_ref, before_ref, after_ref, side_ref, k_ref, out_ref, margin_ref):
    bands, rows, cols, cout = out_ref.shape
    pixels = rows * cols
    lanes = slice(first, first + width)
    col = lax.broadcasted_iota(jnp.int32, (rows, cols, cout), 1).reshape(pixels, cout)
    for band in range(bands):
        ext = jnp.concatenate(
            [before_ref[band, :, :, lanes], src_ref[band, :, :, lanes], after_ref[band, :, :, lanes]],
            axis=0,
        )
        lhs = jnp.concatenate(
            [ext[dy : dy + rows].reshape(pixels, width) for dy in range(3)], axis=1
        )
        stacks = []
        for col_tap in range(3):
            taps = [k_ref[tap_index(band, dy, col_tap, backward)] for dy in range(3)]
            if backward:
                stacks.append(jnp.concatenate(taps, axis=1))
            else:
                stacks.append(jnp.concatenate(taps, axis=0))

        def product(values, stack):
            if backward:
                return lax.dot_general(
                    values, stack, (((1,), (1,)), ((), ())), preferred_element_type=jnp.float32
                )
            return jnp.dot(values, stack, preferred_element_type=jnp.float32)

        z_left = product(lhs, stacks[0])
        z_mid = product(lhs, stacks[1])
        z_right = product(lhs, stacks[2])
        if backward or side_ref is None:
            left_full = jnp.zeros((pixels, cout), jnp.float32)
            right_full = left_full
        else:
            sides = side_ref[band]
            left = jnp.concatenate([sides[0, dy : dy + rows] for dy in range(3)], axis=1)
            right = jnp.concatenate([sides[1, dy : dy + rows] for dy in range(3)], axis=1)
            left_term = product(left, stacks[0])
            right_term = product(right, stacks[2])
            left_full = jnp.broadcast_to(left_term[:, None, :], (rows, cols, cout)).reshape(pixels, cout)
            right_full = jnp.broadcast_to(right_term[:, None, :], (rows, cols, cout)).reshape(pixels, cout)
        from_left = jnp.where(col == 0, left_full, pltpu.roll(z_left, 1, 0))
        from_right = jnp.where(col == cols - 1, right_full, pltpu.roll(z_right, pixels - 1, 0))
        out_ref[band] = (z_mid + from_left + from_right).reshape(rows, cols, cout)
        if backward:
            margin_ref[band, 0] = z_right.reshape(rows, cols, cout)[:, 0, :]
            margin_ref[band, 1] = z_left.reshape(rows, cols, cout)[:, cols - 1, :]


def conv_pallas(pieces, first, width, sides, kernel, backward):
    source, before, after = pieces
    bands, rows, cols, _ = source.shape
    cout = kernel.shape[1] if backward else kernel.shape[2]
    if sides is None:
        sides = jnp.zeros((bands, 2, rows + 2, width), jnp.bfloat16)
    vmem = pl.BlockSpec(memory_space=pltpu.VMEM)
    out, margins = pl.pallas_call(
        functools.partial(conv_kernel, backward, first, width),
        in_specs=[vmem] * 5,
        out_specs=[vmem, vmem],
        out_shape=[
            jax.ShapeDtypeStruct((bands, rows, cols, cout), jnp.float32),
            jax.ShapeDtypeStruct((bands, 2, rows, cout), jnp.float32),
        ],
        compiler_params=pltpu.CompilerParams(vmem_limit_bytes=60 * 1024 * 1024),
    )(source, before, after, sides, kernel)
    return out, margins


def back_kernel(src_ref, before_ref, after_ref, k_ref, *rest):
    residual_ref = rest[0] if len(rest) == 3 else None
    out_ref, margin_ref = rest[-2:]
    band = pl.program_id(0)
    _, rows, cols, cout = out_ref.shape
    width = src_ref.shape[3]
    pixels = rows * cols
    col = lax.broadcasted_iota(jnp.int32, (rows, cols, cout), 1).reshape(pixels, cout)
    ext = jnp.concatenate([before_ref[0], src_ref[0], after_ref[0]], axis=0)
    lhs = jnp.concatenate([ext[dy : dy + rows].reshape(pixels, width) for dy in range(3)], axis=1)
    stacks = []
    for col_tap in range(3):
        taps = [k_ref[3 * (2 - dy + band * (2 * dy - 2)) + 2 - col_tap] for dy in range(3)]
        stacks.append(jnp.concatenate(taps, axis=1))
    joined = lax.dot_general(
        lhs, jnp.concatenate(stacks, axis=0), (((1,), (1,)), ((), ())), preferred_element_type=jnp.float32
    )
    z_left, z_mid, z_right = [joined[:, i * cout : (i + 1) * cout] for i in range(3)]
    from_left = jnp.where(col == 0, 0.0, pltpu.roll(z_left, 1, 0))
    from_right = jnp.where(col == cols - 1, 0.0, pltpu.roll(z_right, pixels - 1, 0))
    total = (z_mid + from_left + from_right).reshape(rows, cols, cout)
    if residual_ref is not None:
        total = total + residual_ref[0].astype(jnp.float32)
    out_ref[0] = total
    margin_ref[0, 0] = z_right.reshape(rows, cols, cout)[:, 0, :]
    margin_ref[0, 1] = z_left.reshape(rows, cols, cout)[:, cols - 1, :]


def conv_back(pieces, first, width, kernel, residual=None):
    source, before, after = pieces
    bands, rows, cols, _ = source.shape
    cout = kernel.shape[1]
    block = first // width
    extra_specs = []
    extra_args = ()
    if residual is not None:
        extra_specs = [pl.BlockSpec((1, rows, cols, cout), lambda b: (b, 0, 0, 0))]
        extra_args = (residual,)
    return pl.pallas_call(
        back_kernel,
        grid=(bands,),
        in_specs=[
            pl.BlockSpec((1, rows, cols, width), lambda b: (b, 0, 0, block)),
            pl.BlockSpec((1, 1, cols, width), lambda b: (b, 0, 0, block)),
            pl.BlockSpec((1, 1, cols, width), lambda b: (b, 0, 0, block)),
            pl.BlockSpec(kernel.shape, lambda b: (0, 0, 0)),
        ]
        + extra_specs,
        out_specs=[
            pl.BlockSpec((1, rows, cols, cout), lambda b: (b, 0, 0, 0)),
            pl.BlockSpec((1, 2, rows, cout), lambda b: (b, 0, 0, 0)),
        ],
        out_shape=[
            jax.ShapeDtypeStruct((bands, rows, cols, cout), jnp.float32),
            jax.ShapeDtypeStruct((bands, 2, rows, cout), jnp.float32),
        ],
        compiler_params=pltpu.CompilerParams(vmem_limit_bytes=60 * 1024 * 1024),
    )(source, before, after, kernel, *extra_args)


def conv_gather_kernel(count, block_ref, src_ref, before_ref, after_ref, k_ref, *rest):
    if len(rest) == 7:
        residual_ref, bias_ref = rest[:2]
    else:
        residual_ref = None
    out_ref, gathered_ref, landed, send_sems, recv_sems = rest[-5:]
    step_at = pl.program_id(0)
    face = lax.axis_index("face")
    tile = lax.axis_index("tile")
    copies = []
    for step in range(1, count):
        peer = lax.rem(face + step, count)
        copies.append(
            pltpu.make_async_remote_copy(
                src_ref=block_ref,
                dst_ref=landed.at[step],
                send_sem=send_sems.at[step],
                recv_sem=recv_sems.at[step],
                device_id=(peer, tile),
                device_id_type=MESH_IDS,
            )
        )

    @pl.when(step_at == 0)
    def _():
        barrier = pltpu.get_barrier_semaphore()
        for step in range(1, count):
            peer = lax.rem(face + step, count)
            pl.semaphore_signal(barrier, inc=1, device_id=(peer, tile), device_id_type=MESH_IDS)
        pl.semaphore_wait(barrier, count - 1)
        for copy in copies:
            copy.start()
        gathered_ref[0] = block_ref[...]

    _, rows, cols, cout = out_ref.shape
    width = src_ref.shape[3]
    pixels = rows * cols
    col = lax.broadcasted_iota(jnp.int32, (rows, cols, cout), 1).reshape(pixels, cout)
    ext = jnp.concatenate([before_ref[0], src_ref[0], after_ref[0]], axis=0)
    lhs = jnp.concatenate([ext[dy : dy + rows].reshape(pixels, width) for dy in range(3)], axis=1)
    stacks = []
    for col_tap in range(3):
        taps = [k_ref[3 * (dy + step_at * (2 - 2 * dy)) + col_tap] for dy in range(3)]
        stacks.append(jnp.concatenate(taps, axis=0))
    joined = jnp.dot(lhs, jnp.concatenate(stacks, axis=1), preferred_element_type=jnp.float32)
    z_left, z_mid, z_right = [joined[:, i * cout : (i + 1) * cout] for i in range(3)]
    from_left = jnp.where(col == 0, 0.0, pltpu.roll(z_left, 1, 0))
    from_right = jnp.where(col == cols - 1, 0.0, pltpu.roll(z_right, pixels - 1, 0))
    total = (z_mid + from_left + from_right).reshape(rows, cols, cout)
    if residual_ref is not None:
        total = total + residual_ref[0].astype(jnp.float32) + bias_ref[...]
    out_ref[0] = total

    @pl.when(step_at == pl.num_programs(0) - 1)
    def _():
        for copy in copies:
            copy.wait()
        for step in range(1, count):
            gathered_ref[step] = landed[step]


def conv_gather(pieces, first, width, block, kernel, gather_id, residual=None, bias=None):
    source, before, after = pieces
    bands, rows, cols, _ = source.shape
    cout = kernel.shape[2]
    extra_specs = []
    extra_args = ()
    if residual is not None:
        extra_specs = [
            pl.BlockSpec((1, rows, cols, cout), lambda b: (b, 0, 0, 0)),
            pl.BlockSpec((1, cout), lambda b: (0, 0)),
        ]
        extra_args = (residual, bias.reshape(1, cout))
    count = lax.axis_size("face")
    block_rows, lanes = block.shape
    lane_block = first // width
    return pl.pallas_call(
        functools.partial(conv_gather_kernel, count),
        grid=(bands,),
        in_specs=[
            pl.BlockSpec((block_rows, lanes), lambda b: (0, 0)),
            pl.BlockSpec((1, rows, cols, width), lambda b: (b, 0, 0, lane_block)),
            pl.BlockSpec((1, 1, cols, width), lambda b: (b, 0, 0, lane_block)),
            pl.BlockSpec((1, 1, cols, width), lambda b: (b, 0, 0, lane_block)),
            pl.BlockSpec(kernel.shape, lambda b: (0, 0, 0)),
        ]
        + extra_specs,
        out_specs=[
            pl.BlockSpec((1, rows, cols, cout), lambda b: (b, 0, 0, 0)),
            pl.BlockSpec((count, block_rows, lanes), lambda b: (0, 0, 0)),
        ],
        out_shape=[
            jax.ShapeDtypeStruct((bands, rows, cols, cout), jnp.float32),
            jax.ShapeDtypeStruct((count, block_rows, lanes), block.dtype),
        ],
        scratch_shapes=[
            pltpu.VMEM((count, block_rows, lanes), block.dtype),
            pltpu.SemaphoreType.DMA((count,)),
            pltpu.SemaphoreType.DMA((count,)),
        ],
        compiler_params=pltpu.CompilerParams(
            collective_id=gather_id, has_side_effects=True, vmem_limit_bytes=60 * 1024 * 1024
        ),
    )(block, source, before, after, kernel, *extra_args)


def side_terms(sides, kernel):
    bands, _, ext_rows, width = sides.shape
    rows = ext_rows - 2
    terms = []
    for band in range(bands):
        per_side = []
        for side, col_tap in ((0, 0), (1, 2)):
            stacked = jnp.concatenate([sides[band, side, dy : dy + rows] for dy in range(3)], axis=1)
            weights = jnp.concatenate(
                [kernel[tap_index(band, dy, col_tap, False)] for dy in range(3)], axis=0
            )
            per_side.append(jnp.dot(stacked, weights, preferred_element_type=jnp.float32))
        terms.append(jnp.stack(per_side))
    return jnp.stack(terms)


def at_edges(field, left_add, right_add):
    cols = field.shape[2]
    col = lax.broadcasted_iota(jnp.int32, field.shape, 2)
    return field + jnp.where(col == 0, left_add[:, :, None], 0.0) + jnp.where(
        col == cols - 1, right_add[:, :, None], 0.0
    )


def extend_rows(source, last_tile):
    count = lax.axis_size("tile")
    band_rows = source.shape[1]
    head = source[:, 0:1]
    tail = source[:, band_rows - 1 : band_rows]
    before = lax.ppermute(tail, "tile", [(i, i + 1) for i in range(count - 1)])
    after = lax.ppermute(head, "tile", [(i + 1, i) for i in range(count - 1)])
    after = jnp.where(last_tile, tail[::-1], after)
    return source, before, after


def edge_cols(pieces, first, width):
    extended = jnp.concatenate([piece[..., first : first + width] for piece in (pieces[1], pieces[0], pieces[2])], axis=1)
    return jnp.stack([extended[:, :, 0], extended[:, :, -1]], axis=2)


def pick_partner(gathered, matching_row):
    picked_sides = []
    for side_number in range(2):
        partner = matching_row[side_number, 0]
        their_side = matching_row[side_number, 1]
        flipped = matching_row[side_number, 2]
        face_count = lax.axis_size("face")
        slot = lax.rem(lax.axis_index("face") - partner + face_count, face_count)
        chosen = lax.dynamic_index_in_dim(gathered, slot, 0, keepdims=False)
        column = jnp.where(their_side == 0, chosen[:, :, 0], chosen[:, :, 1])
        column = jnp.where(flipped == 1, column[::-1], column)
        picked_sides.append(column)
    return picked_sides


def pack_parts(parts):
    flat = jnp.concatenate([part.astype(jnp.float32).reshape(-1) for part in parts])
    return flat.reshape(-1, 128)


def unpack_parts(landed, parts):
    face_count = lax.axis_size("face")
    face_at = lax.axis_index("face")
    gathered = landed.reshape(face_count, -1)
    pieces = []
    offset = 0
    for part in parts:
        size = part.size
        piece = gathered[:, offset : offset + size].reshape((face_count,) + part.shape)
        pieces.append(piece)
        offset += size
    return pieces


def side_columns(gathered_edges, matching_row):
    left_side, right_side = pick_partner(gathered_edges, matching_row)
    return jnp.stack([left_side, right_side], axis=1).astype(jnp.bfloat16)


def add_ends(field, first_add, last_add, axis):
    length = field.shape[axis]
    head = lax.slice_in_dim(field, 0, 1, axis=axis) + jnp.expand_dims(first_add, axis)
    middle = lax.slice_in_dim(field, 1, length - 1, axis=axis)
    tail = lax.slice_in_dim(field, length - 1, length, axis=axis) + jnp.expand_dims(last_add, axis)
    return jnp.concatenate([head, middle, tail], axis=axis)


def return_sides(inside, gathered_margins, matching_row):
    left_back, right_back = pick_partner(gathered_margins, matching_row)
    return at_edges(inside, left_back, right_back)


def route_observations(obs_values, obs_dest, obs_pixel, device_count):
    obs_rows = obs_values.shape[0]
    obs_width = obs_values.shape[1]
    capacity = 2 * obs_rows // device_count
    target = obs_dest[:, 0]
    positions = lax.iota(jnp.int32, obs_rows)
    same_target = (target[:, None] == target[None, :]) & (positions[None, :] < positions[:, None])
    rank_within = jnp.sum(same_target.astype(jnp.int32), axis=1)
    slot_index = target * capacity + rank_within
    slot_ids = lax.iota(jnp.int32, device_count * capacity)
    hits = slot_ids[:, None] == slot_index[None, :]
    value_slots = jnp.dot(
        hits.astype(jnp.bfloat16), obs_values, preferred_element_type=jnp.float32
    ).astype(jnp.bfloat16)
    pixel_slots = jnp.sum(jnp.where(hits, obs_pixel[None, :], 0), axis=1)
    high = (pixel_slots // 16).astype(jnp.bfloat16).reshape(device_count, capacity)
    low = (pixel_slots % 16).astype(jnp.bfloat16).reshape(device_count, capacity)
    pixel_row = jnp.concatenate(
        [high, low, jnp.zeros((device_count, obs_width - 2 * capacity), jnp.bfloat16)], axis=1
    )
    payload = jnp.concatenate(
        [value_slots.reshape(device_count, capacity, obs_width), pixel_row[:, None]], axis=1
    )
    arrived = lax.all_to_all(payload, ("face", "tile"), split_axis=0, concat_axis=0, tiled=True)
    got_values = arrived[:, :capacity].reshape(-1, obs_width)
    got_high = arrived[:, capacity, 0:capacity].astype(jnp.int32)
    got_low = arrived[:, capacity, capacity : 2 * capacity].astype(jnp.int32)
    got_pixels = (got_high * 16 + got_low).reshape(-1)
    return got_values, got_pixels


def per_device(
    state,
    obs_values,
    obs_dest,
    obs_pixel,
    matching,
    kernel_one,
    bias_one,
    kernel_two,
    bias_two,
    cotangent,
):
    base_field = state[0, 0]
    cot_field = cotangent[0, 0]
    band_rows = base_field.shape[1]
    column_count = base_field.shape[2]
    channels = base_field.shape[3]
    tile_count = lax.axis_size("tile")
    face_count = lax.axis_size("face")
    tile_at = lax.axis_index("tile")
    face_at = lax.axis_index("face")
    device_count = tile_count * face_count
    obs_width = obs_values.shape[1]

    got_values, got_pixels = route_observations(obs_values, obs_dest, obs_pixel, device_count)
    pixel_count = 2 * band_rows * column_count
    pixel_ids = lax.iota(jnp.int32, pixel_count)
    onehot = (pixel_ids[:, None] == got_pixels[None, :]).astype(jnp.bfloat16)
    gridded = jnp.dot(onehot, got_values, preferred_element_type=jnp.float32)
    gridded = gridded.reshape(2, band_rows, column_count, obs_width)

    last_tile = tile_at == tile_count - 1
    matching_row = lax.dynamic_index_in_dim(matching, face_at, 0, keepdims=False)

    lifted = kernel_one.shape[2]
    both = extend_rows(jnp.concatenate([base_field, cot_field], axis=3), last_tile)
    cot_back, cot_margins = conv_back(both, channels, channels, kernel_two)
    parts = [edge_cols(both, 0, channels), jnp.swapaxes(cot_margins, 1, 2)]
    first_out, landed = conv_gather(both, 0, channels, pack_parts(parts), kernel_one, 0)
    base_edges, cot_gathered = unpack_parts(landed, parts)
    first_sides = side_terms(side_columns(base_edges, matching_row), kernel_one)

    pre_act = at_edges(first_out, first_sides[:, 0], first_sides[:, 1]) + bias_one + gridded
    inner = activation(pre_act).astype(jnp.bfloat16)
    grad_inner = return_sides(cot_back, cot_gathered, matching_row)
    grad_pre = jax.vjp(activation, pre_act)[1](grad_inner)[0].astype(jnp.bfloat16)

    pair = extend_rows(jnp.concatenate([inner, grad_pre], axis=3), last_tile)
    pre_back, pre_margins = conv_back(pair, lifted, lifted, kernel_one, cot_field)
    parts = [edge_cols(pair, 0, lifted), jnp.swapaxes(pre_margins, 1, 2)]
    second_out, landed = conv_gather(
        pair, 0, lifted, pack_parts(parts), kernel_two, 1, base_field, bias_two
    )
    inner_edges, pre_gathered = unpack_parts(landed, parts)
    second_sides = side_terms(side_columns(inner_edges, matching_row), kernel_two)

    second_out = at_edges(second_out, second_sides[:, 0], second_sides[:, 1])
    analysis = second_out.astype(jnp.bfloat16)
    grad_base = return_sides(pre_back, pre_gathered, matching_row)
    return (analysis[None, None], grad_base[None, None])


def solution(mesh):
    return jax.shard_map(
        per_device,
        mesh=mesh,
        in_specs=(
            P("face", "tile", None, None, None, None),
            P(("face", "tile"), None),
            P(("face", "tile"), None),
            P(("face", "tile")),
            P(),
            P(),
            P(),
            P(),
            P(),
            P("face", "tile", None, None, None, None),
        ),
        out_specs=(
            P("face", "tile", None, None, None, None),
            P("face", "tile", None, None, None, None),
        ),
        check_vma=False,
    )
```
